32 devices in a mesh: wide: 8 (over z, x), narrow: 4 (over y, core).
Axes of the slice: x: 2, y: 2, z: 4, core: 2. Of those that a mesh axis runs over, the one named last changes fastest.
Arguments:
- tractions: float32 [16, 8, 3, 256], P('wide', 'narrow'), may hold values from -6 to 6
- centers: float32 [16, 8, 3], P('wide', 'narrow'), may hold values from 0 to 272, as said below
- node_offsets: float32 [3, 256], replicated, may hold values from -3 to 3
- occupied: int32 [16, 8], P('wide', 'narrow'), may hold values from 0 to 1, as said below
- anchors: int32 [16, 8, 3], P('wide', 'narrow'), may hold values from 0 to 255, as said below
- near_list: int32 [16, 8, 2], P('wide', 'narrow'), may hold values from 0 to 127, as said below
- contact_pairs: int32 [2, 1024], P(None, ('wide', 'narrow')), may hold values from 0 to 127, as said below
- contact_gap: float32 [1024], P(('wide', 'narrow')), may hold values from -1 to 1
- contact_angles: float32 [2, 1024], P(None, ('wide', 'narrow')), may hold values from -3.140625 to 3.140625
Outputs:
- node_velocity: float32 [16, 8, 3, 256], P('wide', 'narrow')
- contact_force: float32 [1024], P(('wide', 'narrow'))
- moved_centers: float32 [16, 8, 3], P('wide', 'narrow')
The draws below stay inside these ranges and needn't reach their ends.
Inputs may be any that keep to these rules, and one draw needn't show every extreme that they name: `occupied`: in every device's 2 x 2 block of slots the live slots come first in row-major order, and each device holds at least one; some device has all 4 slots live. `anchors`: for a slot of the device with indices w along wide and n along narrow, the first entry lies in [w * 32, (w + 1) * 32) and the second in [n * 64, (n + 1) * 64). `centers`: each component of a centre is its slot's anchor entry plus 16/2 plus at most 0.5 either way. `near_list`: entries of live slots name live spheres other than the slot's own, held by the same device or by one whose wide and narrow indices each differ by at most one, cyclically; entries may repeat. `contact_pairs`: the first sphere of a contact is live and held by the device that holds the contact; the second is an entry of the first's near list.
All inputs are finite; a program needn't handle non-finite values.
Results may differ from the reference program's by a relative error of at most 0.0003.
Values sent between devices are 32-bit elements; how exact they have to be, the bound alone decides.
No kernel may reach another device: no remote copies, remote signals or barrier semaphores. Data moves between devices by JAX's collectives and lax.ppermute only.
A program may use at most 192 MiB of HBM per device.

```python
import jax
import jax.numpy as jnp
from jax import lax

NODES = 256
GRID = 256
BLOCK = 16
NEAR = 2
SWEEPS = 6
S_SIDE = 2
CONT_DEV = 32
ROWS = 16
COLS = 8
SLOTS = 128
CONTACTS = 1024
N_WIDE = 8
N_NARROW = 4


def to_grid(array):
    trailing = array.shape[2:]
    shaped = array.reshape((N_WIDE, N_NARROW, S_SIDE, S_SIDE) + trailing)
    return jnp.swapaxes(shaped, 1, 2).reshape((S_SIDE * N_WIDE, S_SIDE * N_NARROW) + trailing)


def geometry(key):
    folded = jax.random.fold_in(key, 31)
    streams = jax.random.split(folded, 12)
    devices_all = N_WIDE * N_NARROW
    per_device = S_SIDE * S_SIDE
    device_ids = jnp.arange(devices_all, dtype=jnp.int32)
    counts = jax.random.randint(streams[0], (devices_all,), 1, per_device + 1, dtype=jnp.int32)
    busiest = jax.random.randint(streams[1], (), 0, devices_all, dtype=jnp.int32)
    counts = jnp.where(device_ids == busiest, per_device, counts)
    slot_ids = jnp.arange(per_device, dtype=jnp.int32)
    occupied = (slot_ids[None, :] < counts[:, None]).astype(jnp.int32)
    wide_ids = device_ids // N_NARROW
    narrow_ids = device_ids % N_NARROW
    side_x = slot_ids % 2
    side_y = slot_ids // 2 % 2
    corner_ids = jnp.arange(4, dtype=jnp.int32)
    corner_x = corner_ids % 2
    corner_y = corner_ids // 2
    partner_w = (wide_ids[:, None, None] + side_x[None, :, None] - corner_x[None, None, :]) % N_WIDE
    partner_n = (narrow_ids[:, None, None] + side_y[None, :, None] - corner_y[None, None, :]) % N_NARROW
    partners = (partner_w * N_NARROW + partner_n).astype(jnp.int32)
    live_cand = slot_ids[None, None, None, :] < counts[partners][..., None]
    type_cand = (side_x[None, None, None, :] == corner_x[None, None, :, None]) & (side_y[None, None, None, :] == corner_y[None, None, :, None])
    self_cand = (partners[..., None] == device_ids[:, None, None, None]) & (slot_ids[None, None, None, :] == slot_ids[None, :, None, None])
    same_corner = live_cand & type_cand & ~self_cand
    any_valid = live_cand & ~self_cand
    priority = same_corner.astype(jnp.int32) * 2 ** 26 + any_valid.astype(jnp.int32) * 2 ** 25
    priority = priority.reshape(devices_all, per_device, 1, 4 * per_device)
    near_shape = (devices_all, per_device, NEAR, 4 * per_device)
    noise = jax.random.randint(streams[2], near_shape, 0, 2 ** 16, dtype=jnp.int32) * (4 * per_device) + jnp.arange(4 * per_device, dtype=jnp.int32)
    scores = noise + priority
    best = lax.top_k(scores, 1)[1][..., 0].astype(jnp.int32)
    corner_pick = best // per_device
    slot_pick = best % per_device
    chosen = jnp.sum(jnp.where(corner_pick[..., None] == corner_ids, partners[:, :, None, :], 0), axis=-1).astype(jnp.int32)
    near_ids = (chosen * per_device + slot_pick).astype(jnp.int32)
    contact_shape = (devices_all, CONT_DEV)
    first_local = jax.random.randint(streams[6], contact_shape, 0, counts[:, None], dtype=jnp.int32)
    which_entry = jax.random.randint(streams[7], contact_shape, 0, NEAR, dtype=jnp.int32)
    second_ids = near_ids[device_ids[:, None], first_local, which_entry]
    first_ids = device_ids[:, None] * per_device + first_local
    pairs = jnp.stack([first_ids.reshape(-1), second_ids.reshape(-1)]).astype(jnp.int32)
    anchor_shape = (devices_all, per_device)
    pencil_x = GRID // N_WIDE
    pencil_y = GRID // N_NARROW
    step_x = jnp.minimum(jax.random.randint(streams[8], anchor_shape, 0, 2, dtype=jnp.int32), pencil_x - 1)
    step_y = jnp.minimum(jax.random.randint(streams[9], anchor_shape, 0, 2, dtype=jnp.int32), pencil_y - 1)
    anchor_x = wide_ids[:, None] * pencil_x + jnp.where(side_x[None, :] == 1, pencil_x - 1 - step_x, step_x)
    anchor_y = narrow_ids[:, None] * pencil_y + jnp.where(side_y[None, :] == 1, pencil_y - 1 - step_y, step_y)
    corner_w = (wide_ids[:, None] + side_x[None, :]) % N_WIDE
    corner_n = (narrow_ids[:, None] + side_y[None, :]) % N_NARROW
    base_z = jax.random.randint(streams[10], (devices_all,), 0, GRID, dtype=jnp.int32)
    step_z = jax.random.randint(streams[11], anchor_shape, 0, 3, dtype=jnp.int32)
    anchor_z = (base_z[corner_w * N_NARROW + corner_n] + step_z) % GRID
    anchors = jnp.stack([anchor_x, anchor_y, anchor_z], axis=-1).astype(jnp.int32)
    return (to_grid(occupied), to_grid(anchors), to_grid(near_ids), pairs)


def draw_occupied(key, part):
    return geometry(key)[0]


def draw_anchors(key, part):
    return geometry(key)[1]


def draw_near_list(key, part):
    return geometry(key)[2]


def draw_contact_pairs(key, part):
    return geometry(key)[3]


def draw_centers(key, part):
    anchors = geometry(key)[1].astype(jnp.float32)
    jitter = jax.random.uniform(jax.random.fold_in(key, 57), anchors.shape, jnp.float32, -0.5, 0.5)
    return anchors + BLOCK // 2 + jitter


def block_scale(rng, extent, pieces, smallest, largest):
    def one(axis_at, shards_of):
        steps = jax.random.uniform(jax.random.fold_in(jax.random.fold_in(rng, 6), axis_at), (shards_of,), jnp.float32, smallest / len(pieces), largest / len(pieces))
        return jnp.repeat(jnp.exp(steps), extent[axis_at] // shards_of).reshape((-1,) + (1,) * (len(extent) - axis_at - 1))

    gain = one(*pieces[0])
    for cut in pieces[1:]:
        gain = gain * one(*cut)
    return gain


def normal_values(rng, extent, scale, reach, cuts=(), kind=jnp.bfloat16):
    entries = scale * jax.random.normal(rng, extent, jnp.float32)
    if cuts:
        entries = entries * block_scale(rng, extent, cuts, -0.22, 0.18)
    return jnp.clip(entries, -reach, reach).astype(kind)


def setup_inputs(seed: int = 0) -> dict:
    keys = jax.random.split(jax.random.key(seed), 10)
    return {
        "tractions": normal_values(keys[0], (ROWS, COLS, 3, NODES), 1.0, 6.0, ((0, 8), (1, 4)), jnp.float32),
        "centers": draw_centers(jax.random.fold_in(keys[9], 71), 0),
        "node_offsets": jnp.clip(jax.random.uniform(keys[2], (3, NODES), jnp.float32, -3.0, 3.0), -3.0, 3.0),
        "occupied": draw_occupied(jax.random.fold_in(keys[9], 71), 0),
        "anchors": draw_anchors(jax.random.fold_in(keys[9], 71), 0),
        "near_list": draw_near_list(jax.random.fold_in(keys[9], 71), 0),
        "contact_pairs": draw_contact_pairs(jax.random.fold_in(keys[9], 71), 0),
        "contact_gap": jnp.clip(jax.random.uniform(keys[7], (CONTACTS,), jnp.float32, -1.0, 1.0) * block_scale(keys[7], (CONTACTS,), ((0, 32),), -0.4, 0.0), -1.0, 1.0),
        "contact_angles": jnp.clip(jax.random.uniform(keys[8], (2, CONTACTS), jnp.float32, -3.140625, 3.140625), -3.140625, 3.140625),
    }


soften = 1.0
screen = 0.0625
near_scale = 0.05
spread_norm = 0.17958712212516656
mobility = 0.2
time_step = 0.5
relaxation = 0.35
ewald_split = 0.5

def block_weights(coordinate, anchor_cell):
    cell_centres = anchor_cell.astype(jnp.float32) + jnp.arange(BLOCK).astype(jnp.float32)
    distance = coordinate[:, None] - cell_centres[None, :]
    return jnp.exp(-distance * distance)

def spread_block(forces, position, anchor):
    weight_x = block_weights(position[0], anchor[0])
    weight_y = block_weights(position[1], anchor[1])
    weight_z = block_weights(position[2], anchor[2])
    planar = weight_x[:, :, None] * weight_y[:, None, :]
    loaded = forces[:, :, None, None] * planar[None]
    return spread_norm * jnp.einsum('cnab,ne->cabe', loaded, weight_z, precision=lax.Precision.HIGHEST)

def interp_block(mesh_block, position, anchor):
    weight_x = block_weights(position[0], anchor[0])
    weight_y = block_weights(position[1], anchor[1])
    weight_z = block_weights(position[2], anchor[2])
    along_z = jnp.einsum('cabe,ne->cabn', mesh_block, weight_z, precision=lax.Precision.HIGHEST)
    along_y = jnp.einsum('cabn,nb->can', along_z, weight_y, precision=lax.Precision.HIGHEST)
    return spread_norm * jnp.einsum('can,na->cn', along_y, weight_x, precision=lax.Precision.HIGHEST)

def stokes_tile(displacement, offsets, forces):
    separation = [displacement[component] + offsets[component][:, None] - offsets[component][None, :] for component in range(3)]
    radius_sq = separation[0] * separation[0] + separation[1] * separation[1] + separation[2] * separation[2]
    softened = radius_sq + soften
    weight = jnp.exp(-radius_sq * screen) / (softened * jnp.sqrt(softened))
    projected = separation[0] * forces[0][None, :] + separation[1] * forces[1][None, :] + separation[2] * forces[2][None, :]
    diagonal = (radius_sq + 2.0 * soften) * weight
    velocity = [lax.optimization_barrier(jnp.sum(diagonal * forces[component][None, :] + separation[component] * projected * weight, axis=1)) for component in range(3)]
    return near_scale * jnp.stack(velocity)

def nearest_image(difference):
    return difference - GRID * jnp.floor(difference / GRID + 0.5)

def far_kernel(wave_x, wave_y, wave_z, real_part, imag_part):
    wave_sq = wave_x * wave_x + wave_y * wave_y + wave_z * wave_z
    safe_sq = jnp.maximum(wave_sq, 1.0)
    damping = (ewald_split * jnp.pi / GRID) ** 2
    factor = jnp.where(wave_sq > 0.5, jnp.exp(-damping * wave_sq) / safe_sq, 0.0) * (GRID * GRID / (4.0 * jnp.pi * jnp.pi))
    waves = (wave_x, wave_y, wave_z)
    results = []
    for values in (real_part, imag_part):
        inner = waves[0] * values[0] + waves[1] * values[1] + waves[2] * values[2]
        results.append(jnp.stack([factor * (values[component] - waves[component] * inner / safe_sq) for component in range(3)]))
    return (results[0], results[1])

def flatten_slots(array):
    trailing = array.shape[2:]
    shaped = array.reshape((N_WIDE, S_SIDE, N_NARROW, S_SIDE) + trailing)
    return jnp.swapaxes(shaped, 1, 2).reshape((SLOTS,) + trailing)

def unflatten_slots(array):
    trailing = array.shape[1:]
    shaped = array.reshape((N_WIDE, N_NARROW, S_SIDE, S_SIDE) + trailing)
    return jnp.swapaxes(shaped, 1, 2).reshape((ROWS, COLS) + trailing)

def fold_wrap(mesh, dimension):
    head = lax.slice_in_dim(mesh, 0, GRID, axis=dimension)
    tail = lax.slice_in_dim(mesh, GRID, GRID + BLOCK, axis=dimension)
    return lax.dynamic_update_slice_in_dim(head, lax.slice_in_dim(head, 0, BLOCK, axis=dimension) + tail, 0, dimension)

def reference(tractions, centers, node_offsets, occupied, anchors, near_list, contact_pairs, contact_gap, contact_angles):
    forces = flatten_slots(tractions)
    centres = flatten_slots(centers)
    live = flatten_slots(occupied).astype(jnp.float32)
    starts = flatten_slots(anchors).astype(jnp.int32)
    neighbours = flatten_slots(near_list).astype(jnp.int32)
    zero_index = jnp.zeros((), jnp.int32)
    padded = jnp.zeros((3, GRID + BLOCK, GRID + BLOCK, GRID + BLOCK), jnp.float32)

    def deposit(slot_index, buffer):
        corner = starts[slot_index]
        location = (zero_index, corner[0], corner[1], corner[2])
        sphere_block = spread_block(forces[slot_index] * live[slot_index], centres[slot_index][:, None] + node_offsets, corner)
        current = lax.dynamic_slice(buffer, location, (3, BLOCK, BLOCK, BLOCK))
        return lax.dynamic_update_slice(buffer, current + sphere_block, location)
    mesh = lax.fori_loop(0, SLOTS, deposit, padded)
    for dimension in (1, 2, 3):
        mesh = fold_wrap(mesh, dimension)
    spectrum = jnp.fft.fftn(mesh, axes=(1, 2, 3))
    waves = (jnp.fft.fftfreq(GRID) * GRID).astype(jnp.float32)
    out_real, out_imag = far_kernel(waves[:, None, None], waves[None, :, None], waves[None, None, :], jnp.real(spectrum), jnp.imag(spectrum))
    velocity_mesh = jnp.real(jnp.fft.ifftn(lax.complex(out_real, out_imag), axes=(1, 2, 3))).astype(jnp.float32)
    wrapped = jnp.concatenate([velocity_mesh, velocity_mesh[:, :BLOCK]], axis=1)
    wrapped = jnp.concatenate([wrapped, wrapped[:, :, :BLOCK]], axis=2)
    wrapped = jnp.concatenate([wrapped, wrapped[:, :, :, :BLOCK]], axis=3)

    def sample(slot_index):
        corner = starts[slot_index]
        mesh_block = lax.dynamic_slice(wrapped, (zero_index, corner[0], corner[1], corner[2]), (3, BLOCK, BLOCK, BLOCK))
        return interp_block(mesh_block, centres[slot_index][:, None] + node_offsets, corner)
    far = lax.map(sample, jnp.arange(SLOTS, dtype=jnp.int32))

    def near_one(slot_index):
        centre = centres[slot_index]
        summed = stokes_tile(jnp.zeros((3,), jnp.float32), node_offsets, forces[slot_index])
        for neighbour_rank in range(NEAR):
            neighbour = neighbours[slot_index, neighbour_rank]
            summed = summed + stokes_tile(nearest_image(centre - centres[neighbour]), node_offsets, forces[neighbour])
        return summed

    def near_group(group_index):
        return jax.vmap(near_one)(group_index * 8 + jnp.arange(8, dtype=jnp.int32))
    near = lax.map(near_group, jnp.arange(SLOTS // 8, dtype=jnp.int32)).reshape(SLOTS, 3, NODES)
    node_velocity = (near + far) * live[:, None, None]
    hydro = lax.optimization_barrier(jnp.mean(node_velocity, axis=2))
    first_ids = contact_pairs[0]
    second_ids = contact_pairs[1]
    polar = contact_angles[0]
    azimuth = contact_angles[1]
    normal = jnp.stack([jnp.sin(polar) * jnp.cos(azimuth), jnp.sin(polar) * jnp.sin(azimuth), jnp.cos(polar)], axis=1)

    def totals(magnitude):
        loading = magnitude[:, None] * normal
        return jax.ops.segment_sum(loading, first_ids, num_segments=SLOTS) - jax.ops.segment_sum(loading, second_ids, num_segments=SLOTS)
    magnitude = jnp.zeros_like(contact_gap)
    for sweep_index in range(SWEEPS):
        velocity = hydro + mobility * totals(magnitude)
        relative = lax.optimization_barrier(jnp.sum(normal * (velocity[first_ids] - velocity[second_ids]), axis=1))
        magnitude = jnp.maximum(magnitude - relaxation * (contact_gap + time_step * relative) / (2.0 * time_step * mobility), 0.0)
    moved = centres + time_step * (hydro + mobility * totals(magnitude))
    return (unflatten_slots(node_velocity), magnitude, unflatten_slots(moved))
```

```python
import jax
import jax.numpy as jnp
import numpy as np
from jax import lax
from jax.experimental import pallas as pl
from jax.experimental.pallas import tpu as pltpu
from jax.sharding import PartitionSpec as P

GRID = 256
HALF = GRID // 2
BLOCK = 16
SWEEPS = 6
MIN_PAIRS = 4
AXES = ("wide", "narrow")

soften = 1.0
screen = 0.0625
near_scale = 0.05
spread_norm = 0.17958712212516656
mobility = 0.2
time_step = 0.5
relaxation = 0.35
ewald_split = 0.5

F32 = jnp.float32
BF16 = jnp.bfloat16
NT = (((1,), (1,)), ((), ()))
NN = (((1,), (0,)), ((), ()))


def real_basis():
    cells = np.arange(GRID)
    angle = 2.0 * np.pi * (np.outer(cells, np.arange(HALF)) % GRID) / GRID
    sine = np.sin(angle)
    sine[:, 0] = np.cos(np.pi * cells)
    return np.concatenate([np.cos(angle), sine], axis=1)


def z_tables():
    pairs = np.arange(HALF)
    cells = np.arange(GRID + BLOCK)
    angle = 2.0 * np.pi * (np.outer(pairs, cells) % GRID) / GRID
    cosine, sine = np.cos(angle), np.sin(angle)
    nyquist = np.cos(np.pi * cells)
    xy = np.stack([cosine, sine], axis=1)
    zz = np.stack([-sine, cosine], axis=1)
    xy[0, 0] = zz[0, 0] = 1.0
    xy[0, 1] = zz[0, 1] = nyquist
    return xy, zz


def split_np(table):
    high = np.asarray(table, dtype=BF16)
    low = np.asarray(table - high.astype(np.float64), dtype=BF16)
    return high, low


def split2(value):
    high = value.astype(BF16)
    return high, (value - high.astype(F32)).astype(BF16)


def dot(a, b, dims=NN):
    return lax.dot_general(a, b, dims, preferred_element_type=F32)


def dot3(a, b, dims=NN):
    return dot(a[0], b[0], dims) + (dot(a[1], b[0], dims) + dot(a[0], b[1], dims))


def split_rows(value):
    high = value.astype(BF16).astype(F32)
    rest = value - high
    middle = rest.astype(BF16).astype(F32)
    return jnp.concatenate([high, middle, rest - middle], axis=0).astype(BF16)


def far_kernel(pairs, slots, devices, hydro_rows):
    rows_c = 2 * pairs
    rows = 3 * rows_c

    def kernel(
        misc,
        ranks,
        g_ref,
        off_ref,
        offt_ref,
        tab_ref,
        ryh,
        ryl,
        ryth,
        rytl,
        rxh,
        rxl,
        rxth,
        rxtl,
        out_ref,
        listed,
        acc,
        wyh,
        wyl,
        sbuf,
        hyd,
        ft,
    ):
        z_group, x_group, device = ranks[0], ranks[1], ranks[2]
        nodes = off_ref.shape[1]
        half_x = rxh.shape[1] // 2

        def clear(i, c):
            at = pl.ds(pl.multiple_of(i * 192, 64), 192)
            acc[0, at, :] = jnp.zeros((192, HALF), F32)
            acc[1, at, :] = jnp.zeros((192, HALF), F32)
            return c

        lax.fori_loop(0, acc.shape[1] // 192, clear, 0)
        wyh[...] = jnp.zeros(wyh.shape, BF16)
        wyl[...] = jnp.zeros(wyl.shape, BF16)
        hyd[...] = jnp.zeros(hyd.shape, F32)

        def clear_out(i, c):
            out_ref[i] = jnp.zeros(out_ref.shape[1:], F32)
            return c

        lax.fori_loop(0, slots, clear_out, 0)

        def scan(s, n):
            held = misc[s * 16 + 6] > 0.5

            @pl.when(held)
            def _():
                listed[n] = s

            return n + held.astype(jnp.int32)

        count = lax.fori_loop(0, slots, scan, jnp.int32(0))
        steps = lax.broadcasted_iota(jnp.int32, (BLOCK, nodes), 0)

        def prepare(s):
            anchor = [misc[s * 16 + 3 + d].astype(jnp.int32) for d in range(3)]
            pos = [off_ref[d : d + 1, :] + misc[s * 16 + d] for d in range(3)]

            def weights(d, shift):
                away = pos[d] - (anchor[d] + steps + shift).astype(F32)
                return jnp.exp(-away * away)

            wx = weights(0, 0)
            wz = weights(2, 0)
            first = anchor[1] // BLOCK
            inner = anchor[1] % BLOCK
            places = []
            for i in range(2):
                t = steps + (i * BLOCK - inner)
                wy = jnp.where((t >= 0) & (t < BLOCK), weights(1, i * BLOCK - inner), 0.0)
                row = pl.multiple_of(((first + i) % (GRID // BLOCK)) * BLOCK, BLOCK)
                high, low = split2(wy)
                wyh[pl.ds(row, BLOCK), :] = high
                wyl[pl.ds(row, BLOCK), :] = low
                places.append(row)
            table = jnp.zeros((2 * rows_c, nodes), F32)
            for t in range(BLOCK):
                phase = tab_ref[anchor[2] + t]
                phase = jnp.concatenate([phase] * (nodes // 128), axis=1)
                table = table + phase * wz[t : t + 1, :]
            zed = jnp.concatenate([table[:rows_c], table], axis=0)
            return anchor, wx, zed, places

        def forget(places):
            for row in places:
                wyh[pl.ds(row, BLOCK), :] = jnp.zeros((BLOCK, nodes), BF16)
                wyl[pl.ds(row, BLOCK), :] = jnp.zeros((BLOCK, nodes), BF16)

        def spread(i, c):
            s = listed[i]
            anchor, wx, zed, places = prepare(s)
            force = jnp.concatenate(
                [jnp.broadcast_to(g_ref[s, d : d + 1, :], (rows_c, nodes)) for d in range(3)], axis=0
            )
            loaded = force * zed
            left = jnp.concatenate([loaded * wx[a : a + 1, :] for a in range(BLOCK)], axis=0)
            patch = dot3(split2(left), (wyh[...], wyl[...]), NT)
            where = pl.ds(pl.multiple_of(anchor[0] * rows, rows), BLOCK * rows)
            acc[0, where, :] = acc[0, where, :] + patch[:, :HALF]
            acc[1, where, :] = acc[1, where, :] + patch[:, HALF:]
            forget(places)
            return c

        lax.fori_loop(0, count, spread, 0)
        acc[:, : BLOCK * rows, :] = acc[:, : BLOCK * rows, :] + acc[:, GRID * rows :, :]

        damping = (ewald_split * np.pi / GRID) ** 2
        constant = spread_norm**2 * GRID * GRID / (4.0 * np.pi**2) / GRID**3
        k_lane = lax.broadcasted_iota(jnp.int32, (8, HALF), 1).astype(F32)
        y_edge = jnp.where(k_lane == 0.0, float(HALF), 0.0)
        ky = ((k_lane, jnp.zeros_like(k_lane)), (k_lane, y_edge))
        y_factor = jnp.where(k_lane == 0.0, 1.0, 2.0)

        def wave_slot(r, c):
            pair = z_group * pairs + r // 2
            is_first = pair == 0
            kz = jnp.where(is_first, 0, pair).astype(F32)
            nz = jnp.where(is_first & (r % 2 == 1), HALF, 0).astype(F32)
            kz2 = kz * kz + nz * nz
            z_factor = jnp.where(is_first, 1.0, 2.0) * constant
            for comp in range(3):
                line = pl.ds(comp * rows_c + r, GRID, stride=rows)
                data = jnp.concatenate([acc[0, line, :], acc[1, line, :]], axis=1)
                mid = dot3(split2(data), (ryh[...], ryl[...]))
                sbuf[comp] = dot3((rxth[...], rxtl[...]), split2(mid))

            def filtered(i, c2):
                row = pl.multiple_of(i * 8, 8)
                k_row = (
                    lax.broadcasted_iota(jnp.int32, (8, HALF), 0) + (row + x_group * half_x)
                ).astype(F32)
                x_edge = jnp.where(k_row == 0.0, float(HALF), 0.0)
                kxn = (None, x_edge)
                scale = jnp.where(k_row == 0.0, 1.0, 2.0) * y_factor * z_factor
                spectrum = [
                    [
                        [
                            sbuf[comp, pl.ds(row + hx * half_x, 8), hy * HALF : (hy + 1) * HALF]
                            for hy in range(2)
                        ]
                        for hx in range(2)
                    ]
                    for comp in range(3)
                ]
                sx, sy, sz = spectrum
                total = [[None, None], [None, None]]
                for hx in range(2):
                    for hy in range(2):
                        jx = sx[0][hy] if hx else -sx[1][hy]
                        jy = sy[hx][0] if hy else -sy[hx][1]
                        total[hx][hy] = k_row * jx + k_lane * jy + kz * sz[hx][hy]
                for hx in range(2):
                    for hy in range(2):
                        square = k_row * k_row + k_lane * k_lane + kz2
                        edge = nz * sz[hx][hy]
                        if hx:
                            square = square + x_edge * x_edge
                            edge = edge + x_edge * sx[hx][hy]
                        if hy:
                            square = square + y_edge * y_edge
                            edge = edge + y_edge * sy[hx][hy]
                        inverse = 1.0 / jnp.maximum(square, 1.0)
                        factor = jnp.where(
                            square > 0.5, jnp.exp(-damping * square) * inverse, 0.0
                        ) * scale
                        tx = total[0][hy] if hx else -total[1][hy]
                        ty = total[hx][0] if hy else -total[hx][1]
                        along_x = k_row * tx
                        along_y = k_lane * ty
                        if hx:
                            along_x = along_x - x_edge * edge
                        if hy:
                            along_y = along_y - y_edge * edge
                        along_z = kz * total[hx][hy] + nz * edge
                        lanes = slice(hy * HALF, (hy + 1) * HALF)
                        at = pl.ds(row + hx * half_x, 8)
                        sbuf[0, at, lanes] = factor * (sx[hx][hy] + along_x * inverse)
                        sbuf[1, at, lanes] = factor * (sy[hx][hy] + along_y * inverse)
                        sbuf[2, at, lanes] = factor * (sz[hx][hy] - along_z * inverse)
                return c2

            lax.fori_loop(0, half_x // 8, filtered, 0)
            for comp in range(3):
                mid = dot3((rxh[...], rxl[...]), split2(sbuf[comp]))
                line = pl.ds(comp * rows_c + r, GRID, stride=rows)
                data = dot3(split2(mid), (ryth[...], rytl[...]))
                acc[0, line, :] = data[:, :HALF]
                acc[1, line, :] = data[:, HALF:]
            return c

        lax.fori_loop(0, rows_c, wave_slot, 0)
        acc[:, GRID * rows :, :] = acc[:, : BLOCK * rows, :]
        slot_lane = lax.broadcasted_iota(jnp.int32, (8, hyd.shape[1]), 1)

        def add_out(s, values):
            padded = jnp.concatenate([values, jnp.zeros((5, nodes), F32)], axis=0)
            out_ref[s, 0:3, :] = out_ref[s, 0:3, :] + values
            mean = jnp.sum(padded, axis=1, keepdims=True) * (1.0 / nodes)
            hyd[...] = hyd[...] + jnp.where(slot_lane == s, mean, 0.0)

        def sample(i, c):
            s = listed[i]
            anchor, wx, zed, places = prepare(s)
            where = pl.ds(pl.multiple_of(anchor[0] * rows, rows), BLOCK * rows)
            near_mesh = jnp.concatenate([acc[0, where, :], acc[1, where, :]], axis=1)
            seen = dot3(split2(near_mesh), (wyh[...], wyl[...]))
            total = seen[:rows] * wx[0:1, :]
            for a in range(1, BLOCK):
                total = total + seen[a * rows : (a + 1) * rows] * wx[a : a + 1, :]
            total = total * zed
            values = jnp.concatenate(
                [
                    jnp.sum(total[d * rows_c : (d + 1) * rows_c], axis=0, keepdims=True)
                    for d in range(3)
                ],
                axis=0,
            )
            add_out(s, values)
            forget(places)
            return c

        lax.fori_loop(0, count, sample, 0)

        chunk = 16

        def near_task(i, c):
            task = device + i * devices
            s = listed[task // 3]
            which = task % 3
            source = jnp.where(
                which == 0, s, misc[s * 16 + 6 + jnp.maximum(which, 1)].astype(jnp.int32)
            )
            force = jnp.concatenate(
                [g_ref[source, 0:3, :], jnp.zeros((5, nodes), F32)], axis=0
            )
            ft[...] = force.T
            shifted = []
            for d in range(3):
                gap = jnp.full((1, nodes), misc[s * 16 + d] - misc[source * 16 + d], F32)
                gap = gap - GRID * jnp.floor(gap / GRID + 0.5)
                gap = jnp.where(which == 0, 0.0, gap)
                shifted.append(gap + off_ref[d : d + 1, :])

            def part(j, sums):
                at = pl.ds(pl.multiple_of(j * chunk, chunk), chunk)
                own = offt_ref[at, :]
                push = ft[at, :]
                sep = [shifted[d] - own[:, d : d + 1] for d in range(3)]
                pushes = [push[:, d : d + 1] for d in range(3)]
                square = sep[0] * sep[0] + sep[1] * sep[1] + sep[2] * sep[2]
                root = lax.rsqrt(square + soften)
                weight = jnp.exp(-square * screen) * (root * root * root)
                projected = sep[0] * pushes[0] + sep[1] * pushes[1] + sep[2] * pushes[2]
                diagonal = (square + 2.0 * soften) * weight
                leaning = projected * weight
                new = []
                for d in range(3):
                    value = diagonal * pushes[d] + sep[d] * leaning
                    new.append(sums[d] + (value[:8] + value[8:]))
                return tuple(new)

            zero = jnp.zeros((8, nodes), F32)
            sums = lax.fori_loop(0, nodes // chunk, part, (zero, zero, zero), unroll=2)
            values = jnp.concatenate(
                [jnp.sum(v, axis=0, keepdims=True) for v in sums], axis=0
            )
            add_out(s, near_scale * values)
            return c

        tasks = (3 * count - device + (devices - 1)) // devices
        lax.fori_loop(0, tasks, near_task, 0)
        per_device = slots // devices

        def publish(holder, c):
            for d in range(3):
                for h in range(hydro_rows):
                    low = h * nodes
                    high = min(low + nodes, hyd.shape[1])
                    out_ref[holder * per_device + d, 3 + h : 4 + h, : high - low] = hyd[
                        d : d + 1, low:high
                    ]
            return c

        lax.fori_loop(0, devices, publish, 0)

    return kernel


def contact_kernel(slots, devices, hydro_rows):
    per_device = slots // devices

    def kernel(recv_ref, contacts_ref, velocity_ref, force_ref, drift_ref, incidence, loads):
        contacts = contacts_ref.shape[1]

        def gather(holder, total):
            return total + recv_ref[pl.ds(holder * per_device, per_device)]

        summed = lax.fori_loop(
            1, devices, gather, recv_ref[pl.ds(0, per_device)]
        )
        velocity_ref[...] = summed[:, :3, :]
        hydro = jnp.concatenate(
            [
                jnp.concatenate(
                    [summed[d, 3 + h : 4 + h, :] for h in range(hydro_rows)], axis=1
                )[:, :slots]
                for d in range(3)
            ]
            + [jnp.zeros((5, slots), F32)],
            axis=0,
        )
        first = contacts_ref[0:1, :].astype(jnp.int32)
        second = contacts_ref[1:2, :].astype(jnp.int32)
        gap = contacts_ref[2:3, :]
        polar = contacts_ref[3:4, :]
        azimuth = contacts_ref[4:5, :]
        normal = jnp.concatenate(
            [
                jnp.sin(polar) * jnp.cos(azimuth),
                jnp.sin(polar) * jnp.sin(azimuth),
                jnp.cos(polar),
                jnp.zeros((5, contacts), F32),
            ],
            axis=0,
        )

        def build(i, c):
            row = pl.multiple_of(i * 16, 16)
            ids = lax.broadcasted_iota(jnp.int32, (16, contacts), 0) + row
            value = jnp.where(first == ids, 1.0, 0.0) - jnp.where(second == ids, 1.0, 0.0)
            incidence[pl.ds(row, 16), :] = value.astype(BF16)
            return c

        lax.fori_loop(0, slots // 16, build, 0)

        def totals(magnitude):
            spread = dot(split_rows(magnitude * normal), incidence[...], NT)
            return spread[0:8] + (spread[8:16] + spread[16:24])

        def sweep(i, magnitude):
            velocity = hydro + mobility * totals(magnitude)
            seen = dot(split_rows(velocity), incidence[...])
            relative = jnp.sum(
                normal * (seen[0:8] + (seen[8:16] + seen[16:24])), axis=0, keepdims=True
            )
            return jnp.maximum(
                magnitude
                - relaxation * (gap + time_step * relative) / (2.0 * time_step * mobility),
                0.0,
            )

        magnitude = lax.fori_loop(0, SWEEPS, sweep, jnp.zeros((1, contacts), F32))
        force_ref[...] = magnitude
        drift_ref[...] = time_step * (hydro + mobility * totals(magnitude))

    return kernel


def local(
    tractions,
    centers,
    node_offsets,
    occupied,
    anchors,
    near_list,
    contact_pairs,
    contact_gap,
    contact_angles,
):
    side = tractions.shape[0]
    per_device = side * side
    nodes = tractions.shape[3]
    near = near_list.shape[2]
    narrow_count = lax.axis_size("narrow")
    devices = lax.axis_size("wide") * narrow_count
    rank = lax.axis_index("wide") * narrow_count + lax.axis_index("narrow")
    slots = devices * per_device
    contacts_own = contact_gap.shape[0]
    contacts = contacts_own * devices
    pairs = max(MIN_PAIRS, HALF // devices)
    z_groups = HALF // pairs
    x_groups = max(1, devices // z_groups)
    half_x = HALF // x_groups
    z_group = rank % z_groups
    x_group = rank // z_groups
    rows = 6 * pairs
    hydro_rows = -(-slots // nodes)

    fields = jnp.concatenate(
        [
            contact_pairs.astype(F32),
            contact_gap[None],
            contact_angles,
        ],
        axis=0,
    ).reshape(per_device, -1)
    misc = jnp.concatenate(
        [
            centers.reshape(per_device, 3),
            anchors.reshape(per_device, 3).astype(F32),
            occupied.reshape(per_device, 1).astype(F32),
            near_list.reshape(per_device, near).astype(F32),
            jnp.zeros((per_device, 16 - 7 - near), F32),
            fields,
        ],
        axis=1,
    )
    misc = jnp.pad(misc, ((0, 0), (0, nodes - misc.shape[1])))
    own = jnp.concatenate([tractions.reshape(per_device, 3, nodes), misc[:, None]], axis=1)
    packed = jnp.broadcast_to(own[None], (devices,) + own.shape).reshape(slots, 4, nodes)
    gathered = lax.all_to_all(packed, AXES, split_axis=0, concat_axis=0, tiled=True)
    scalars = gathered[:, 3, :16].reshape(slots * 16)

    xy, zz = z_tables()
    tables = np.concatenate(
        [
            xy.reshape(z_groups, 2 * pairs, GRID + BLOCK),
            zz.reshape(z_groups, 2 * pairs, GRID + BLOCK),
        ],
        axis=1,
    ).transpose(0, 2, 1)
    table = lax.dynamic_index_in_dim(jnp.asarray(tables, F32), z_group, 0, keepdims=False)
    table = jnp.broadcast_to(table[:, :, None], table.shape + (128,))
    basis = real_basis()
    turned = np.ascontiguousarray(basis.T)
    ry = [jnp.asarray(v) for v in split_np(basis)]
    ryt = [jnp.asarray(v) for v in split_np(turned)]
    if x_groups == 1:
        rx, rxt = ry, ryt
    else:
        rxt = [
            lax.dynamic_index_in_dim(
                v.reshape(2, x_groups, half_x, GRID), x_group, 1, keepdims=False
            ).reshape(2 * half_x, GRID)
            for v in ryt
        ]
        rx = [v.T for v in rxt]

    vmem = pl.BlockSpec(memory_space=pltpu.VMEM)
    smem = pl.BlockSpec(memory_space=pltpu.SMEM)
    ranks = jnp.stack([z_group, x_group, rank]).astype(jnp.int32)
    partial = pl.pallas_call(
        far_kernel(pairs, slots, devices, hydro_rows),
        out_shape=jax.ShapeDtypeStruct((slots, 3 + hydro_rows, nodes), F32),
        in_specs=[smem, smem] + [vmem] * 12,
        out_specs=vmem,
        scratch_shapes=[
            pltpu.SMEM((slots,), jnp.int32),
            pltpu.VMEM((2, (GRID + BLOCK) * rows, HALF), F32),
            pltpu.VMEM((GRID, nodes), BF16),
            pltpu.VMEM((GRID, nodes), BF16),
            pltpu.VMEM((3, 2 * half_x, GRID), F32),
            pltpu.VMEM((8, slots), F32),
            pltpu.VMEM((nodes, 8), F32),
        ],
        compiler_params=pltpu.CompilerParams(vmem_limit_bytes=60 * 1024 * 1024),
        name="far_near",
    )(
        scalars,
        ranks,
        gathered,
        node_offsets,
        node_offsets.T,
        table,
        *ry,
        *ryt,
        *rx,
        *rxt,
    )
    received = lax.all_to_all(partial, AXES, split_axis=0, concat_axis=0, tiled=True)
    listed = gathered[:, 3, 16 : 16 + fields.shape[1]].reshape(devices, 5, contacts_own)
    listed = listed.transpose(1, 0, 2).reshape(5, contacts)
    velocity, magnitude, drift = pl.pallas_call(
        contact_kernel(slots, devices, hydro_rows),
        out_shape=(
            jax.ShapeDtypeStruct((per_device, 3, nodes), F32),
            jax.ShapeDtypeStruct((1, contacts), F32),
            jax.ShapeDtypeStruct((8, slots), F32),
        ),
        in_specs=[vmem, vmem],
        out_specs=(vmem, vmem, vmem),
        scratch_shapes=[
            pltpu.VMEM((slots, contacts), BF16),
            pltpu.VMEM((8, 128), F32),
        ],
        compiler_params=pltpu.CompilerParams(vmem_limit_bytes=60 * 1024 * 1024),
        name="contacts",
    )(received, listed)
    own_force = lax.dynamic_slice(magnitude, (0, rank * contacts_own), (1, contacts_own))[0]
    own_drift = lax.dynamic_slice(drift, (0, rank * per_device), (3, per_device)).T
    moved = centers + own_drift.reshape(side, side, 3)
    return (velocity.reshape(side, side, 3, nodes), own_force, moved)


def solution(mesh):
    placed = (
        P("wide", "narrow", None, None),
        P("wide", "narrow", None),
        P(),
        P("wide", "narrow"),
        P("wide", "narrow", None),
        P("wide", "narrow", None),
        P(None, ("wide", "narrow")),
        P(("wide", "narrow")),
        P(None, ("wide", "narrow")),
    )
    return jax.shard_map(
        local,
        mesh=mesh,
        in_specs=placed,
        out_specs=(
            P("wide", "narrow", None, None),
            P(("wide", "narrow")),
            P("wide", "narrow", None),
        ),
        check_vma=False,
    )
```

```python
import jax
import jax.numpy as jnp
import numpy as np
from jax import lax
from jax.experimental import pallas as pl
from jax.experimental.pallas import tpu as pltpu
from jax.sharding import PartitionSpec as P

GRID = 256
HALF = GRID // 2
BLOCK = 16
SWEEPS = 6
MIN_PAIRS = 4
AXES = ("wide", "narrow")
UNROLL = 4

soften = 1.0
screen = 0.0625
near_scale = 0.05
spread_norm = 0.17958712212516656
mobility = 0.2
time_step = 0.5
relaxation = 0.35
ewald_split = 0.5

F32 = jnp.float32
BF16 = jnp.bfloat16
NT = (((1,), (1,)), ((), ()))
NN = (((1,), (0,)), ((), ()))


def real_basis():
    cells = np.arange(GRID)
    angle = 2.0 * np.pi * (np.outer(cells, np.arange(HALF)) % GRID) / GRID
    sine = np.sin(angle)
    sine[:, 0] = np.cos(np.pi * cells)
    return np.concatenate([np.cos(angle), sine], axis=1)


def z_tables():
    pairs = np.arange(HALF)
    cells = np.arange(GRID + BLOCK)
    angle = 2.0 * np.pi * (np.outer(pairs, cells) % GRID) / GRID
    cosine, sine = np.cos(angle), np.sin(angle)
    nyquist = np.cos(np.pi * cells)
    xy = np.stack([cosine, sine], axis=1)
    zz = np.stack([-sine, cosine], axis=1)
    xy[0, 0] = zz[0, 0] = 1.0
    xy[0, 1] = zz[0, 1] = nyquist
    return xy, zz


def split_np(table):
    high = np.asarray(table, dtype=BF16)
    low = np.asarray(table - high.astype(np.float64), dtype=BF16)
    return high, low


def split2(value):
    high = value.astype(BF16)
    return high, (value - high.astype(F32)).astype(BF16)


def dot(a, b, dims=NN):
    return lax.dot_general(a, b, dims, preferred_element_type=F32)


def dot3(a, b, dims=NN):
    return dot(a[0], b[0], dims) + (dot(a[1], b[0], dims) + dot(a[0], b[1], dims))


def split_rows(value):
    high = value.astype(BF16).astype(F32)
    rest = value - high
    middle = rest.astype(BF16).astype(F32)
    return jnp.concatenate([high, middle, rest - middle], axis=0).astype(BF16)


def far_kernel(pairs, slots, devices, hydro_rows):
    rows_c = 2 * pairs
    rows = 3 * rows_c

    def kernel(
        misc,
        ranks,
        g_ref,
        off_ref,
        offt_ref,
        tab_ref,
        ryh,
        ryl,
        ryth,
        rytl,
        rxh,
        rxl,
        rxth,
        rxtl,
        out_ref,
        listed,
        acc,
        wy,
        sbuf,
        hyd,
        ft,
    ):
        z_group, x_group, device = ranks[0], ranks[1], ranks[2]
        nodes = off_ref.shape[1]
        half_x = rxh.shape[1] // 2

        def clear(i, c):
            at = pl.ds(pl.multiple_of(i * 192, 64), 192)
            for tile in range(4):
                acc[tile, at, :] = jnp.zeros((192, HALF), F32)
            return c

        lax.fori_loop(0, acc.shape[1] // 192, clear, 0)
        wy[...] = jnp.zeros(wy.shape, BF16)
        hyd[...] = jnp.zeros(hyd.shape, F32)

        def clear_out(i, c):
            out_ref[i] = jnp.zeros(out_ref.shape[1:], F32)
            return c

        lax.fori_loop(0, slots, clear_out, 0)

        def scan(s, n):
            held = misc[s * 16 + 6] > 0.5

            @pl.when(held)
            def _():
                listed[n] = s

            return n + held.astype(jnp.int32)

        count = lax.fori_loop(0, slots, scan, jnp.int32(0))
        steps = lax.broadcasted_iota(jnp.int32, (BLOCK, nodes), 0)

        def prepare(s, buffer, doubled):
            anchor = [misc[s * 16 + 3 + d].astype(jnp.int32) for d in range(3)]
            pos = [off_ref[d : d + 1, :] + misc[s * 16 + d] for d in range(3)]

            def weights(d, shift):
                away = pos[d] - (anchor[d] + steps + shift).astype(F32)
                return jnp.exp(-away * away)

            wx = weights(0, 0)
            wz = weights(2, 0)
            local_y = anchor[1] % HALF
            late = (local_y > HALF - BLOCK).astype(jnp.int32)
            local_y = local_y - late * (HALF // 2)
            tile = 2 * (anchor[1] // HALF) + late
            first = local_y // BLOCK
            inner = local_y % BLOCK
            places = []
            for i in range(2):
                t = steps + (i * BLOCK - inner)
                value = jnp.where((t >= 0) & (t < BLOCK), weights(1, i * BLOCK - inner), 0.0)
                high, low = split2(value)
                near_row = ((first + i) % 8) * BLOCK
                if doubled:
                    writes = (
                        (near_row, high),
                        (((first + i + 4) % 8) * BLOCK, low),
                        (near_row + HALF, high),
                    )
                else:
                    writes = ((near_row, high), (near_row + HALF, low))
                for row, part in writes:
                    row = pl.multiple_of(row, BLOCK)
                    wy[buffer, pl.ds(row, BLOCK), :] = part
                    places.append(row)
            table = jnp.zeros((2 * rows_c, nodes), F32)
            for t in range(BLOCK):
                phase = tab_ref[anchor[2] + t]
                phase = jnp.concatenate([phase] * (nodes // 128), axis=1)
                table = table + phase * wz[t : t + 1, :]
            zed = jnp.concatenate([table[:rows_c], table], axis=0)
            where = pl.ds(pl.multiple_of(anchor[0] * rows, rows), BLOCK * rows)
            return where, tile, local_y, wx, zed, places

        def forget(buffer, places):
            for row in places:
                wy[buffer, pl.ds(row, BLOCK), :] = jnp.zeros((BLOCK, nodes), BF16)

        def members(i):
            found = []
            for u in range(UNROLL):
                at = i * UNROLL + u
                there = (at < count).astype(F32)
                found.append((listed[jnp.minimum(at, count - 1)], there))
            return found

        trips = (count + (UNROLL - 1)) // UNROLL

        def spread(i, c):
            group = members(i)
            ready = [prepare(s, u, False) for u, (s, _) in enumerate(group)]
            patches = []
            for u, (s, there) in enumerate(group):
                _, _, _, wx, zed, _ = ready[u]
                force = jnp.concatenate(
                    [
                        jnp.broadcast_to(g_ref[s, d : d + 1, :] * there, (rows_c, nodes))
                        for d in range(3)
                    ],
                    axis=0,
                )
                loaded = force * zed
                left = jnp.concatenate([loaded * wx[a : a + 1, :] for a in range(BLOCK)], axis=0)
                high, low = split2(left)
                upper = dot(high, wy[u], NT)
                lower = dot(low, wy[u], NT)
                patches.append(upper[:, :HALF] + (upper[:, HALF:] + lower[:, :HALF]))
            for u, patch in enumerate(patches):
                where, tile, _, _, _, places = ready[u]
                acc[tile, where, :] = acc[tile, where, :] + patch
                forget(u, places)
            return c

        lax.fori_loop(0, trips, spread, 0)
        acc[:, : BLOCK * rows, :] = acc[:, : BLOCK * rows, :] + acc[:, GRID * rows :, :]
        low_half = lax.broadcasted_iota(jnp.int32, (GRID, HALF), 1) < HALF // 2

        def turned(value):
            return pltpu.roll(value, HALF // 2, 1)

        damping = (ewald_split * np.pi / GRID) ** 2
        constant = spread_norm**2 * GRID * GRID / (4.0 * np.pi**2) / GRID**3
        k_lane = lax.broadcasted_iota(jnp.int32, (8, HALF), 1).astype(F32)
        y_edge = jnp.where(k_lane == 0.0, float(HALF), 0.0)
        ky = ((k_lane, jnp.zeros_like(k_lane)), (k_lane, y_edge))
        y_factor = jnp.where(k_lane == 0.0, 1.0, 2.0)

        def wave_slot(r, c):
            pair = z_group * pairs + r // 2
            is_first = pair == 0
            kz = jnp.where(is_first, 0, pair).astype(F32)
            nz = jnp.where(is_first & (r % 2 == 1), HALF, 0).astype(F32)
            kz2 = kz * kz + nz * nz
            z_factor = jnp.where(is_first, 1.0, 2.0) * constant
            for comp in range(3):
                line = pl.ds(comp * rows_c + r, GRID, stride=rows)
                odd0, odd1 = turned(acc[1, line, :]), turned(acc[3, line, :])
                data = jnp.concatenate(
                    [
                        acc[0, line, :] + jnp.where(low_half, odd1, odd0),
                        acc[2, line, :] + jnp.where(low_half, odd0, odd1),
                    ],
                    axis=1,
                )
                mid = dot3(split2(data), (ryh[...], ryl[...]))
                sbuf[comp] = dot3((rxth[...], rxtl[...]), split2(mid))

            def filtered(i, c2):
                row = pl.multiple_of(i * 8, 8)
                k_row = (
                    lax.broadcasted_iota(jnp.int32, (8, HALF), 0) + (row + x_group * half_x)
                ).astype(F32)
                x_edge = jnp.where(k_row == 0.0, float(HALF), 0.0)
                kxn = (None, x_edge)
                scale = jnp.where(k_row == 0.0, 1.0, 2.0) * y_factor * z_factor
                spectrum = [
                    [
                        [
                            sbuf[comp, pl.ds(row + hx * half_x, 8), hy * HALF : (hy + 1) * HALF]
                            for hy in range(2)
                        ]
                        for hx in range(2)
                    ]
                    for comp in range(3)
                ]
                sx, sy, sz = spectrum
                total = [[None, None], [None, None]]
                for hx in range(2):
                    for hy in range(2):
                        jx = sx[0][hy] if hx else -sx[1][hy]
                        jy = sy[hx][0] if hy else -sy[hx][1]
                        total[hx][hy] = k_row * jx + k_lane * jy + kz * sz[hx][hy]
                for hx in range(2):
                    for hy in range(2):
                        square = k_row * k_row + k_lane * k_lane + kz2
                        edge = nz * sz[hx][hy]
                        if hx:
                            square = square + x_edge * x_edge
                            edge = edge + x_edge * sx[hx][hy]
                        if hy:
                            square = square + y_edge * y_edge
                            edge = edge + y_edge * sy[hx][hy]
                        inverse = 1.0 / jnp.maximum(square, 1.0)
                        factor = jnp.where(
                            square > 0.5, jnp.exp(-damping * square) * inverse, 0.0
                        ) * scale
                        tx = total[0][hy] if hx else -total[1][hy]
                        ty = total[hx][0] if hy else -total[hx][1]
                        along_x = k_row * tx
                        along_y = k_lane * ty
                        if hx:
                            along_x = along_x - x_edge * edge
                        if hy:
                            along_y = along_y - y_edge * edge
                        along_z = kz * total[hx][hy] + nz * edge
                        lanes = slice(hy * HALF, (hy + 1) * HALF)
                        at = pl.ds(row + hx * half_x, 8)
                        sbuf[0, at, lanes] = factor * (sx[hx][hy] + along_x * inverse)
                        sbuf[1, at, lanes] = factor * (sy[hx][hy] + along_y * inverse)
                        sbuf[2, at, lanes] = factor * (sz[hx][hy] - along_z * inverse)
                return c2

            lax.fori_loop(0, half_x // 8, filtered, 0, unroll=2)
            for comp in range(3):
                mid = dot3((rxh[...], rxl[...]), split2(sbuf[comp]))
                line = pl.ds(comp * rows_c + r, GRID, stride=rows)
                data = dot3(split2(mid), (ryth[...], rytl[...]))
                even0, even1 = data[:, :HALF], data[:, HALF:]
                odd0, odd1 = turned(even0), turned(even1)
                acc[0, line, :] = even0
                acc[1, line, :] = jnp.where(low_half, odd0, odd1)
                acc[2, line, :] = even1
                acc[3, line, :] = jnp.where(low_half, odd1, odd0)
            return c

        lax.fori_loop(0, rows_c, wave_slot, 0)
        acc[:, GRID * rows :, :] = acc[:, : BLOCK * rows, :]
        slot_lane = lax.broadcasted_iota(jnp.int32, (8, hyd.shape[1]), 1)

        def add_out(s, values):
            padded = jnp.concatenate([values, jnp.zeros((5, nodes), F32)], axis=0)
            out_ref[s, 0:3, :] = out_ref[s, 0:3, :] + values
            mean = jnp.sum(padded, axis=1, keepdims=True) * (1.0 / nodes)
            hyd[...] = hyd[...] + jnp.where(slot_lane == s, mean, 0.0)

        lanes = lax.broadcasted_iota(jnp.int32, (BLOCK * rows, HALF), 1)

        def sample(i, c):
            group = members(i)
            ready = [prepare(s, u, True) for u, (s, _) in enumerate(group)]
            results = []
            for u in range(UNROLL):
                where, tile, local_y, wx, zed, _ = ready[u]
                block = acc[tile, where, :]
                chosen = ((lanes - local_y) & (HALF - 1)) < HALF // 2
                high, low = split2(jnp.where(chosen, block, turned(block)))
                seen = dot(jnp.concatenate([high, low], axis=1), wy[u])
                total = seen[:rows] * wx[0:1, :]
                for a in range(1, BLOCK):
                    total = total + seen[a * rows : (a + 1) * rows] * wx[a : a + 1, :]
                total = total * zed
                results.append(
                    jnp.concatenate(
                        [
                            jnp.sum(total[d * rows_c : (d + 1) * rows_c], axis=0, keepdims=True)
                            for d in range(3)
                        ],
                        axis=0,
                    )
                )
            for u, (s, there) in enumerate(group):
                add_out(s, results[u] * there)
                forget(u, ready[u][5])
            return c

        lax.fori_loop(0, trips, sample, 0)

        chunk = 8

        def near_task(i, c):
            task = device + i * devices
            s = listed[task // 3]
            which = task % 3
            source = jnp.where(
                which == 0, s, misc[s * 16 + 6 + jnp.maximum(which, 1)].astype(jnp.int32)
            )
            force = jnp.concatenate(
                [g_ref[source, 0:3, :], jnp.zeros((5, nodes), F32)], axis=0
            )
            ft[...] = force.T
            shifted = []
            for d in range(3):
                gap = jnp.full((1, nodes), misc[s * 16 + d] - misc[source * 16 + d], F32)
                gap = gap - GRID * jnp.floor(gap / GRID + 0.5)
                gap = jnp.where(which == 0, 0.0, gap)
                shifted.append(gap + off_ref[d : d + 1, :])

            def part(j, sums):
                at = pl.ds(pl.multiple_of(j * chunk, chunk), chunk)
                own = offt_ref[at, :]
                push = ft[at, :]
                sep = [shifted[d] - own[:, d : d + 1] for d in range(3)]
                pushes = [push[:, d : d + 1] for d in range(3)]
                square = sep[0] * sep[0] + sep[1] * sep[1] + sep[2] * sep[2]
                root = lax.rsqrt(square + soften)
                weight = jnp.exp(-square * screen) * (root * root * root)
                projected = sep[0] * pushes[0] + sep[1] * pushes[1] + sep[2] * pushes[2]
                diagonal = (square + 2.0 * soften) * weight
                leaning = projected * weight
                new = []
                for d in range(3):
                    value = diagonal * pushes[d] + sep[d] * leaning
                    new.append(sums[d] + value)
                return tuple(new)

            zero = jnp.zeros((8, nodes), F32)
            sums = lax.fori_loop(0, nodes // chunk, part, (zero, zero, zero), unroll=8)
            values = jnp.concatenate(
                [jnp.sum(v, axis=0, keepdims=True) for v in sums], axis=0
            )
            add_out(s, near_scale * values)
            return c

        tasks = (3 * count - device + (devices - 1)) // devices
        lax.fori_loop(0, tasks, near_task, 0)
        per_device = slots // devices

        def publish(holder, c):
            for d in range(3):
                for h in range(hydro_rows):
                    low = h * nodes
                    high = min(low + nodes, hyd.shape[1])
                    out_ref[holder * per_device + d, 3 + h : 4 + h, : high - low] = hyd[
                        d : d + 1, low:high
                    ]
            return c

        lax.fori_loop(0, devices, publish, 0)

    return kernel


def contact_kernel(slots, devices, hydro_rows):
    per_device = slots // devices

    def kernel(recv_ref, contacts_ref, velocity_ref, force_ref, drift_ref, incidence, loads):
        contacts = contacts_ref.shape[1]

        def gather(holder, total):
            return total + recv_ref[pl.ds(holder * per_device, per_device)]

        summed = lax.fori_loop(
            1, devices, gather, recv_ref[pl.ds(0, per_device)]
        )
        velocity_ref[...] = summed[:, :3, :]
        hydro = jnp.concatenate(
            [
                jnp.concatenate(
                    [summed[d, 3 + h : 4 + h, :] for h in range(hydro_rows)], axis=1
                )[:, :slots]
                for d in range(3)
            ]
            + [jnp.zeros((5, slots), F32)],
            axis=0,
        )
        first = contacts_ref[0:1, :].astype(jnp.int32)
        second = contacts_ref[1:2, :].astype(jnp.int32)
        gap = contacts_ref[2:3, :]
        polar = contacts_ref[3:4, :]
        azimuth = contacts_ref[4:5, :]
        normal = jnp.concatenate(
            [
                jnp.sin(polar) * jnp.cos(azimuth),
                jnp.sin(polar) * jnp.sin(azimuth),
                jnp.cos(polar),
                jnp.zeros((5, contacts), F32),
            ],
            axis=0,
        )

        def build(i, c):
            row = pl.multiple_of(i * 16, 16)
            ids = lax.broadcasted_iota(jnp.int32, (16, contacts), 0) + row
            value = jnp.where(first == ids, 1.0, 0.0) - jnp.where(second == ids, 1.0, 0.0)
            incidence[pl.ds(row, 16), :] = value.astype(BF16)
            return c

        lax.fori_loop(0, slots // 16, build, 0)

        def totals(magnitude):
            spread = dot(split_rows(magnitude * normal), incidence[...], NT)
            return spread[0:8] + (spread[8:16] + spread[16:24])

        def sweep(i, magnitude):
            velocity = hydro + mobility * totals(magnitude)
            seen = dot(split_rows(velocity), incidence[...])
            relative = jnp.sum(
                normal * (seen[0:8] + (seen[8:16] + seen[16:24])), axis=0, keepdims=True
            )
            return jnp.maximum(
                magnitude
                - relaxation * (gap + time_step * relative) / (2.0 * time_step * mobility),
                0.0,
            )

        magnitude = lax.fori_loop(0, SWEEPS, sweep, jnp.zeros((1, contacts), F32))
        force_ref[...] = magnitude
        drift_ref[...] = time_step * (hydro + mobility * totals(magnitude))

    return kernel


def local(
    tractions,
    centers,
    node_offsets,
    occupied,
    anchors,
    near_list,
    contact_pairs,
    contact_gap,
    contact_angles,
):
    side = tractions.shape[0]
    per_device = side * side
    nodes = tractions.shape[3]
    near = near_list.shape[2]
    narrow_count = lax.axis_size("narrow")
    devices = lax.axis_size("wide") * narrow_count
    rank = lax.axis_index("wide") * narrow_count + lax.axis_index("narrow")
    slots = devices * per_device
    contacts_own = contact_gap.shape[0]
    contacts = contacts_own * devices
    pairs = max(MIN_PAIRS, HALF // devices)
    z_groups = HALF // pairs
    x_groups = max(1, devices // z_groups)
    half_x = HALF // x_groups
    z_group = rank % z_groups
    x_group = rank // z_groups
    rows = 6 * pairs
    hydro_rows = -(-slots // nodes)

    fields = jnp.concatenate(
        [
            contact_pairs.astype(F32),
            contact_gap[None],
            contact_angles,
        ],
        axis=0,
    ).reshape(per_device, -1)
    misc = jnp.concatenate(
        [
            centers.reshape(per_device, 3),
            anchors.reshape(per_device, 3).astype(F32),
            occupied.reshape(per_device, 1).astype(F32),
            near_list.reshape(per_device, near).astype(F32),
            jnp.zeros((per_device, 16 - 7 - near), F32),
            fields,
        ],
        axis=1,
    )
    misc = jnp.pad(misc, ((0, 0), (0, nodes - misc.shape[1])))
    own = jnp.concatenate([tractions.reshape(per_device, 3, nodes), misc[:, None]], axis=1)
    packed = jnp.broadcast_to(own[None], (devices,) + own.shape).reshape(slots, 4, nodes)
    gathered = lax.all_to_all(packed, AXES, split_axis=0, concat_axis=0, tiled=True)
    scalars = gathered[:, 3, :16].reshape(slots * 16)

    xy, zz = z_tables()
    tables = np.concatenate(
        [
            xy.reshape(z_groups, 2 * pairs, GRID + BLOCK),
            zz.reshape(z_groups, 2 * pairs, GRID + BLOCK),
        ],
        axis=1,
    ).transpose(0, 2, 1)
    table = lax.dynamic_index_in_dim(jnp.asarray(tables, F32), z_group, 0, keepdims=False)
    table = jnp.broadcast_to(table[:, :, None], table.shape + (128,))
    basis = real_basis()
    turned = np.ascontiguousarray(basis.T)
    ry = [jnp.asarray(v) for v in split_np(basis)]
    ryt = [jnp.asarray(v) for v in split_np(turned)]
    if x_groups == 1:
        rx, rxt = ry, ryt
    else:
        rxt = [
            lax.dynamic_index_in_dim(
                v.reshape(2, x_groups, half_x, GRID), x_group, 1, keepdims=False
            ).reshape(2 * half_x, GRID)
            for v in ryt
        ]
        rx = [v.T for v in rxt]

    vmem = pl.BlockSpec(memory_space=pltpu.VMEM)
    smem = pl.BlockSpec(memory_space=pltpu.SMEM)
    ranks = jnp.stack([z_group, x_group, rank]).astype(jnp.int32)
    partial = pl.pallas_call(
        far_kernel(pairs, slots, devices, hydro_rows),
        out_shape=jax.ShapeDtypeStruct((slots, 3 + hydro_rows, nodes), F32),
        in_specs=[smem, smem] + [vmem] * 12,
        out_specs=vmem,
        scratch_shapes=[
            pltpu.SMEM((slots,), jnp.int32),
            pltpu.VMEM((4, (GRID + BLOCK) * rows, HALF), F32),
            pltpu.VMEM((UNROLL, GRID, nodes), BF16),
            pltpu.VMEM((3, 2 * half_x, GRID), F32),
            pltpu.VMEM((8, slots), F32),
            pltpu.VMEM((nodes, 8), F32),
        ],
        compiler_params=pltpu.CompilerParams(vmem_limit_bytes=60 * 1024 * 1024),
        name="far_near",
    )(
        scalars,
        ranks,
        gathered,
        node_offsets,
        node_offsets.T,
        table,
        *ry,
        *ryt,
        *rx,
        *rxt,
    )
    received = lax.all_to_all(partial, AXES, split_axis=0, concat_axis=0, tiled=True)
    listed = gathered[:, 3, 16 : 16 + fields.shape[1]].reshape(devices, 5, contacts_own)
    listed = listed.transpose(1, 0, 2).reshape(5, contacts)
    velocity, magnitude, drift = pl.pallas_call(
        contact_kernel(slots, devices, hydro_rows),
        out_shape=(
            jax.ShapeDtypeStruct((per_device, 3, nodes), F32),
            jax.ShapeDtypeStruct((1, contacts), F32),
            jax.ShapeDtypeStruct((8, slots), F32),
        ),
        in_specs=[vmem, vmem],
        out_specs=(vmem, vmem, vmem),
        scratch_shapes=[
            pltpu.VMEM((slots, contacts), BF16),
            pltpu.VMEM((8, 128), F32),
        ],
        compiler_params=pltpu.CompilerParams(vmem_limit_bytes=60 * 1024 * 1024),
        name="contacts",
    )(received, listed)
    own_force = lax.dynamic_slice(magnitude, (0, rank * contacts_own), (1, contacts_own))[0]
    own_drift = lax.dynamic_slice(drift, (0, rank * per_device), (3, per_device)).T
    moved = centers + own_drift.reshape(side, side, 3)
    return (velocity.reshape(side, side, 3, nodes), own_force, moved)


def solution(mesh):
    placed = (
        P("wide", "narrow", None, None),
        P("wide", "narrow", None),
        P(),
        P("wide", "narrow"),
        P("wide", "narrow", None),
        P("wide", "narrow", None),
        P(None, ("wide", "narrow")),
        P(("wide", "narrow")),
        P(None, ("wide", "narrow")),
    )
    return jax.shard_map(
        local,
        mesh=mesh,
        in_specs=placed,
        out_specs=(
            P("wide", "narrow", None, None),
            P(("wide", "narrow")),
            P("wide", "narrow", None),
        ),
        check_vma=False,
    )
```

```python
import jax
import jax.numpy as jnp
import numpy as np
from jax import lax
from jax.experimental import pallas as pl
from jax.experimental.pallas import tpu as pltpu
from jax.sharding import PartitionSpec as P

GRID = 256
HALF = GRID // 2
BLOCK = 16
SWEEPS = 6
MIN_PAIRS = 4
AXES = ("wide", "narrow")
UNROLL = 4

soften = 1.0
screen = 0.0625
near_scale = 0.05
spread_norm = 0.17958712212516656
mobility = 0.2
time_step = 0.5
relaxation = 0.35
ewald_split = 0.5

F32 = jnp.float32
BF16 = jnp.bfloat16
NT = (((1,), (1,)), ((), ()))
NN = (((1,), (0,)), ((), ()))


def real_basis():
    cells = np.arange(GRID)
    angle = 2.0 * np.pi * (np.outer(cells, np.arange(HALF)) % GRID) / GRID
    sine = np.sin(angle)
    sine[:, 0] = np.cos(np.pi * cells)
    return np.concatenate([np.cos(angle), sine], axis=1)


def z_tables():
    pairs = np.arange(HALF)
    cells = np.arange(GRID + BLOCK)
    angle = 2.0 * np.pi * (np.outer(pairs, cells) % GRID) / GRID
    cosine, sine = np.cos(angle), np.sin(angle)
    nyquist = np.cos(np.pi * cells)
    xy = np.stack([cosine, sine], axis=1)
    zz = np.stack([-sine, cosine], axis=1)
    xy[0, 0] = zz[0, 0] = 1.0
    xy[0, 1] = zz[0, 1] = nyquist
    return xy, zz


def split_np(table):
    high = np.asarray(table, dtype=BF16)
    low = np.asarray(table - high.astype(np.float64), dtype=BF16)
    return high, low


def split2(value):
    high = value.astype(BF16)
    return high, (value - high.astype(F32)).astype(BF16)


def dot(a, b, dims=NN):
    return lax.dot_general(a, b, dims, preferred_element_type=F32)


def dot3(a, b):
    return dot(a[0], b[0]) + (dot(a[1], b[0]) + dot(a[0], b[1]))


def split_rows(value):
    high = value.astype(BF16).astype(F32)
    rest = value - high
    middle = rest.astype(BF16).astype(F32)
    return jnp.concatenate([high, middle, rest - middle], axis=0).astype(BF16)


def near_tile(shifted, offt_ref, push_ref, nodes):
    def part(j, sums):
        at = pl.ds(pl.multiple_of(j * 8, 8), 8)
        own = offt_ref[at, :]
        push = push_ref[at, :]
        sep = [shifted[d] - own[:, d : d + 1] for d in range(3)]
        pushes = [push[:, d : d + 1] for d in range(3)]
        square = sep[0] * sep[0] + sep[1] * sep[1] + sep[2] * sep[2]
        root = lax.rsqrt(square + soften)
        weight = jnp.exp(-square * screen) * (root * root * root)
        projected = sep[0] * pushes[0] + sep[1] * pushes[1] + sep[2] * pushes[2]
        diagonal = (square + 2.0 * soften) * weight
        leaning = projected * weight
        return tuple(sums[d] + (diagonal * pushes[d] + sep[d] * leaning) for d in range(3))

    zero = jnp.zeros((8, nodes), F32)
    sums = lax.fori_loop(0, nodes // 8, part, (zero, zero, zero), unroll=8)
    return near_scale * jnp.concatenate(
        [jnp.sum(v, axis=0, keepdims=True) for v in sums], axis=0
    )


def pack_kernel(
    centers, anchors, occupied, near_list, tractions, pairs, gap, angles, out_ref, fields
):
    side = tractions.shape[0]
    nodes = tractions.shape[3]
    per_device = side * side
    own_contacts = pairs.shape[1]
    fields[...] = jnp.zeros(fields.shape, F32)
    fields[0:2, :own_contacts] = pairs[...].astype(F32)
    fields[2:3, :own_contacts] = gap[...]
    fields[3:5, :own_contacts] = angles[...]
    lane = lax.broadcasted_iota(jnp.int32, (1, 128), 1)
    for k in range(per_device):
        a, b = divmod(k, side)
        values = [centers[a, b, d] for d in range(3)]
        values += [anchors[a, b, d].astype(F32) for d in range(3)]
        values.append(occupied[a, b].astype(F32))
        values += [near_list[a, b, j].astype(F32) for j in range(near_list.shape[2])]
        row = jnp.zeros((1, 128), F32)
        for j, value in enumerate(values):
            row = jnp.where(lane == j, value, row)
        field = fields[k : k + 1, :]
        if k == 0:
            field = field + pltpu.roll(fields[4:5, :], 64, 1)
        block = jnp.concatenate(
            [tractions[a, :, b], jnp.concatenate([row, field], axis=1)], axis=0
        )

        def send(holder, c):
            out_ref[holder * per_device + k] = block
            return c

        lax.fori_loop(0, out_ref.shape[0] // per_device, send, 0, unroll=8)


def self_kernel(occupied, tractions, off_ref, offt_ref, out_ref, push):
    side = tractions.shape[0]
    nodes = tractions.shape[3]
    out_ref[...] = jnp.zeros(out_ref.shape, F32)

    for k in range(side * side):
        a, b = divmod(k, side)

        @pl.when(occupied[a, b] > 0)
        def _(a=a, b=b, k=k):
            push[...] = jnp.concatenate(
                [tractions[a, :, b], jnp.zeros((5, nodes), F32)], axis=0
            ).T
            shifted = [off_ref[d : d + 1, :] for d in range(3)]
            out_ref[k] = near_tile(shifted, offt_ref, push, nodes)


def far_kernel(pairs, slots, devices, hydro_rows):
    rows_c = 2 * pairs
    rows = 3 * rows_c

    def kernel(
        misc,
        ranks,
        g_ref,
        off_ref,
        offt_ref,
        self_ref,
        tab_in,
        ryh,
        ryl,
        ryth,
        rytl,
        rxh,
        rxl,
        rxth,
        rxtl,
        out_ref,
        listed,
        acc,
        wy,
        sbuf,
        hyd,
        ft,
        tab_ref,
    ):
        z_group, x_group, device = ranks[0], ranks[1], ranks[2]
        nodes = off_ref.shape[1]
        half_x = rxh.shape[1] // 2

        def clear(i, c):
            at = pl.ds(pl.multiple_of(i * 192, 64), 192)
            for tile in range(4):
                acc[tile, at, :] = jnp.zeros((192, HALF), F32)
            return c

        lax.fori_loop(0, acc.shape[1] // 192, clear, 0)
        for z in range(GRID + BLOCK):
            tab_ref[z] = jnp.broadcast_to(tab_in[:, z : z + 1], tab_ref.shape[1:])
        wy[...] = jnp.zeros(wy.shape, BF16)
        hyd[...] = jnp.zeros(hyd.shape, F32)

        def clear_out(i, c):
            out_ref[i] = jnp.zeros(out_ref.shape[1:], F32)
            return c

        lax.fori_loop(0, slots, clear_out, 0)

        def scan(s, n):
            held = misc[s, 6] > 0.5

            @pl.when(held)
            def _():
                listed[n] = s

            return n + held.astype(jnp.int32)

        count = lax.fori_loop(0, slots, scan, jnp.int32(0))
        steps = lax.broadcasted_iota(jnp.int32, (BLOCK, nodes), 0)

        def prepare(s, buffer, doubled):
            anchor = [misc[s, 3 + d].astype(jnp.int32) for d in range(3)]
            pos = [off_ref[d : d + 1, :] + misc[s, d] for d in range(3)]

            def weights(d, shift):
                away = pos[d] - (anchor[d] + steps + shift).astype(F32)
                return jnp.exp(-away * away)

            wx = weights(0, 0)
            wz = weights(2, 0)
            local_y = anchor[1] % HALF
            late = (local_y > HALF - BLOCK).astype(jnp.int32)
            local_y = local_y - late * (HALF // 2)
            tile = 2 * (anchor[1] // HALF) + late
            first = local_y // BLOCK
            inner = local_y % BLOCK
            places = []
            for i in range(2):
                t = steps + (i * BLOCK - inner)
                value = jnp.where((t >= 0) & (t < BLOCK), weights(1, i * BLOCK - inner), 0.0)
                high, low = split2(value)
                near_row = ((first + i) % 8) * BLOCK
                if doubled:
                    writes = (
                        (near_row, high),
                        (((first + i + 4) % 8) * BLOCK, low),
                        (near_row + HALF, high),
                    )
                else:
                    writes = ((near_row, high), (near_row + HALF, low))
                for row, part in writes:
                    row = pl.multiple_of(row, BLOCK)
                    wy[buffer, pl.ds(row, BLOCK), :] = part
                    places.append(row)
            table = jnp.zeros((2 * rows_c, nodes), F32)
            for t in range(BLOCK):
                phase = tab_ref[anchor[2] + t]
                phase = jnp.concatenate([phase] * (nodes // 128), axis=1)
                table = table + phase * wz[t : t + 1, :]
            zed = jnp.concatenate([table[:rows_c], table], axis=0)
            where = pl.ds(pl.multiple_of(anchor[0] * rows, rows), BLOCK * rows)
            return where, tile, local_y, wx, zed, places

        def forget(buffer, places):
            for row in places:
                wy[buffer, pl.ds(row, BLOCK), :] = jnp.zeros((BLOCK, nodes), BF16)

        def members(i):
            found = []
            for u in range(UNROLL):
                at = i * UNROLL + u
                there = (at < count).astype(F32)
                found.append((listed[jnp.minimum(at, count - 1)], there))
            return found

        trips = (count + (UNROLL - 1)) // UNROLL

        def spread(i, c):
            group = members(i)
            ready = [prepare(s, u, False) for u, (s, _) in enumerate(group)]
            patches = []
            for u, (s, there) in enumerate(group):
                _, _, _, wx, zed, _ = ready[u]
                force = jnp.concatenate(
                    [
                        jnp.broadcast_to(g_ref[s, d : d + 1, :] * there, (rows_c, nodes))
                        for d in range(3)
                    ],
                    axis=0,
                )
                loaded = force * zed
                left = jnp.concatenate([loaded * wx[a : a + 1, :] for a in range(BLOCK)], axis=0)
                high, low = split2(left)
                upper = dot(high, wy[u], NT)
                lower = dot(low, wy[u], NT)
                patches.append(upper[:, :HALF] + (upper[:, HALF:] + lower[:, :HALF]))
            for u, patch in enumerate(patches):
                where, tile, _, _, _, places = ready[u]
                acc[tile, where, :] = acc[tile, where, :] + patch
                forget(u, places)
            return c

        lax.fori_loop(0, trips, spread, 0)
        acc[:, : BLOCK * rows, :] = acc[:, : BLOCK * rows, :] + acc[:, GRID * rows :, :]
        low_half = lax.broadcasted_iota(jnp.int32, (GRID, HALF), 1) < HALF // 2

        def turned(value):
            return pltpu.roll(value, HALF // 2, 1)

        damping = (ewald_split * np.pi / GRID) ** 2
        constant = spread_norm**2 * GRID * GRID / (4.0 * np.pi**2) / GRID**3
        k_lane = lax.broadcasted_iota(jnp.int32, (8, HALF), 1).astype(F32)
        y_edge = jnp.where(k_lane == 0.0, float(HALF), 0.0)
        ky = ((k_lane, jnp.zeros_like(k_lane)), (k_lane, y_edge))
        y_factor = jnp.where(k_lane == 0.0, 1.0, 2.0)

        def wave_slot(r, c):
            pair = z_group * pairs + r // 2
            is_first = pair == 0
            kz = jnp.where(is_first, 0, pair).astype(F32)
            nz = jnp.where(is_first & (r % 2 == 1), HALF, 0).astype(F32)
            kz2 = kz * kz + nz * nz
            z_factor = jnp.where(is_first, 1.0, 2.0) * constant
            lines = []
            for comp in range(3):
                line = pl.ds(comp * rows_c + r, GRID, stride=rows)
                odd0, odd1 = turned(acc[1, line, :]), turned(acc[3, line, :])
                data = jnp.concatenate(
                    [
                        acc[0, line, :] + jnp.where(low_half, odd1, odd0),
                        acc[2, line, :] + jnp.where(low_half, odd0, odd1),
                    ],
                    axis=1,
                )
                lines.append(data)
            for comp in range(3):
                mid = dot3(split2(lines[comp]), (ryh[...], ryl[...]))
                sbuf[comp] = dot3((rxth[...], rxtl[...]), split2(mid))

            def filtered(i, c2):
                row = pl.multiple_of(i * 8, 8)
                k_row = (
                    lax.broadcasted_iota(jnp.int32, (8, HALF), 0) + (row + x_group * half_x)
                ).astype(F32)
                x_edge = jnp.where(k_row == 0.0, float(HALF), 0.0)
                kxn = (None, x_edge)
                scale = jnp.where(k_row == 0.0, 1.0, 2.0) * y_factor * z_factor
                spectrum = [
                    [
                        [
                            sbuf[comp, pl.ds(row + hx * half_x, 8), hy * HALF : (hy + 1) * HALF]
                            for hy in range(2)
                        ]
                        for hx in range(2)
                    ]
                    for comp in range(3)
                ]
                sx, sy, sz = spectrum
                total = [[None, None], [None, None]]
                for hx in range(2):
                    for hy in range(2):
                        jx = sx[0][hy] if hx else -sx[1][hy]
                        jy = sy[hx][0] if hy else -sy[hx][1]
                        total[hx][hy] = k_row * jx + k_lane * jy + kz * sz[hx][hy]
                for hx in range(2):
                    for hy in range(2):
                        square = k_row * k_row + k_lane * k_lane + kz2
                        edge = nz * sz[hx][hy]
                        if hx:
                            square = square + x_edge * x_edge
                            edge = edge + x_edge * sx[hx][hy]
                        if hy:
                            square = square + y_edge * y_edge
                            edge = edge + y_edge * sy[hx][hy]
                        inverse = 1.0 / jnp.maximum(square, 1.0)
                        factor = jnp.where(
                            square > 0.5, jnp.exp(-damping * square) * inverse, 0.0
                        ) * scale
                        tx = total[0][hy] if hx else -total[1][hy]
                        ty = total[hx][0] if hy else -total[hx][1]
                        along_x = k_row * tx
                        along_y = k_lane * ty
                        if hx:
                            along_x = along_x - x_edge * edge
                        if hy:
                            along_y = along_y - y_edge * edge
                        along_z = kz * total[hx][hy] + nz * edge
                        lanes = slice(hy * HALF, (hy + 1) * HALF)
                        at = pl.ds(row + hx * half_x, 8)
                        sbuf[0, at, lanes] = factor * (sx[hx][hy] + along_x * inverse)
                        sbuf[1, at, lanes] = factor * (sy[hx][hy] + along_y * inverse)
                        sbuf[2, at, lanes] = factor * (sz[hx][hy] - along_z * inverse)
                return c2

            lax.fori_loop(0, half_x // 8, filtered, 0, unroll=4)
            for comp in range(3):
                line = pl.ds(comp * rows_c + r, GRID, stride=rows)
                mid = dot3((rxh[...], rxl[...]), split2(sbuf[comp]))
                data = dot3(split2(mid), (ryth[...], rytl[...]))
                even0, even1 = data[:, :HALF], data[:, HALF:]
                odd0, odd1 = turned(even0), turned(even1)
                acc[0, line, :] = even0
                acc[1, line, :] = jnp.where(low_half, odd0, odd1)
                acc[2, line, :] = even1
                acc[3, line, :] = jnp.where(low_half, odd1, odd0)
            return c

        lax.fori_loop(0, rows_c, wave_slot, 0)
        acc[:, GRID * rows :, :] = acc[:, : BLOCK * rows, :]
        slot_lane = lax.broadcasted_iota(jnp.int32, (8, hyd.shape[1]), 1)

        def add_out(s, values):
            padded = jnp.concatenate([values, jnp.zeros((5, nodes), F32)], axis=0)
            out_ref[s, 0:3, :] = out_ref[s, 0:3, :] + values
            mean = jnp.sum(padded, axis=1, keepdims=True) * (1.0 / nodes)
            hyd[...] = hyd[...] + jnp.where(slot_lane == s, mean, 0.0)

        lanes = lax.broadcasted_iota(jnp.int32, (BLOCK * rows, HALF), 1)

        def sample(i, c):
            group = members(i)
            ready = [prepare(s, u, True) for u, (s, _) in enumerate(group)]
            results = []
            for u in range(UNROLL):
                where, tile, local_y, wx, zed, _ = ready[u]
                block = acc[tile, where, :]
                chosen = ((lanes - local_y) & (HALF - 1)) < HALF // 2
                high, low = split2(jnp.where(chosen, block, turned(block)))
                seen = dot(jnp.concatenate([high, low], axis=1), wy[u])
                total = seen[:rows] * wx[0:1, :]
                for a in range(1, BLOCK):
                    total = total + seen[a * rows : (a + 1) * rows] * wx[a : a + 1, :]
                total = total * zed
                results.append(
                    jnp.concatenate(
                        [
                            jnp.sum(total[d * rows_c : (d + 1) * rows_c], axis=0, keepdims=True)
                            for d in range(3)
                        ],
                        axis=0,
                    )
                )
            for u, (s, there) in enumerate(group):
                add_out(s, results[u] * there)
                forget(u, ready[u][5])
            return c

        lax.fori_loop(0, trips, sample, 0)

        per_device = slots // devices

        def near_task(i, c):
            task = device + i * devices
            s = listed[task // 2]
            source = misc[s, 7 + task % 2].astype(jnp.int32)
            ft[...] = jnp.concatenate([g_ref[source, 0:3, :], jnp.zeros((5, nodes), F32)], axis=0).T
            shifted = []
            for d in range(3):
                gap = jnp.full((1, nodes), misc[s, d] - misc[source, d], F32)
                gap = gap - GRID * jnp.floor(gap / GRID + 0.5)
                shifted.append(gap + off_ref[d : d + 1, :])
            add_out(s, near_tile(shifted, offt_ref, ft, nodes))
            return c

        tasks = (2 * count - device + (devices - 1)) // devices
        lax.fori_loop(0, tasks, near_task, 0)
        for k in range(per_device):
            add_out(device * per_device + k, self_ref[k])

        def publish(holder, c):
            for d in range(3):
                for h in range(hydro_rows):
                    low = h * nodes
                    high = min(low + nodes, hyd.shape[1])
                    out_ref[holder * per_device + d, 3 + h : 4 + h, : high - low] = hyd[
                        d : d + 1, low:high
                    ]
            return c

        lax.fori_loop(0, devices, publish, 0)

    return kernel


def prepare_kernel(slots, devices, own_contacts):
    per_device = slots // devices
    per_tile = 128 // own_contacts
    tiles = devices // per_tile

    def kernel(g_ref, incidence, rows_ref):
        contacts = incidence.shape[1]
        lane = lax.broadcasted_iota(jnp.int32, (tiles, 128), 1)

        def field(q):
            slot = q % per_device
            shift = 64 * (q // per_device)
            total = jnp.zeros((tiles, 128), F32)
            for j in range(per_tile):
                part = jnp.concatenate(
                    [
                        g_ref[(t * per_tile + j) * per_device + slot, 3:4, 128:256]
                        for t in range(tiles)
                    ],
                    axis=0,
                )
                turn = (j * own_contacts - shift) % 128
                if turn:
                    part = pltpu.roll(part, turn, 1)
                total = jnp.where(lane // own_contacts == j, part, total)
            return jnp.concatenate([total[t : t + 1] for t in range(tiles)], axis=1)

        first = field(0).astype(jnp.int32)
        second = field(1).astype(jnp.int32)
        polar = field(3)
        azimuth = field(4)
        rows_ref[...] = jnp.concatenate(
            [
                jnp.sin(polar) * jnp.cos(azimuth),
                jnp.sin(polar) * jnp.sin(azimuth),
                jnp.cos(polar),
                field(2),
                jnp.zeros((4, contacts), F32),
            ],
            axis=0,
        )

        def build(i, c):
            row = pl.multiple_of(i * 16, 16)
            ids = lax.broadcasted_iota(jnp.int32, (16, contacts), 0) + row
            value = jnp.where(first == ids, 1.0, 0.0) - jnp.where(second == ids, 1.0, 0.0)
            incidence[pl.ds(row, 16), :] = value.astype(BF16)
            return c

        lax.fori_loop(0, slots // 16, build, 0)

    return kernel


def contact_kernel(slots, devices, hydro_rows, own_contacts):
    per_device = slots // devices

    def kernel(
        ranks,
        recv_ref,
        incidence,
        rows_ref,
        centers,
        velocity_ref,
        force_ref,
        moved_ref,
        wide_force,
        wide_drift,
    ):
        contacts = rows_ref.shape[1]
        side = centers.shape[0]
        device = ranks[2]

        def gather(holder, total):
            return total + recv_ref[pl.ds(holder * per_device, per_device)]

        summed = lax.fori_loop(1, devices, gather, recv_ref[pl.ds(0, per_device)], unroll=8)
        for a in range(side):
            for b in range(side):
                velocity_ref[a, :, b] = summed[a * side + b, :3, :]
        hydro = jnp.concatenate(
            [
                jnp.concatenate(
                    [summed[d, 3 + h : 4 + h, :] for h in range(hydro_rows)], axis=1
                )[:, :slots]
                for d in range(3)
            ]
            + [jnp.zeros((5, slots), F32)],
            axis=0,
        )
        gap = rows_ref[3:4, :]
        kind = lax.broadcasted_iota(jnp.int32, (8, contacts), 0)
        normal = jnp.where(kind < 3, rows_ref[...], 0.0)

        def totals(magnitude):
            spread = dot(split_rows(magnitude * normal), incidence[...], NT)
            return spread[0:8] + (spread[8:16] + spread[16:24])

        def sweep(i, magnitude):
            velocity = hydro + mobility * totals(magnitude)
            seen = dot(split_rows(velocity), incidence[...])
            relative = jnp.sum(
                normal * (seen[0:8] + (seen[8:16] + seen[16:24])), axis=0, keepdims=True
            )
            return jnp.maximum(
                magnitude
                - relaxation * (gap + time_step * relative) / (2.0 * time_step * mobility),
                0.0,
            )

        magnitude = lax.fori_loop(0, SWEEPS, sweep, jnp.zeros((1, contacts), F32))
        drift = time_step * (hydro + mobility * totals(magnitude))
        wide_force[...] = jnp.broadcast_to(magnitude, wide_force.shape)
        wide_drift[...] = drift
        place = device * own_contacts
        at = pl.ds(pl.multiple_of(place // 128 * 128, 128), 128)
        turned = pltpu.roll(wide_force[:, at], (128 - place % 128) % 128, 1)
        force_ref[...] = turned[0:1, :own_contacts]
        place = device * per_device
        at = pl.ds(pl.multiple_of(place // 128 * 128, 128), 128)
        own = pltpu.roll(wide_drift[:, at], (128 - place % 128) % 128, 1).T
        for a in range(side):
            moved_ref[a] = centers[a] + own[a * side : (a + 1) * side, 0:3]

    return kernel


def vmem_of(held):
    return pltpu.CompilerParams(vmem_limit_bytes=min(60 << 20, 2 * held + (12 << 20)))


def local(
    tractions,
    centers,
    node_offsets,
    occupied,
    anchors,
    near_list,
    contact_pairs,
    contact_gap,
    contact_angles,
):
    side = tractions.shape[0]
    per_device = side * side
    nodes = tractions.shape[3]
    narrow_count = lax.axis_size("narrow")
    devices = lax.axis_size("wide") * narrow_count
    rank = lax.axis_index("wide") * narrow_count + lax.axis_index("narrow")
    slots = devices * per_device
    contacts_own = contact_gap.shape[0]
    contacts = contacts_own * devices
    pairs = max(MIN_PAIRS, HALF // devices)
    z_groups = HALF // pairs
    x_groups = max(1, devices // z_groups)
    half_x = HALF // x_groups
    z_group = rank % z_groups
    x_group = rank // z_groups
    rows = 6 * pairs
    hydro_rows = -(-slots // nodes)

    vmem = pl.BlockSpec(memory_space=pltpu.VMEM)
    smem = pl.BlockSpec(memory_space=pltpu.SMEM)
    by_row = tractions.transpose(0, 2, 1, 3)
    packed = pl.pallas_call(
        pack_kernel,
        out_shape=jax.ShapeDtypeStruct((slots, 4, nodes), F32),
        in_specs=[smem] * 4 + [vmem] * 4,
        out_specs=vmem,
        scratch_shapes=[pltpu.VMEM((8, 128), F32)],
        name="pack",
    )(
        centers,
        anchors,
        occupied,
        near_list,
        by_row,
        contact_pairs,
        contact_gap[None],
        contact_angles,
    )
    gathered = lax.all_to_all(packed, AXES, split_axis=0, concat_axis=0, tiled=True)
    offsets_t = node_offsets.T
    self_near = pl.pallas_call(
        self_kernel,
        out_shape=jax.ShapeDtypeStruct((per_device, 3, nodes), F32),
        in_specs=[smem] + [vmem] * 3,
        out_specs=vmem,
        scratch_shapes=[pltpu.VMEM((nodes, 8), F32)],
        name="near_self",
    )(occupied, by_row, node_offsets, offsets_t)
    scalars = gathered[:, 3, :16]

    xy, zz = z_tables()
    tables = np.concatenate(
        [
            xy.reshape(z_groups, 2 * pairs, GRID + BLOCK),
            zz.reshape(z_groups, 2 * pairs, GRID + BLOCK),
        ],
        axis=1,
    )
    table = lax.dynamic_index_in_dim(jnp.asarray(tables, F32), z_group, 0, keepdims=False)
    basis = real_basis()
    turned = np.ascontiguousarray(basis.T)
    ry = [jnp.asarray(v) for v in split_np(basis)]
    ryt = [jnp.asarray(v) for v in split_np(turned)]
    if x_groups == 1:
        rx, rxt = ry, ryt
    else:
        rxt = [
            lax.dynamic_index_in_dim(
                v.reshape(2, x_groups, half_x, GRID), x_group, 1, keepdims=False
            ).reshape(2 * half_x, GRID)
            for v in ryt
        ]
        rx = [v.T for v in rxt]

    ranks = jnp.stack([z_group, x_group, rank]).astype(jnp.int32)
    partial = pl.pallas_call(
        far_kernel(pairs, slots, devices, hydro_rows),
        out_shape=jax.ShapeDtypeStruct((slots, 3 + hydro_rows, nodes), F32),
        in_specs=[smem, smem] + [vmem] * 13,
        out_specs=vmem,
        scratch_shapes=[
            pltpu.SMEM((slots,), jnp.int32),
            pltpu.VMEM((4, (GRID + BLOCK) * rows, HALF), F32),
            pltpu.VMEM((UNROLL, GRID, nodes), BF16),
            pltpu.VMEM((3, 2 * half_x, GRID), F32),
            pltpu.VMEM((8, slots), F32),
            pltpu.VMEM((nodes, 8), F32),
            pltpu.VMEM((GRID + BLOCK, 4 * pairs, 128), F32),
        ],
        compiler_params=vmem_of(8 * slots * nodes * 4 + 4 * (GRID + BLOCK) * 6 * pairs * GRID * 4),
        name="far_near",
    )(
        scalars,
        ranks,
        gathered,
        node_offsets,
        offsets_t,
        self_near,
        table,
        *ry,
        *ryt,
        *rx,
        *rxt,
    )
    received = lax.all_to_all(partial, AXES, split_axis=0, concat_axis=0, tiled=True)
    incidence, contact_rows = pl.pallas_call(
        prepare_kernel(slots, devices, contacts_own),
        out_shape=(
            jax.ShapeDtypeStruct((slots, contacts), BF16),
            jax.ShapeDtypeStruct((8, contacts), F32),
        ),
        in_specs=[vmem],
        out_specs=(vmem, vmem),
        compiler_params=vmem_of(4 * slots * nodes * 4 + slots * contacts * 2),
        name="contact_rows",
    )(gathered)
    velocity, force, moved = pl.pallas_call(
        contact_kernel(slots, devices, hydro_rows, contacts_own),
        out_shape=(
            jax.ShapeDtypeStruct((side, 3, side, nodes), F32),
            jax.ShapeDtypeStruct((1, contacts_own), F32),
            jax.ShapeDtypeStruct((side, side, 3), F32),
        ),
        in_specs=[smem, vmem, vmem, vmem, vmem],
        out_specs=(vmem, vmem, vmem),
        scratch_shapes=[
            pltpu.VMEM((8, contacts), F32),
            pltpu.VMEM((8, slots), F32),
        ],
        compiler_params=vmem_of((3 + hydro_rows) * slots * nodes * 4 + slots * contacts * 2),
        name="contacts",
    )(ranks, received, incidence, contact_rows, centers)
    return (velocity.transpose(0, 2, 1, 3), force[0], moved)


def solution(mesh):
    placed = (
        P("wide", "narrow", None, None),
        P("wide", "narrow", None),
        P(),
        P("wide", "narrow"),
        P("wide", "narrow", None),
        P("wide", "narrow", None),
        P(None, ("wide", "narrow")),
        P(("wide", "narrow")),
        P(None, ("wide", "narrow")),
    )
    return jax.shard_map(
        local,
        mesh=mesh,
        in_specs=placed,
        out_specs=(
            P("wide", "narrow", None, None),
            P(("wide", "narrow")),
            P("wide", "narrow", None),
        ),
        check_vma=False,
    )
```

```python
import jax
import jax.numpy as jnp
import numpy as np
from jax import lax
from jax.experimental import pallas as pl
from jax.experimental.pallas import tpu as pltpu
from jax.sharding import PartitionSpec as P

GRID = 256
HALF = GRID // 2
BLOCK = 16
SWEEPS = 6
MIN_PAIRS = 4
AXES = ("wide", "narrow")
KEEP_BYTES = 16 << 20
UNROLL = 6

soften = 1.0
screen = 0.0625
near_scale = 0.05
spread_norm = 0.17958712212516656
mobility = 0.2
time_step = 0.5
relaxation = 0.35
ewald_split = 0.5

F32 = jnp.float32
BF16 = jnp.bfloat16
NT = (((1,), (1,)), ((), ()))
NN = (((1,), (0,)), ((), ()))


def real_basis():
    cells = np.arange(GRID)
    angle = 2.0 * np.pi * (np.outer(cells, np.arange(HALF)) % GRID) / GRID
    sine = np.sin(angle)
    sine[:, 0] = np.cos(np.pi * cells)
    return np.concatenate([np.cos(angle), sine], axis=1)


def z_tables():
    pairs = np.arange(HALF)
    cells = np.arange(GRID + BLOCK)
    angle = 2.0 * np.pi * (np.outer(pairs, cells) % GRID) / GRID
    cosine, sine = np.cos(angle), np.sin(angle)
    nyquist = np.cos(np.pi * cells)
    xy = np.stack([cosine, sine], axis=1)
    zz = np.stack([-sine, cosine], axis=1)
    xy[0, 0] = zz[0, 0] = 1.0
    xy[0, 1] = zz[0, 1] = nyquist
    return xy, zz


def split_np(table):
    high = np.asarray(table, dtype=BF16)
    low = np.asarray(table - high.astype(np.float64), dtype=BF16)
    return high, low


def split2(value):
    high = value.astype(BF16)
    return high, (value - high.astype(F32)).astype(BF16)


def dot(a, b, dims=NN):
    return lax.dot_general(a, b, dims, preferred_element_type=F32)


def dot3(a, b):
    count = a[0].shape[0]
    both = dot(jnp.concatenate([a[0], a[1]], axis=0), b[0])
    return both[:count] + (both[count:] + dot(a[0], b[1]))


def split_rows(value):
    high = value.astype(BF16).astype(F32)
    rest = value - high
    middle = rest.astype(BF16).astype(F32)
    return jnp.concatenate([high, middle, rest - middle], axis=0).astype(BF16)


def near_tile(shifted, offt_ref, push_ref, nodes):
    def part(j, sums):
        at = pl.ds(pl.multiple_of(j * 8, 8), 8)
        own = offt_ref[at, :]
        push = push_ref[at, :]
        sep = [shifted[d] - own[:, d : d + 1] for d in range(3)]
        pushes = [push[:, d : d + 1] for d in range(3)]
        square = sep[0] * sep[0] + sep[1] * sep[1] + sep[2] * sep[2]
        root = lax.rsqrt(square + soften)
        weight = jnp.exp(-square * screen) * (root * root * root)
        projected = sep[0] * pushes[0] + sep[1] * pushes[1] + sep[2] * pushes[2]
        diagonal = (square + 2.0 * soften) * weight
        leaning = projected * weight
        return tuple(sums[d] + (diagonal * pushes[d] + sep[d] * leaning) for d in range(3))

    zero = jnp.zeros((8, nodes), F32)
    sums = lax.fori_loop(0, nodes // 8, part, (zero, zero, zero), unroll=True)
    return near_scale * jnp.concatenate(
        [jnp.sum(v, axis=0, keepdims=True) for v in sums], axis=0
    )


def pack_kernel(
    centers, anchors, occupied, near_list, tractions, pairs, gap, angles, out_ref, fields
):
    side = tractions.shape[0]
    nodes = tractions.shape[3]
    per_device = side * side
    own_contacts = pairs.shape[1]
    fields[...] = jnp.zeros(fields.shape, F32)
    fields[0:2, :own_contacts] = pairs[...].astype(F32)
    fields[2:3, :own_contacts] = gap[...]
    fields[3:5, :own_contacts] = angles[...]
    lane = lax.broadcasted_iota(jnp.int32, (1, 128), 1)
    for k in range(per_device):
        a, b = divmod(k, side)
        values = [centers[a, b, d] for d in range(3)]
        values += [anchors[a, b, d].astype(F32) for d in range(3)]
        values.append(occupied[a, b].astype(F32))
        values += [near_list[a, b, j].astype(F32) for j in range(near_list.shape[2])]
        row = jnp.zeros((1, 128), F32)
        for j, value in enumerate(values):
            row = jnp.where(lane == j, value, row)
        field = fields[k : k + 1, :]
        if k == 0:
            field = field + pltpu.roll(fields[4:5, :], 64, 1)
        block = jnp.concatenate(
            [tractions[a, :, b], jnp.concatenate([row, field], axis=1)], axis=0
        )

        def send(holder, c):
            out_ref[holder * per_device + k] = block
            return c

        lax.fori_loop(0, out_ref.shape[0] // per_device, send, 0, unroll=8)


def self_kernel(occupied, tractions, off_ref, offt_ref, out_ref, push):
    side = tractions.shape[0]
    nodes = tractions.shape[3]
    out_ref[...] = jnp.zeros(out_ref.shape, F32)

    for k in range(side * side):
        a, b = divmod(k, side)

        @pl.when(occupied[a, b] > 0)
        def _(a=a, b=b, k=k):
            push[...] = jnp.concatenate(
                [tractions[a, :, b], jnp.zeros((5, nodes), F32)], axis=0
            ).T
            shifted = [off_ref[d : d + 1, :] for d in range(3)]
            out_ref[k] = near_tile(shifted, offt_ref, push, nodes)


def far_kernel(pairs, slots, devices, hydro_rows, keep):
    rows_c = 2 * pairs
    rows = 3 * rows_c

    def kernel(
        misc,
        ranks,
        g_ref,
        off_ref,
        offt_ref,
        self_ref,
        tab_in,
        ryh,
        ryl,
        ryth,
        rytl,
        rxh,
        rxl,
        rxth,
        rxtl,
        out_ref,
        listed,
        acc,
        wy,
        sbuf,
        hyd,
        ft,
        tab_ref,
        kept_wx,
        kept_table,
        kept_wy,
    ):
        z_group, x_group, device = ranks[0], ranks[1], ranks[2]
        nodes = off_ref.shape[1]
        half_x = rxh.shape[1] // 2

        out_ref[...] = jnp.zeros(out_ref.shape, F32)
        strip = acc.shape[1] // BLOCK
        scanned = slots // BLOCK

        def start(i, n):
            at = pl.ds(pl.multiple_of(i * strip, 8), strip)
            for tile in range(4):
                acc[tile, at, :] = jnp.zeros((strip, HALF), F32)
            for j in range(scanned):
                s = i * scanned + j
                listed[n] = s
                n = n + (misc[s, 6] > 0.5).astype(jnp.int32)
            return n

        count = lax.fori_loop(0, BLOCK, start, jnp.int32(0))
        for z in range(GRID + BLOCK):
            tab_ref[z] = jnp.broadcast_to(tab_in[:, z : z + 1], tab_ref.shape[1:])
        wy[...] = jnp.zeros(wy.shape, BF16)
        hyd[...] = jnp.zeros(hyd.shape, F32)

        steps = lax.broadcasted_iota(jnp.int32, (BLOCK, nodes), 0)

        def positions(s):
            anchor = [misc[s, 3 + d].astype(jnp.int32) for d in range(3)]
            local_y = anchor[1] % HALF
            late = (local_y > HALF - BLOCK).astype(jnp.int32)
            local_y = local_y - late * (HALF // 2)
            tile = 2 * (anchor[1] // HALF) + late
            where = pl.ds(pl.multiple_of(anchor[0] * rows, rows), BLOCK * rows)
            return anchor, where, tile, local_y

        def factors(s, anchor, local_y):
            pos = [off_ref[d : d + 1, :] + misc[s, d] for d in range(3)]

            def weights(d, shift):
                away = pos[d] - (anchor[d] + steps + shift).astype(F32)
                return jnp.exp(-away * away)

            wx = weights(0, 0)
            wz = weights(2, 0)
            inner = local_y % BLOCK
            parts = []
            for i in range(2):
                t = steps + (i * BLOCK - inner)
                parts.append(
                    split2(
                        jnp.where((t >= 0) & (t < BLOCK), weights(1, i * BLOCK - inner), 0.0)
                    )
                )
            table = jnp.zeros((2 * rows_c, nodes), F32)
            for t in range(BLOCK):
                phase = tab_ref[anchor[2] + t]
                phase = jnp.concatenate([phase] * (nodes // 128), axis=1)
                table = table + phase * wz[t : t + 1, :]
            return wx, table, parts

        def lay(buffer, local_y, parts, doubled):
            first = local_y // BLOCK
            places = []
            for i, (high, low) in enumerate(parts):
                near_row = ((first + i) % 8) * BLOCK
                if doubled:
                    writes = (
                        (near_row, high),
                        (((first + i + 4) % 8) * BLOCK, low),
                        (near_row + HALF, high),
                    )
                else:
                    writes = ((near_row, high), (near_row + HALF, low))
                for row, part in writes:
                    row = pl.multiple_of(row, BLOCK)
                    wy[buffer, pl.ds(row, BLOCK), :] = part
                    places.append(row)
            return places

        def prepare(at, s, buffer, doubled):
            anchor, where, tile, local_y = positions(s)
            if doubled and keep:
                wx, table = kept_wx[at], kept_table[at]
                parts = [(kept_wy[at, i], kept_wy[at, 2 + i]) for i in range(2)]
            else:
                wx, table, parts = factors(s, anchor, local_y)
                if keep:
                    kept_wx[at] = wx
                    kept_table[at] = table
                    for i in range(2):
                        kept_wy[at, i] = parts[i][0]
                        kept_wy[at, 2 + i] = parts[i][1]
            places = lay(buffer, local_y, parts, doubled)
            zed = jnp.concatenate([table[:rows_c], table], axis=0)
            return where, tile, local_y, wx, zed, places

        def forget(buffer, places):
            for row in places:
                wy[buffer, pl.ds(row, BLOCK), :] = jnp.zeros((BLOCK, nodes), BF16)

        def members(i):
            found = []
            for u in range(UNROLL):
                at = i * UNROLL + u
                there = (at < count).astype(F32)
                found.append((listed[jnp.minimum(at, count - 1)], there))
            return found

        trips = (count + (UNROLL - 1)) // UNROLL

        def spread(i, c):
            group = members(i)
            ready = [prepare(i * UNROLL + u, s, u, False) for u, (s, _) in enumerate(group)]
            patches = []
            for u, (s, there) in enumerate(group):
                _, _, _, wx, zed, _ = ready[u]
                force = jnp.concatenate(
                    [
                        jnp.broadcast_to(g_ref[s, d : d + 1, :] * there, (rows_c, nodes))
                        for d in range(3)
                    ],
                    axis=0,
                )
                loaded = force * zed
                left = jnp.concatenate([loaded * wx[a : a + 1, :] for a in range(BLOCK)], axis=0)
                high, low = split2(left)
                upper = dot(high, wy[u], NT)
                lower = dot(low, wy[u], NT)
                patches.append(upper[:, :HALF] + (upper[:, HALF:] + lower[:, :HALF]))
            for u, patch in enumerate(patches):
                where, tile, _, _, _, places = ready[u]
                acc[tile, where, :] = acc[tile, where, :] + patch
                forget(u, places)
            return c

        lax.fori_loop(0, trips, spread, 0)
        acc[:, : BLOCK * rows, :] = acc[:, : BLOCK * rows, :] + acc[:, GRID * rows :, :]
        low_half = lax.broadcasted_iota(jnp.int32, (GRID, HALF), 1) < HALF // 2

        def turned(value):
            return pltpu.roll(value, HALF // 2, 1)

        damping = (ewald_split * np.pi / GRID) ** 2
        constant = spread_norm**2 * GRID * GRID / (4.0 * np.pi**2) / GRID**3
        k_lane = lax.broadcasted_iota(jnp.int32, (8, HALF), 1).astype(F32)
        y_edge = jnp.where(k_lane == 0.0, float(HALF), 0.0)
        ky = ((k_lane, jnp.zeros_like(k_lane)), (k_lane, y_edge))
        y_factor = jnp.where(k_lane == 0.0, 1.0, 2.0)

        def wave_slot(r, c):
            pair = z_group * pairs + r // 2
            is_first = pair == 0
            kz = jnp.where(is_first, 0, pair).astype(F32)
            nz = jnp.where(is_first & (r % 2 == 1), HALF, 0).astype(F32)
            kz2 = kz * kz + nz * nz
            z_factor = jnp.where(is_first, 1.0, 2.0) * constant
            lines = []
            for comp in range(3):
                line = pl.ds(comp * rows_c + r, GRID, stride=rows)
                odd0, odd1 = turned(acc[1, line, :]), turned(acc[3, line, :])
                data = jnp.concatenate(
                    [
                        acc[0, line, :] + jnp.where(low_half, odd1, odd0),
                        acc[2, line, :] + jnp.where(low_half, odd0, odd1),
                    ],
                    axis=1,
                )
                lines.append(data)
            for comp in range(3):
                mid = dot3(split2(lines[comp]), (ryh[...], ryl[...]))
                sbuf[comp] = dot3((rxth[...], rxtl[...]), split2(mid))

            def filtered(i, c2):
                row = pl.multiple_of(i * 8, 8)
                k_row = (
                    lax.broadcasted_iota(jnp.int32, (8, HALF), 0) + (row + x_group * half_x)
                ).astype(F32)
                x_edge = jnp.where(k_row == 0.0, float(HALF), 0.0)
                kxn = (None, x_edge)
                scale = jnp.where(k_row == 0.0, 1.0, 2.0) * y_factor * z_factor
                spectrum = [
                    [
                        [
                            sbuf[comp, pl.ds(row + hx * half_x, 8), hy * HALF : (hy + 1) * HALF]
                            for hy in range(2)
                        ]
                        for hx in range(2)
                    ]
                    for comp in range(3)
                ]
                sx, sy, sz = spectrum
                total = [[None, None], [None, None]]
                for hx in range(2):
                    for hy in range(2):
                        jx = sx[0][hy] if hx else -sx[1][hy]
                        jy = sy[hx][0] if hy else -sy[hx][1]
                        total[hx][hy] = k_row * jx + k_lane * jy + kz * sz[hx][hy]
                for hx in range(2):
                    for hy in range(2):
                        square = k_row * k_row + k_lane * k_lane + kz2
                        edge = nz * sz[hx][hy]
                        if hx:
                            square = square + x_edge * x_edge
                            edge = edge + x_edge * sx[hx][hy]
                        if hy:
                            square = square + y_edge * y_edge
                            edge = edge + y_edge * sy[hx][hy]
                        inverse = 1.0 / jnp.maximum(square, 1.0)
                        factor = jnp.where(
                            square > 0.5, jnp.exp(-damping * square) * inverse, 0.0
                        ) * scale
                        tx = total[0][hy] if hx else -total[1][hy]
                        ty = total[hx][0] if hy else -total[hx][1]
                        along_x = k_row * tx
                        along_y = k_lane * ty
                        if hx:
                            along_x = along_x - x_edge * edge
                        if hy:
                            along_y = along_y - y_edge * edge
                        along_z = kz * total[hx][hy] + nz * edge
                        lanes = slice(hy * HALF, (hy + 1) * HALF)
                        at = pl.ds(row + hx * half_x, 8)
                        sbuf[0, at, lanes] = factor * (sx[hx][hy] + along_x * inverse)
                        sbuf[1, at, lanes] = factor * (sy[hx][hy] + along_y * inverse)
                        sbuf[2, at, lanes] = factor * (sz[hx][hy] - along_z * inverse)
                return c2

            lax.fori_loop(0, half_x // 8, filtered, 0, unroll=True)
            for comp in range(3):
                line = pl.ds(comp * rows_c + r, GRID, stride=rows)
                mid = dot3((rxh[...], rxl[...]), split2(sbuf[comp]))
                data = dot3(split2(mid), (ryth[...], rytl[...]))
                even0, even1 = data[:, :HALF], data[:, HALF:]
                odd0, odd1 = turned(even0), turned(even1)
                acc[0, line, :] = even0
                acc[1, line, :] = jnp.where(low_half, odd0, odd1)
                acc[2, line, :] = even1
                acc[3, line, :] = jnp.where(low_half, odd1, odd0)
            return c

        lax.fori_loop(0, rows_c, wave_slot, 0, unroll=2)
        acc[:, GRID * rows :, :] = acc[:, : BLOCK * rows, :]
        slot_lane = lax.broadcasted_iota(jnp.int32, (8, hyd.shape[1]), 1)

        def add_out(s, values):
            padded = jnp.concatenate([values, jnp.zeros((5, nodes), F32)], axis=0)
            out_ref[s, 0:3, :] = out_ref[s, 0:3, :] + values
            mean = jnp.sum(padded, axis=1, keepdims=True) * (1.0 / nodes)
            hyd[...] = hyd[...] + jnp.where(slot_lane == s, mean, 0.0)

        lanes = lax.broadcasted_iota(jnp.int32, (BLOCK * rows, HALF), 1)

        def sample(i, c):
            group = members(i)
            ready = [prepare(i * UNROLL + u, s, u, True) for u, (s, _) in enumerate(group)]
            results = []
            for u in range(UNROLL):
                where, tile, local_y, wx, zed, _ = ready[u]
                block = acc[tile, where, :]
                chosen = ((lanes - local_y) & (HALF - 1)) < HALF // 2
                high, low = split2(jnp.where(chosen, block, turned(block)))
                seen = dot(jnp.concatenate([high, low], axis=1), wy[u])
                total = seen[:rows] * wx[0:1, :]
                for a in range(1, BLOCK):
                    total = total + seen[a * rows : (a + 1) * rows] * wx[a : a + 1, :]
                total = total * zed
                results.append(
                    jnp.concatenate(
                        [
                            jnp.sum(total[d * rows_c : (d + 1) * rows_c], axis=0, keepdims=True)
                            for d in range(3)
                        ],
                        axis=0,
                    )
                )
            for u, (s, there) in enumerate(group):
                add_out(s, results[u] * there)
                forget(u, ready[u][5])
            return c

        lax.fori_loop(0, trips, sample, 0)

        per_device = slots // devices

        def near_task(i, c):
            task = device + i * devices
            s = listed[task // 2]
            source = misc[s, 7 + task % 2].astype(jnp.int32)
            ft[...] = jnp.concatenate([g_ref[source, 0:3, :], jnp.zeros((5, nodes), F32)], axis=0).T
            shifted = []
            for d in range(3):
                gap = jnp.full((1, nodes), misc[s, d] - misc[source, d], F32)
                gap = gap - GRID * jnp.floor(gap / GRID + 0.5)
                shifted.append(gap + off_ref[d : d + 1, :])
            add_out(s, near_tile(shifted, offt_ref, ft, nodes))
            return c

        tasks = (2 * count - device + (devices - 1)) // devices
        lax.fori_loop(0, tasks, near_task, 0)
        for k in range(per_device):
            add_out(device * per_device + k, self_ref[k])

        def publish(holder, c):
            for d in range(3):
                for h in range(hydro_rows):
                    low = h * nodes
                    high = min(low + nodes, hyd.shape[1])
                    out_ref[holder * per_device + d, 3 + h : 4 + h, : high - low] = hyd[
                        d : d + 1, low:high
                    ]
            return c

        lax.fori_loop(0, devices, publish, 0)

    return kernel


def prepare_kernel(slots, devices, own_contacts):
    per_device = slots // devices
    per_tile = 128 // own_contacts
    tiles = devices // per_tile

    def kernel(g_ref, incidence, rows_ref):
        contacts = incidence.shape[1]
        lane = lax.broadcasted_iota(jnp.int32, (tiles, 128), 1)

        def field(q):
            slot = q % per_device
            shift = 64 * (q // per_device)
            total = jnp.zeros((tiles, 128), F32)
            for j in range(per_tile):
                part = jnp.concatenate(
                    [
                        g_ref[(t * per_tile + j) * per_device + slot, 3:4, 128:256]
                        for t in range(tiles)
                    ],
                    axis=0,
                )
                turn = (j * own_contacts - shift) % 128
                if turn:
                    part = pltpu.roll(part, turn, 1)
                total = jnp.where(lane // own_contacts == j, part, total)
            return jnp.concatenate([total[t : t + 1] for t in range(tiles)], axis=1)

        first = field(0).astype(jnp.int32)
        second = field(1).astype(jnp.int32)
        polar = field(3)
        azimuth = field(4)
        rows_ref[...] = jnp.concatenate(
            [
                jnp.sin(polar) * jnp.cos(azimuth),
                jnp.sin(polar) * jnp.sin(azimuth),
                jnp.cos(polar),
                field(2),
                jnp.zeros((4, contacts), F32),
            ],
            axis=0,
        )

        def build(i, c):
            row = pl.multiple_of(i * 16, 16)
            ids = lax.broadcasted_iota(jnp.int32, (16, contacts), 0) + row
            value = jnp.where(first == ids, 1.0, 0.0) - jnp.where(second == ids, 1.0, 0.0)
            incidence[pl.ds(row, 16), :] = value.astype(BF16)
            return c

        lax.fori_loop(0, slots // 16, build, 0)

    return kernel


def contact_kernel(slots, devices, hydro_rows, own_contacts):
    per_device = slots // devices

    def kernel(
        ranks,
        recv_ref,
        incidence,
        rows_ref,
        centers,
        velocity_ref,
        force_ref,
        moved_ref,
        wide_force,
        wide_drift,
    ):
        contacts = rows_ref.shape[1]
        side = centers.shape[0]
        device = ranks[2]

        def gather(holder, total):
            return total + recv_ref[pl.ds(holder * per_device, per_device)]

        summed = lax.fori_loop(1, devices, gather, recv_ref[pl.ds(0, per_device)], unroll=8)
        for a in range(side):
            for b in range(side):
                velocity_ref[a, :, b] = summed[a * side + b, :3, :]
        hydro = jnp.concatenate(
            [
                jnp.concatenate(
                    [summed[d, 3 + h : 4 + h, :] for h in range(hydro_rows)], axis=1
                )[:, :slots]
                for d in range(3)
            ]
            + [jnp.zeros((5, slots), F32)],
            axis=0,
        )
        gap = rows_ref[3:4, :]
        kind = lax.broadcasted_iota(jnp.int32, (8, contacts), 0)
        normal = jnp.where(kind < 3, rows_ref[...], 0.0)

        def totals(magnitude):
            spread = dot(split_rows(magnitude * normal), incidence[...], NT)
            return spread[0:8] + (spread[8:16] + spread[16:24])

        def sweep(i, magnitude):
            velocity = hydro + mobility * totals(magnitude)
            seen = dot(split_rows(velocity), incidence[...])
            relative = jnp.sum(
                normal * (seen[0:8] + (seen[8:16] + seen[16:24])), axis=0, keepdims=True
            )
            return jnp.maximum(
                magnitude
                - relaxation * (gap + time_step * relative) / (2.0 * time_step * mobility),
                0.0,
            )

        magnitude = lax.fori_loop(0, SWEEPS, sweep, jnp.zeros((1, contacts), F32))
        drift = time_step * (hydro + mobility * totals(magnitude))
        wide_force[...] = jnp.broadcast_to(magnitude, wide_force.shape)
        wide_drift[...] = drift
        place = device * own_contacts
        at = pl.ds(pl.multiple_of(place // 128 * 128, 128), 128)
        turned = pltpu.roll(wide_force[:, at], (128 - place % 128) % 128, 1)
        force_ref[...] = turned[0:1, :own_contacts]
        place = device * per_device
        at = pl.ds(pl.multiple_of(place // 128 * 128, 128), 128)
        own = pltpu.roll(wide_drift[:, at], (128 - place % 128) % 128, 1).T
        for a in range(side):
            moved_ref[a] = centers[a] + own[a * side : (a + 1) * side, 0:3]

    return kernel


def vmem_of(held):
    return pltpu.CompilerParams(vmem_limit_bytes=min(60 << 20, 2 * held + (12 << 20)))


def local(
    tractions,
    centers,
    node_offsets,
    occupied,
    anchors,
    near_list,
    contact_pairs,
    contact_gap,
    contact_angles,
):
    side = tractions.shape[0]
    per_device = side * side
    nodes = tractions.shape[3]
    narrow_count = lax.axis_size("narrow")
    devices = lax.axis_size("wide") * narrow_count
    rank = lax.axis_index("wide") * narrow_count + lax.axis_index("narrow")
    slots = devices * per_device
    contacts_own = contact_gap.shape[0]
    contacts = contacts_own * devices
    pairs = max(MIN_PAIRS, HALF // devices)
    z_groups = HALF // pairs
    x_groups = max(1, devices // z_groups)
    half_x = HALF // x_groups
    z_group = rank % z_groups
    x_group = rank // z_groups
    rows = 6 * pairs
    hydro_rows = -(-slots // nodes)

    vmem = pl.BlockSpec(memory_space=pltpu.VMEM)
    smem = pl.BlockSpec(memory_space=pltpu.SMEM)
    by_row = tractions.transpose(0, 2, 1, 3)
    packed = pl.pallas_call(
        pack_kernel,
        out_shape=jax.ShapeDtypeStruct((slots, 4, nodes), F32),
        in_specs=[smem] * 4 + [vmem] * 4,
        out_specs=vmem,
        scratch_shapes=[pltpu.VMEM((8, 128), F32)],
        name="pack",
    )(
        centers,
        anchors,
        occupied,
        near_list,
        by_row,
        contact_pairs,
        contact_gap[None],
        contact_angles,
    )
    gathered = lax.all_to_all(packed, AXES, split_axis=0, concat_axis=0, tiled=True)
    offsets_t = node_offsets.T
    self_near = pl.pallas_call(
        self_kernel,
        out_shape=jax.ShapeDtypeStruct((per_device, 3, nodes), F32),
        in_specs=[smem] + [vmem] * 3,
        out_specs=vmem,
        scratch_shapes=[pltpu.VMEM((nodes, 8), F32)],
        name="near_self",
    )(occupied, by_row, node_offsets, offsets_t)
    scalars = gathered[:, 3, :16]

    xy, zz = z_tables()
    tables = np.concatenate(
        [
            xy.reshape(z_groups, 2 * pairs, GRID + BLOCK),
            zz.reshape(z_groups, 2 * pairs, GRID + BLOCK),
        ],
        axis=1,
    )
    table = lax.dynamic_index_in_dim(jnp.asarray(tables, F32), z_group, 0, keepdims=False)
    basis = real_basis()
    turned = np.ascontiguousarray(basis.T)
    ry = [jnp.asarray(v) for v in split_np(basis)]
    ryt = [jnp.asarray(v) for v in split_np(turned)]
    if x_groups == 1:
        rx, rxt = ry, ryt
    else:
        rxt = [
            lax.dynamic_index_in_dim(
                v.reshape(2, x_groups, half_x, GRID), x_group, 1, keepdims=False
            ).reshape(2 * half_x, GRID)
            for v in ryt
        ]
        rx = [v.T for v in rxt]

    keep = slots * nodes * BLOCK * 16 <= KEEP_BYTES
    kept = slots + UNROLL if keep else 1
    ranks = jnp.stack([z_group, x_group, rank]).astype(jnp.int32)
    partial = pl.pallas_call(
        far_kernel(pairs, slots, devices, hydro_rows, keep),
        out_shape=jax.ShapeDtypeStruct((slots, 3 + hydro_rows, nodes), F32),
        in_specs=[smem, smem] + [vmem] * 13,
        out_specs=vmem,
        scratch_shapes=[
            pltpu.SMEM((slots + 1,), jnp.int32),
            pltpu.VMEM((4, (GRID + BLOCK) * rows, HALF), F32),
            pltpu.VMEM((UNROLL, GRID, nodes), BF16),
            pltpu.VMEM((3, 2 * half_x, GRID), F32),
            pltpu.VMEM((8, slots), F32),
            pltpu.VMEM((nodes, 8), F32),
            pltpu.VMEM((GRID + BLOCK, 4 * pairs, 128), F32),
            pltpu.VMEM((kept, BLOCK, nodes), F32),
            pltpu.VMEM((kept, 4 * pairs, nodes), F32),
            pltpu.VMEM((kept, 4, BLOCK, nodes), BF16),
        ],
        compiler_params=vmem_of(8 * slots * nodes * 4 + 4 * (GRID + BLOCK) * 6 * pairs * HALF * 4),
        name="far_near",
    )(
        scalars,
        ranks,
        gathered,
        node_offsets,
        offsets_t,
        self_near,
        table,
        *ry,
        *ryt,
        *rx,
        *rxt,
    )
    received = lax.all_to_all(partial, AXES, split_axis=0, concat_axis=0, tiled=True)
    incidence, contact_rows = pl.pallas_call(
        prepare_kernel(slots, devices, contacts_own),
        out_shape=(
            jax.ShapeDtypeStruct((slots, contacts), BF16),
            jax.ShapeDtypeStruct((8, contacts), F32),
        ),
        in_specs=[vmem],
        out_specs=(vmem, vmem),
        compiler_params=vmem_of(4 * slots * nodes * 4 + slots * contacts * 2),
        name="contact_rows",
    )(gathered)
    velocity, force, moved = pl.pallas_call(
        contact_kernel(slots, devices, hydro_rows, contacts_own),
        out_shape=(
            jax.ShapeDtypeStruct((side, 3, side, nodes), F32),
            jax.ShapeDtypeStruct((1, contacts_own), F32),
            jax.ShapeDtypeStruct((side, side, 3), F32),
        ),
        in_specs=[smem, vmem, vmem, vmem, vmem],
        out_specs=(vmem, vmem, vmem),
        scratch_shapes=[
            pltpu.VMEM((8, contacts), F32),
            pltpu.VMEM((8, slots), F32),
        ],
        compiler_params=vmem_of((3 + hydro_rows) * slots * nodes * 4 + slots * contacts * 2),
        name="contacts",
    )(ranks, received, incidence, contact_rows, centers)
    return (velocity.transpose(0, 2, 1, 3), force[0], moved)


def solution(mesh):
    placed = (
        P("wide", "narrow", None, None),
        P("wide", "narrow", None),
        P(),
        P("wide", "narrow"),
        P("wide", "narrow", None),
        P("wide", "narrow", None),
        P(None, ("wide", "narrow")),
        P(("wide", "narrow")),
        P(None, ("wide", "narrow")),
    )
    return jax.shard_map(
        local,
        mesh=mesh,
        in_specs=placed,
        out_specs=(
            P("wide", "narrow", None, None),
            P(("wide", "narrow")),
            P("wide", "narrow", None),
        ),
        check_vma=False,
    )
```

```python
import jax
import jax.numpy as jnp
import numpy as np
from jax import lax
from jax.experimental import pallas as pl
from jax.experimental.pallas import tpu as pltpu
from jax.sharding import PartitionSpec as P

GRID = 256
HALF = GRID // 2
BLOCK = 16
SWEEPS = 6
MIN_PAIRS = 4
AXES = ("wide", "narrow")
KEEP_BYTES = 16 << 20
UNROLL = 6

soften = 1.0
screen = 0.0625
near_scale = 0.05
spread_norm = 0.17958712212516656
mobility = 0.2
time_step = 0.5
relaxation = 0.35
ewald_split = 0.5

F32 = jnp.float32
BF16 = jnp.bfloat16
NT = (((1,), (1,)), ((), ()))
NN = (((1,), (0,)), ((), ()))


def real_basis():
    cells = np.arange(GRID)
    angle = 2.0 * np.pi * (np.outer(cells, np.arange(HALF)) % GRID) / GRID
    sine = np.sin(angle)
    sine[:, 0] = np.cos(np.pi * cells)
    return np.concatenate([np.cos(angle), sine], axis=1)


def z_tables():
    pairs = np.arange(HALF)
    cells = np.arange(GRID + BLOCK)
    angle = 2.0 * np.pi * (np.outer(pairs, cells) % GRID) / GRID
    cosine, sine = np.cos(angle), np.sin(angle)
    nyquist = np.cos(np.pi * cells)
    xy = np.stack([cosine, sine], axis=1)
    zz = np.stack([-sine, cosine], axis=1)
    xy[0, 0] = zz[0, 0] = 1.0
    xy[0, 1] = zz[0, 1] = nyquist
    return xy, zz


def split_np(table):
    high = np.asarray(table, dtype=BF16)
    low = np.asarray(table - high.astype(np.float64), dtype=BF16)
    return high, low


def split2(value):
    high = value.astype(BF16)
    return high, (value - high.astype(F32)).astype(BF16)


def dot(a, b, dims=NN):
    return lax.dot_general(a, b, dims, preferred_element_type=F32)


def dot3(a, b):
    count = a[0].shape[0]
    both = dot(jnp.concatenate([a[0], a[1]], axis=0), b[0])
    return both[:count] + (both[count:] + dot(a[0], b[1]))


def split_rows(value):
    high = value.astype(BF16).astype(F32)
    rest = value - high
    middle = rest.astype(BF16).astype(F32)
    return jnp.concatenate([high, middle, rest - middle], axis=0).astype(BF16)


def near_tile(shifted, offt_ref, push_ref, nodes):
    def part(j, sums):
        at = pl.ds(pl.multiple_of(j * 8, 8), 8)
        own = offt_ref[at, :]
        push = push_ref[at, :]
        sep = [shifted[d] - own[:, d : d + 1] for d in range(3)]
        pushes = [push[:, d : d + 1] for d in range(3)]
        square = sep[0] * sep[0] + sep[1] * sep[1] + sep[2] * sep[2]
        root = lax.rsqrt(square + soften)
        weight = jnp.exp(-square * screen) * (root * root * root)
        projected = sep[0] * pushes[0] + sep[1] * pushes[1] + sep[2] * pushes[2]
        diagonal = (square + 2.0 * soften) * weight
        leaning = projected * weight
        return tuple(sums[d] + (diagonal * pushes[d] + sep[d] * leaning) for d in range(3))

    zero = jnp.zeros((8, nodes), F32)
    sums = lax.fori_loop(0, nodes // 8, part, (zero, zero, zero), unroll=True)
    return near_scale * jnp.concatenate(
        [jnp.sum(v, axis=0, keepdims=True) for v in sums], axis=0
    )


def field_lane(q, own_contacts):
    per_tile = 128 // own_contacts
    ahead = per_tile // 2
    return 64 + q * own_contacts if q < ahead else 128 + (q - ahead) * own_contacts


def pack_kernel(
    centers, anchors, occupied, near_list, tractions, pairs, gap, angles, out_ref, fields
):
    side = tractions.shape[0]
    per_device = side * side
    own_contacts = pairs.shape[1]
    fields[...] = jnp.zeros(fields.shape, F32)
    fields[0:2, :own_contacts] = pairs[...].astype(F32)
    fields[2:3, :own_contacts] = gap[...]
    fields[3:5, :own_contacts] = angles[...]
    lane = lax.broadcasted_iota(jnp.int32, (1, 128), 1)
    row = jnp.zeros((1, 128), F32)
    pieces = []
    for k in range(per_device):
        a, b = divmod(k, side)
        values = [centers[a, b, d] for d in range(3)]
        values += [anchors[a, b, d].astype(F32) for d in range(3)]
        values.append(occupied[a, b].astype(F32))
        values += [near_list[a, b, j].astype(F32) for j in range(near_list.shape[2])]
        for j, value in enumerate(values):
            row = jnp.where(lane == k * 16 + j, value, row)
        pieces += [tractions[a, d : d + 1, b] for d in range(3)]
    tail = [row, jnp.zeros((1, 128), F32)]
    for q in range(5):
        which, shift = divmod(field_lane(q, own_contacts), 128)
        field = fields[q : q + 1, :]
        tail[which] = tail[which] + (pltpu.roll(field, shift, 1) if shift else field)
    message = jnp.concatenate(pieces + tail, axis=1)

    def send(holder, c):
        out_ref[holder] = message
        return c

    lax.fori_loop(0, out_ref.shape[0], send, 0, unroll=8)


def self_kernel(occupied, tractions, off_ref, offt_ref, out_ref, push):
    side = tractions.shape[0]
    nodes = tractions.shape[3]
    out_ref[...] = jnp.zeros(out_ref.shape, F32)

    for k in range(side * side):
        a, b = divmod(k, side)

        @pl.when(occupied[a, b] > 0)
        def _(a=a, b=b, k=k):
            push[...] = jnp.concatenate(
                [tractions[a, :, b], jnp.zeros((5, nodes), F32)], axis=0
            ).T
            shifted = [off_ref[d : d + 1, :] for d in range(3)]
            out_ref[k] = near_tile(shifted, offt_ref, push, nodes)


def far_kernel(pairs, slots, devices, keep):
    rows_c = 2 * pairs
    rows = 3 * rows_c

    def kernel(
        misc,
        ranks,
        g_ref,
        off_ref,
        offt_ref,
        self_ref,
        tab_in,
        ryh,
        ryl,
        ryth,
        rytl,
        rxh,
        rxl,
        rxth,
        rxtl,
        out_ref,
        listed,
        acc,
        wy,
        sbuf,
        hyd,
        ft,
        tab_ref,
        kept_wx,
        kept_table,
        kept_wy,
    ):
        z_group, x_group, device = ranks[0], ranks[1], ranks[2]
        nodes = off_ref.shape[1]
        per_device = slots // devices

        def scalar(s, j):
            return misc[s // per_device, s % per_device * 16 + j]

        def lines(s, d):
            return pl.ds(pl.multiple_of((s % per_device * 3 + d) * nodes, nodes), nodes)

        def force_row(s, d):
            return g_ref[s // per_device, :, lines(s, d)]

        half_x = rxh.shape[1] // 2

        out_ref[...] = jnp.zeros(out_ref.shape, F32)
        strip = acc.shape[1] // BLOCK
        scanned = slots // BLOCK

        def start(i, n):
            at = pl.ds(pl.multiple_of(i * strip, 8), strip)
            for tile in range(4):
                acc[tile, at, :] = jnp.zeros((strip, HALF), F32)
            for j in range(scanned):
                s = i * scanned + j
                listed[n] = s
                n = n + (scalar(s, 6) > 0.5).astype(jnp.int32)
            return n

        count = lax.fori_loop(0, BLOCK, start, jnp.int32(0))
        for z in range(GRID + BLOCK):
            tab_ref[z] = jnp.broadcast_to(tab_in[:, z : z + 1], tab_ref.shape[1:])
        wy[...] = jnp.zeros(wy.shape, BF16)
        hyd[...] = jnp.zeros(hyd.shape, F32)

        steps = lax.broadcasted_iota(jnp.int32, (BLOCK, nodes), 0)

        def positions(s):
            anchor = [scalar(s, 3 + d).astype(jnp.int32) for d in range(3)]
            local_y = anchor[1] % HALF
            late = (local_y > HALF - BLOCK).astype(jnp.int32)
            local_y = local_y - late * (HALF // 2)
            tile = 2 * (anchor[1] // HALF) + late
            where = pl.ds(pl.multiple_of(anchor[0] * rows, rows), BLOCK * rows)
            return anchor, where, tile, local_y

        def factors(s, anchor, local_y):
            pos = [off_ref[d : d + 1, :] + scalar(s, d) for d in range(3)]

            def weights(d, shift):
                away = pos[d] - (anchor[d] + steps + shift).astype(F32)
                return jnp.exp(-away * away)

            wx = weights(0, 0)
            wz = weights(2, 0)
            inner = local_y % BLOCK
            parts = []
            for i in range(2):
                t = steps + (i * BLOCK - inner)
                parts.append(
                    split2(
                        jnp.where((t >= 0) & (t < BLOCK), weights(1, i * BLOCK - inner), 0.0)
                    )
                )
            table = jnp.zeros((2 * rows_c, nodes), F32)
            for t in range(BLOCK):
                phase = tab_ref[anchor[2] + t]
                phase = jnp.concatenate([phase] * (nodes // 128), axis=1)
                table = table + phase * wz[t : t + 1, :]
            return wx, table, parts

        def lay(buffer, local_y, parts, doubled):
            first = local_y // BLOCK
            places = []
            for i, (high, low) in enumerate(parts):
                near_row = ((first + i) % 8) * BLOCK
                if doubled:
                    writes = (
                        (near_row, high),
                        (((first + i + 4) % 8) * BLOCK, low),
                        (near_row + HALF, high),
                    )
                else:
                    writes = ((near_row, high), (near_row + HALF, low))
                for row, part in writes:
                    row = pl.multiple_of(row, BLOCK)
                    wy[buffer, pl.ds(row, BLOCK), :] = part
                    places.append(row)
            return places

        def prepare(at, s, buffer, doubled):
            anchor, where, tile, local_y = positions(s)
            if doubled and keep:
                wx, table = kept_wx[at], kept_table[at]
                parts = [(kept_wy[at, i], kept_wy[at, 2 + i]) for i in range(2)]
            else:
                wx, table, parts = factors(s, anchor, local_y)
                if keep:
                    kept_wx[at] = wx
                    kept_table[at] = table
                    for i in range(2):
                        kept_wy[at, i] = parts[i][0]
                        kept_wy[at, 2 + i] = parts[i][1]
            places = lay(buffer, local_y, parts, doubled)
            zed = jnp.concatenate([table[:rows_c], table], axis=0)
            return where, tile, local_y, wx, zed, places

        def forget(buffer, places):
            for row in places:
                wy[buffer, pl.ds(row, BLOCK), :] = jnp.zeros((BLOCK, nodes), BF16)

        def members(i):
            found = []
            for u in range(UNROLL):
                at = i * UNROLL + u
                there = (at < count).astype(F32)
                found.append((listed[jnp.minimum(at, count - 1)], there))
            return found

        trips = (count + (UNROLL - 1)) // UNROLL

        def spread(i, c):
            group = members(i)
            ready = [prepare(i * UNROLL + u, s, u, False) for u, (s, _) in enumerate(group)]
            patches = []
            for u, (s, there) in enumerate(group):
                _, _, _, wx, zed, _ = ready[u]
                force = jnp.concatenate(
                    [
                        jnp.broadcast_to(force_row(s, d) * there, (rows_c, nodes))
                        for d in range(3)
                    ],
                    axis=0,
                )
                loaded = force * zed
                left = jnp.concatenate([loaded * wx[a : a + 1, :] for a in range(BLOCK)], axis=0)
                high, low = split2(left)
                upper = dot(high, wy[u], NT)
                lower = dot(low, wy[u], NT)
                patches.append(upper[:, :HALF] + (upper[:, HALF:] + lower[:, :HALF]))
            for u, patch in enumerate(patches):
                where, tile, _, _, _, places = ready[u]
                acc[tile, where, :] = acc[tile, where, :] + patch
                forget(u, places)
            return c

        lax.fori_loop(0, trips, spread, 0)
        acc[:, : BLOCK * rows, :] = acc[:, : BLOCK * rows, :] + acc[:, GRID * rows :, :]
        low_half = lax.broadcasted_iota(jnp.int32, (GRID, HALF), 1) < HALF // 2

        def turned(value):
            return pltpu.roll(value, HALF // 2, 1)

        damping = (ewald_split * np.pi / GRID) ** 2
        constant = spread_norm**2 * GRID * GRID / (4.0 * np.pi**2) / GRID**3
        k_lane = lax.broadcasted_iota(jnp.int32, (8, HALF), 1).astype(F32)
        y_edge = jnp.where(k_lane == 0.0, float(HALF), 0.0)
        ky = ((k_lane, jnp.zeros_like(k_lane)), (k_lane, y_edge))
        y_factor = jnp.where(k_lane == 0.0, 1.0, 2.0)

        def wave_slot(r, c):
            pair = z_group * pairs + r // 2
            is_first = pair == 0
            kz = jnp.where(is_first, 0, pair).astype(F32)
            nz = jnp.where(is_first & (r % 2 == 1), HALF, 0).astype(F32)
            kz2 = kz * kz + nz * nz
            z_factor = jnp.where(is_first, 1.0, 2.0) * constant
            slabs = []
            for comp in range(3):
                line = pl.ds(comp * rows_c + r, GRID, stride=rows)
                odd0, odd1 = turned(acc[1, line, :]), turned(acc[3, line, :])
                data = jnp.concatenate(
                    [
                        acc[0, line, :] + jnp.where(low_half, odd1, odd0),
                        acc[2, line, :] + jnp.where(low_half, odd0, odd1),
                    ],
                    axis=1,
                )
                slabs.append(data)
            for comp in range(3):
                mid = dot3(split2(slabs[comp]), (ryh[...], ryl[...]))
                sbuf[comp] = dot3((rxth[...], rxtl[...]), split2(mid))

            def filtered(i, c2):
                row = pl.multiple_of(i * 8, 8)
                k_row = (
                    lax.broadcasted_iota(jnp.int32, (8, HALF), 0) + (row + x_group * half_x)
                ).astype(F32)
                x_edge = jnp.where(k_row == 0.0, float(HALF), 0.0)
                kxn = (None, x_edge)
                scale = jnp.where(k_row == 0.0, 1.0, 2.0) * y_factor * z_factor
                spectrum = [
                    [
                        [
                            sbuf[comp, pl.ds(row + hx * half_x, 8), hy * HALF : (hy + 1) * HALF]
                            for hy in range(2)
                        ]
                        for hx in range(2)
                    ]
                    for comp in range(3)
                ]
                sx, sy, sz = spectrum
                total = [[None, None], [None, None]]
                for hx in range(2):
                    for hy in range(2):
                        jx = sx[0][hy] if hx else -sx[1][hy]
                        jy = sy[hx][0] if hy else -sy[hx][1]
                        total[hx][hy] = k_row * jx + k_lane * jy + kz * sz[hx][hy]
                for hx in range(2):
                    for hy in range(2):
                        square = k_row * k_row + k_lane * k_lane + kz2
                        edge = nz * sz[hx][hy]
                        if hx:
                            square = square + x_edge * x_edge
                            edge = edge + x_edge * sx[hx][hy]
                        if hy:
                            square = square + y_edge * y_edge
                            edge = edge + y_edge * sy[hx][hy]
                        inverse = 1.0 / jnp.maximum(square, 1.0)
                        factor = jnp.where(
                            square > 0.5, jnp.exp(-damping * square) * inverse, 0.0
                        ) * scale
                        tx = total[0][hy] if hx else -total[1][hy]
                        ty = total[hx][0] if hy else -total[hx][1]
                        along_x = k_row * tx
                        along_y = k_lane * ty
                        if hx:
                            along_x = along_x - x_edge * edge
                        if hy:
                            along_y = along_y - y_edge * edge
                        along_z = kz * total[hx][hy] + nz * edge
                        lanes = slice(hy * HALF, (hy + 1) * HALF)
                        at = pl.ds(row + hx * half_x, 8)
                        sbuf[0, at, lanes] = factor * (sx[hx][hy] + along_x * inverse)
                        sbuf[1, at, lanes] = factor * (sy[hx][hy] + along_y * inverse)
                        sbuf[2, at, lanes] = factor * (sz[hx][hy] - along_z * inverse)
                return c2

            lax.fori_loop(0, half_x // 8, filtered, 0, unroll=True)
            for comp in range(3):
                line = pl.ds(comp * rows_c + r, GRID, stride=rows)
                mid = dot3((rxh[...], rxl[...]), split2(sbuf[comp]))
                data = dot3(split2(mid), (ryth[...], rytl[...]))
                even0, even1 = data[:, :HALF], data[:, HALF:]
                odd0, odd1 = turned(even0), turned(even1)
                acc[0, line, :] = even0
                acc[1, line, :] = jnp.where(low_half, odd0, odd1)
                acc[2, line, :] = even1
                acc[3, line, :] = jnp.where(low_half, odd1, odd0)
            return c

        lax.fori_loop(0, rows_c, wave_slot, 0, unroll=2)
        acc[:, GRID * rows :, :] = acc[:, : BLOCK * rows, :]
        slot_lane = lax.broadcasted_iota(jnp.int32, (8, hyd.shape[1]), 1)

        def add_out(s, values):
            padded = jnp.concatenate([values, jnp.zeros((5, nodes), F32)], axis=0)
            for d in range(3):
                at = lines(s, d)
                holder = s // per_device
                out_ref[holder, :, at] = out_ref[holder, :, at] + values[d : d + 1]
            mean = jnp.sum(padded, axis=1, keepdims=True) * (1.0 / nodes)
            hyd[...] = hyd[...] + jnp.where(slot_lane == s, mean, 0.0)

        lanes = lax.broadcasted_iota(jnp.int32, (BLOCK * rows, HALF), 1)

        def sample(i, c):
            group = members(i)
            ready = [prepare(i * UNROLL + u, s, u, True) for u, (s, _) in enumerate(group)]
            results = []
            for u in range(UNROLL):
                where, tile, local_y, wx, zed, _ = ready[u]
                block = acc[tile, where, :]
                chosen = ((lanes - local_y) & (HALF - 1)) < HALF // 2
                high, low = split2(jnp.where(chosen, block, turned(block)))
                seen = dot(jnp.concatenate([high, low], axis=1), wy[u])
                total = seen[:rows] * wx[0:1, :]
                for a in range(1, BLOCK):
                    total = total + seen[a * rows : (a + 1) * rows] * wx[a : a + 1, :]
                total = total * zed
                results.append(
                    jnp.concatenate(
                        [
                            jnp.sum(total[d * rows_c : (d + 1) * rows_c], axis=0, keepdims=True)
                            for d in range(3)
                        ],
                        axis=0,
                    )
                )
            for u, (s, there) in enumerate(group):
                add_out(s, results[u] * there)
                forget(u, ready[u][5])
            return c

        lax.fori_loop(0, trips, sample, 0)

        def near_task(i, c):
            task = device + i * devices
            s = listed[task // 2]
            source = scalar(s, 7 + task % 2).astype(jnp.int32)
            ft[...] = jnp.concatenate(
                [force_row(source, d) for d in range(3)] + [jnp.zeros((5, nodes), F32)], axis=0
            ).T
            shifted = []
            for d in range(3):
                gap = jnp.full((1, nodes), scalar(s, d) - scalar(source, d), F32)
                gap = gap - GRID * jnp.floor(gap / GRID + 0.5)
                shifted.append(gap + off_ref[d : d + 1, :])
            add_out(s, near_tile(shifted, offt_ref, ft, nodes))
            return c

        tasks = (2 * count - device + (devices - 1)) // devices
        lax.fori_loop(0, tasks, near_task, 0)
        for k in range(per_device):
            add_out(device * per_device + k, self_ref[k])

        def publish(holder, c):
            for d in range(3):
                first = 3 * per_device * nodes + d * slots
                out_ref[holder, :, first : first + slots] = hyd[d : d + 1, :]
            return c

        lax.fori_loop(0, devices, publish, 0)

    return kernel


def prepare_kernel(slots, devices, own_contacts):
    per_tile = 128 // own_contacts
    tiles = devices // per_tile

    def kernel(g_ref, incidence, rows_ref):
        contacts = incidence.shape[1]
        lane = lax.broadcasted_iota(jnp.int32, (tiles, 128), 1)

        def field(q):
            which, shift = divmod(field_lane(q, own_contacts), 128)
            low = g_ref.shape[2] - 256 + 128 * which
            total = jnp.zeros((tiles, 128), F32)
            for j in range(per_tile):
                part = jnp.concatenate(
                    [
                        g_ref[t * per_tile + j, :, low : low + 128]
                        for t in range(tiles)
                    ],
                    axis=0,
                )
                turn = (j * own_contacts - shift) % 128
                if turn:
                    part = pltpu.roll(part, turn, 1)
                total = jnp.where(lane // own_contacts == j, part, total)
            return jnp.concatenate([total[t : t + 1] for t in range(tiles)], axis=1)

        first = field(0).astype(jnp.int32)
        second = field(1).astype(jnp.int32)
        polar = field(3)
        azimuth = field(4)
        rows_ref[...] = jnp.concatenate(
            [
                jnp.sin(polar) * jnp.cos(azimuth),
                jnp.sin(polar) * jnp.sin(azimuth),
                jnp.cos(polar),
                field(2),
                jnp.zeros((4, contacts), F32),
            ],
            axis=0,
        )

        def build(i, c):
            row = pl.multiple_of(i * 16, 16)
            ids = lax.broadcasted_iota(jnp.int32, (16, contacts), 0) + row
            value = jnp.where(first == ids, 1.0, 0.0) - jnp.where(second == ids, 1.0, 0.0)
            incidence[pl.ds(row, 16), :] = value.astype(BF16)
            return c

        lax.fori_loop(0, slots // 16, build, 0)

    return kernel


def contact_kernel(slots, devices, own_contacts):
    per_device = slots // devices

    def kernel(
        ranks,
        recv_ref,
        incidence,
        rows_ref,
        centers,
        velocity_ref,
        force_ref,
        moved_ref,
        wide_force,
        wide_drift,
    ):
        contacts = rows_ref.shape[1]
        side = centers.shape[0]
        device = ranks[2]

        def gather(holder, total):
            return total + recv_ref[holder]

        summed = lax.fori_loop(1, devices, gather, recv_ref[0], unroll=8)
        nodes = velocity_ref.shape[3]
        for a in range(side):
            for b in range(side):
                for d in range(3):
                    first = ((a * side + b) * 3 + d) * nodes
                    velocity_ref[a, d : d + 1, b] = summed[:, first : first + nodes]
        means = 3 * per_device * nodes
        hydro = jnp.concatenate(
            [summed[:, means + d * slots : means + (d + 1) * slots] for d in range(3)]
            + [jnp.zeros((5, slots), F32)],
            axis=0,
        )
        gap = rows_ref[3:4, :]
        kind = lax.broadcasted_iota(jnp.int32, (8, contacts), 0)
        normal = jnp.where(kind < 3, rows_ref[...], 0.0)

        def totals(magnitude):
            spread = dot(split_rows(magnitude * normal), incidence[...], NT)
            return spread[0:8] + (spread[8:16] + spread[16:24])

        def sweep(i, magnitude):
            velocity = hydro + mobility * totals(magnitude)
            seen = dot(split_rows(velocity), incidence[...])
            relative = jnp.sum(
                normal * (seen[0:8] + (seen[8:16] + seen[16:24])), axis=0, keepdims=True
            )
            return jnp.maximum(
                magnitude
                - relaxation * (gap + time_step * relative) / (2.0 * time_step * mobility),
                0.0,
            )

        magnitude = lax.fori_loop(0, SWEEPS, sweep, jnp.zeros((1, contacts), F32))
        drift = time_step * (hydro + mobility * totals(magnitude))
        wide_force[...] = jnp.broadcast_to(magnitude, wide_force.shape)
        wide_drift[...] = drift
        place = device * own_contacts
        at = pl.ds(pl.multiple_of(place // 128 * 128, 128), 128)
        turned = pltpu.roll(wide_force[:, at], (128 - place % 128) % 128, 1)
        force_ref[...] = turned[0:1, :own_contacts]
        place = device * per_device
        at = pl.ds(pl.multiple_of(place // 128 * 128, 128), 128)
        own = pltpu.roll(wide_drift[:, at], (128 - place % 128) % 128, 1).T
        for a in range(side):
            moved_ref[a] = centers[a] + own[a * side : (a + 1) * side, 0:3]

    return kernel


def vmem_of(held):
    return pltpu.CompilerParams(vmem_limit_bytes=min(60 << 20, 2 * held + (12 << 20)))


def local(
    tractions,
    centers,
    node_offsets,
    occupied,
    anchors,
    near_list,
    contact_pairs,
    contact_gap,
    contact_angles,
):
    side = tractions.shape[0]
    per_device = side * side
    nodes = tractions.shape[3]
    narrow_count = lax.axis_size("narrow")
    devices = lax.axis_size("wide") * narrow_count
    rank = lax.axis_index("wide") * narrow_count + lax.axis_index("narrow")
    slots = devices * per_device
    contacts_own = contact_gap.shape[0]
    contacts = contacts_own * devices
    pairs = max(MIN_PAIRS, HALF // devices)
    z_groups = HALF // pairs
    x_groups = max(1, devices // z_groups)
    half_x = HALF // x_groups
    z_group = rank % z_groups
    x_group = rank // z_groups
    rows = 6 * pairs

    vmem = pl.BlockSpec(memory_space=pltpu.VMEM)
    smem = pl.BlockSpec(memory_space=pltpu.SMEM)
    forces = 3 * per_device * nodes
    by_row = tractions.transpose(0, 2, 1, 3)
    packed = pl.pallas_call(
        pack_kernel,
        out_shape=jax.ShapeDtypeStruct((devices, 1, forces + 256), F32),
        in_specs=[smem] * 4 + [vmem] * 4,
        out_specs=vmem,
        scratch_shapes=[pltpu.VMEM((8, 128), F32)],
        name="pack",
    )(
        centers,
        anchors,
        occupied,
        near_list,
        by_row,
        contact_pairs,
        contact_gap[None],
        contact_angles,
    )
    gathered = lax.all_to_all(packed, AXES, split_axis=0, concat_axis=0, tiled=True)
    offsets_t = node_offsets.T
    self_near = pl.pallas_call(
        self_kernel,
        out_shape=jax.ShapeDtypeStruct((per_device, 3, nodes), F32),
        in_specs=[smem] + [vmem] * 3,
        out_specs=vmem,
        scratch_shapes=[pltpu.VMEM((nodes, 8), F32)],
        name="near_self",
    )(occupied, by_row, node_offsets, offsets_t)
    scalars = gathered[:, 0, forces : forces + 16 * per_device]

    xy, zz = z_tables()
    tables = np.concatenate(
        [
            xy.reshape(z_groups, 2 * pairs, GRID + BLOCK),
            zz.reshape(z_groups, 2 * pairs, GRID + BLOCK),
        ],
        axis=1,
    )
    table = lax.dynamic_index_in_dim(jnp.asarray(tables, F32), z_group, 0, keepdims=False)
    basis = real_basis()
    turned = np.ascontiguousarray(basis.T)
    ry = [jnp.asarray(v) for v in split_np(basis)]
    ryt = [jnp.asarray(v) for v in split_np(turned)]
    if x_groups == 1:
        rx, rxt = ry, ryt
    else:
        rxt = [
            lax.dynamic_index_in_dim(
                v.reshape(2, x_groups, half_x, GRID), x_group, 1, keepdims=False
            ).reshape(2 * half_x, GRID)
            for v in ryt
        ]
        rx = [v.T for v in rxt]

    keep = slots * nodes * BLOCK * 16 <= KEEP_BYTES
    kept = slots + UNROLL if keep else 1
    ranks = jnp.stack([z_group, x_group, rank]).astype(jnp.int32)
    partial = pl.pallas_call(
        far_kernel(pairs, slots, devices, keep),
        out_shape=jax.ShapeDtypeStruct((devices, 1, forces + 3 * slots), F32),
        in_specs=[smem, smem] + [vmem] * 13,
        out_specs=vmem,
        scratch_shapes=[
            pltpu.SMEM((slots + 1,), jnp.int32),
            pltpu.VMEM((4, (GRID + BLOCK) * rows, HALF), F32),
            pltpu.VMEM((UNROLL, GRID, nodes), BF16),
            pltpu.VMEM((3, 2 * half_x, GRID), F32),
            pltpu.VMEM((8, slots), F32),
            pltpu.VMEM((nodes, 8), F32),
            pltpu.VMEM((GRID + BLOCK, 4 * pairs, 128), F32),
            pltpu.VMEM((kept, BLOCK, nodes), F32),
            pltpu.VMEM((kept, 4 * pairs, nodes), F32),
            pltpu.VMEM((kept, 4, BLOCK, nodes), BF16),
        ],
        compiler_params=vmem_of(8 * slots * nodes * 4 + 4 * (GRID + BLOCK) * 6 * pairs * HALF * 4),
        name="far_near",
    )(
        scalars,
        ranks,
        gathered,
        node_offsets,
        offsets_t,
        self_near,
        table,
        *ry,
        *ryt,
        *rx,
        *rxt,
    )
    received = lax.all_to_all(partial, AXES, split_axis=0, concat_axis=0, tiled=True)
    incidence, contact_rows = pl.pallas_call(
        prepare_kernel(slots, devices, contacts_own),
        out_shape=(
            jax.ShapeDtypeStruct((slots, contacts), BF16),
            jax.ShapeDtypeStruct((8, contacts), F32),
        ),
        in_specs=[vmem],
        out_specs=(vmem, vmem),
        compiler_params=vmem_of(4 * slots * nodes * 4 + slots * contacts * 2),
        name="contact_rows",
    )(gathered)
    velocity, force, moved = pl.pallas_call(
        contact_kernel(slots, devices, contacts_own),
        out_shape=(
            jax.ShapeDtypeStruct((side, 3, side, nodes), F32),
            jax.ShapeDtypeStruct((1, contacts_own), F32),
            jax.ShapeDtypeStruct((side, side, 3), F32),
        ),
        in_specs=[smem, vmem, vmem, vmem, vmem],
        out_specs=(vmem, vmem, vmem),
        scratch_shapes=[
            pltpu.VMEM((8, contacts), F32),
            pltpu.VMEM((8, slots), F32),
        ],
        compiler_params=vmem_of(8 * slots * nodes * 4 + slots * contacts * 2),
        name="contacts",
    )(ranks, received, incidence, contact_rows, centers)
    return (velocity.transpose(0, 2, 1, 3), force[0], moved)


def solution(mesh):
    placed = (
        P("wide", "narrow", None, None),
        P("wide", "narrow", None),
        P(),
        P("wide", "narrow"),
        P("wide", "narrow", None),
        P("wide", "narrow", None),
        P(None, ("wide", "narrow")),
        P(("wide", "narrow")),
        P(None, ("wide", "narrow")),
    )
    return jax.shard_map(
        local,
        mesh=mesh,
        in_specs=placed,
        out_specs=(
            P("wide", "narrow", None, None),
            P(("wide", "narrow")),
            P("wide", "narrow", None),
        ),
        check_vma=False,
    )
```

```python
import jax
import jax.numpy as jnp
import numpy as np
from jax import lax
from jax.experimental import pallas as pl
from jax.experimental.pallas import tpu as pltpu
from jax.sharding import PartitionSpec as P

GRID = 256
HALF = GRID // 2
BLOCK = 16
SWEEPS = 6
MIN_PAIRS = 4
AXES = ("wide", "narrow")
KEEP_BYTES = 16 << 20
UNROLL = 7

soften = 1.0
screen = 0.0625
near_scale = 0.05
spread_norm = 0.17958712212516656
mobility = 0.2
time_step = 0.5
relaxation = 0.35
ewald_split = 0.5

F32 = jnp.float32
BF16 = jnp.bfloat16
NT = (((1,), (1,)), ((), ()))
NN = (((1,), (0,)), ((), ()))


def real_basis():
    cells = np.arange(GRID)
    angle = 2.0 * np.pi * (np.outer(cells, np.arange(HALF)) % GRID) / GRID
    sine = np.sin(angle)
    sine[:, 0] = np.cos(np.pi * cells)
    return np.concatenate([np.cos(angle), sine], axis=1)


def z_tables():
    pairs = np.arange(HALF)
    cells = np.arange(GRID + BLOCK)
    angle = 2.0 * np.pi * (np.outer(pairs, cells) % GRID) / GRID
    cosine, sine = np.cos(angle), np.sin(angle)
    nyquist = np.cos(np.pi * cells)
    xy = np.stack([cosine, sine], axis=1)
    zz = np.stack([-sine, cosine], axis=1)
    xy[0, 0] = zz[0, 0] = 1.0
    xy[0, 1] = zz[0, 1] = nyquist
    return xy, zz


def split_np(table):
    high = np.asarray(table, dtype=BF16)
    low = np.asarray(table - high.astype(np.float64), dtype=BF16)
    return high, low


def split2(value):
    high = value.astype(BF16)
    return high, (value - high.astype(F32)).astype(BF16)


def dot(a, b, dims=NN):
    return lax.dot_general(a, b, dims, preferred_element_type=F32)


def dot3(a, b):
    count = a[0].shape[0]
    both = dot(jnp.concatenate([a[0], a[1]], axis=0), b[0])
    return both[:count] + (both[count:] + dot(a[0], b[1]))


def split_rows(value):
    high = value.astype(BF16).astype(F32)
    rest = value - high
    middle = rest.astype(BF16).astype(F32)
    return jnp.concatenate([high, middle, rest - middle], axis=0).astype(BF16)


def near_tile(shifted, offt_ref, push_ref, nodes):
    def part(j, sums):
        at = pl.ds(pl.multiple_of(j * 8, 8), 8)
        own = offt_ref[at, :]
        push = push_ref[at, :]
        sep = [shifted[d] - own[:, d : d + 1] for d in range(3)]
        pushes = [push[:, d : d + 1] for d in range(3)]
        square = sep[0] * sep[0] + sep[1] * sep[1] + sep[2] * sep[2]
        root = lax.rsqrt(square + soften)
        weight = jnp.exp(-square * screen) * (root * root * root)
        projected = sep[0] * pushes[0] + sep[1] * pushes[1] + sep[2] * pushes[2]
        diagonal = (square + 2.0 * soften) * weight
        leaning = projected * weight
        return tuple(sums[d] + (diagonal * pushes[d] + sep[d] * leaning) for d in range(3))

    zero = jnp.zeros((8, nodes), F32)
    sums = lax.fori_loop(0, nodes // 8, part, (zero, zero, zero), unroll=True)
    return near_scale * jnp.concatenate(
        [jnp.sum(v, axis=0, keepdims=True) for v in sums], axis=0
    )


def field_lane(q, own_contacts):
    per_tile = 128 // own_contacts
    ahead = per_tile // 2
    return 64 + q * own_contacts if q < ahead else 128 + (q - ahead) * own_contacts


def pack_kernel(
    centers, anchors, occupied, near_list, tractions, pairs, gap, angles, out_ref, fields
):
    side = tractions.shape[0]
    per_device = side * side
    own_contacts = pairs.shape[1]
    fields[...] = jnp.zeros(fields.shape, F32)
    fields[0:2, :own_contacts] = pairs[...].astype(F32)
    fields[2:3, :own_contacts] = gap[...]
    fields[3:5, :own_contacts] = angles[...]
    lane = lax.broadcasted_iota(jnp.int32, (1, 128), 1)
    row = jnp.zeros((1, 128), F32)
    pieces = []
    for k in range(per_device):
        a, b = divmod(k, side)
        values = [centers[a, b, d] for d in range(3)]
        values += [anchors[a, b, d].astype(F32) for d in range(3)]
        values.append(occupied[a, b].astype(F32))
        values += [near_list[a, b, j].astype(F32) for j in range(near_list.shape[2])]
        for j, value in enumerate(values):
            row = jnp.where(lane == k * 16 + j, value, row)
        pieces += [tractions[a, d : d + 1, b] for d in range(3)]
    tail = [row, jnp.zeros((1, 128), F32)]
    for q in range(5):
        which, shift = divmod(field_lane(q, own_contacts), 128)
        field = fields[q : q + 1, :]
        tail[which] = tail[which] + (pltpu.roll(field, shift, 1) if shift else field)
    message = jnp.concatenate(pieces + tail, axis=1)

    def send(holder, c):
        out_ref[holder] = message
        return c

    lax.fori_loop(0, out_ref.shape[0], send, 0, unroll=8)


def self_kernel(occupied, tractions, off_ref, offt_ref, out_ref, push):
    side = tractions.shape[0]
    nodes = tractions.shape[3]
    out_ref[...] = jnp.zeros(out_ref.shape, F32)

    for k in range(side * side):
        a, b = divmod(k, side)

        @pl.when(occupied[a, b] > 0)
        def _(a=a, b=b, k=k):
            push[...] = jnp.concatenate(
                [tractions[a, :, b], jnp.zeros((5, nodes), F32)], axis=0
            ).T
            shifted = [off_ref[d : d + 1, :] for d in range(3)]
            out_ref[k] = near_tile(shifted, offt_ref, push, nodes)


def far_kernel(pairs, slots, devices, keep):
    rows_c = 2 * pairs
    rows = 3 * rows_c

    def kernel(
        misc,
        ranks,
        g_ref,
        off_ref,
        offt_ref,
        self_ref,
        tab_in,
        ryh,
        ryl,
        ryth,
        rytl,
        rxh,
        rxl,
        rxth,
        rxtl,
        out_ref,
        listed,
        acc,
        wy,
        sbuf,
        hyd,
        ft,
        tab_ref,
        kept_wx,
        kept_table,
        kept_wy,
    ):
        z_group, x_group, device = ranks[0], ranks[1], ranks[2]
        nodes = off_ref.shape[1]
        per_device = slots // devices

        def scalar(s, j):
            return misc[s // per_device, s % per_device * 16 + j]

        def lines(s, d):
            return pl.ds(pl.multiple_of((s % per_device * 3 + d) * nodes, nodes), nodes)

        def force_row(s, d):
            return g_ref[s // per_device, :, lines(s, d)]

        half_x = rxh.shape[1] // 2

        out_ref[...] = jnp.zeros(out_ref.shape, F32)
        strip = acc.shape[1] // BLOCK
        scanned = slots // BLOCK

        def start(i, n):
            at = pl.ds(pl.multiple_of(i * strip, 8), strip)
            for tile in range(4):
                acc[tile, at, :] = jnp.zeros((strip, HALF), F32)
            for j in range(scanned):
                s = i * scanned + j
                listed[n] = s
                n = n + (scalar(s, 6) > 0.5).astype(jnp.int32)
            return n

        count = lax.fori_loop(0, BLOCK, start, jnp.int32(0))
        for z in range(GRID + BLOCK):
            tab_ref[z] = jnp.broadcast_to(tab_in[:, z : z + 1], tab_ref.shape[1:])
        wy[...] = jnp.zeros(wy.shape, BF16)
        hyd[...] = jnp.zeros(hyd.shape, F32)

        steps = lax.broadcasted_iota(jnp.int32, (BLOCK, nodes), 0)

        def positions(s):
            anchor = [scalar(s, 3 + d).astype(jnp.int32) for d in range(3)]
            local_y = anchor[1] % HALF
            late = (local_y > HALF - BLOCK).astype(jnp.int32)
            local_y = local_y - late * (HALF // 2)
            tile = 2 * (anchor[1] // HALF) + late
            where = pl.ds(pl.multiple_of(anchor[0] * rows, rows), BLOCK * rows)
            return anchor, where, tile, local_y

        def factors(s, anchor, local_y):
            pos = [off_ref[d : d + 1, :] + scalar(s, d) for d in range(3)]

            def weights(d, shift):
                away = pos[d] - (anchor[d] + steps + shift).astype(F32)
                return jnp.exp(-away * away)

            wx = weights(0, 0)
            wz = weights(2, 0)
            inner = local_y % BLOCK
            parts = []
            for i in range(2):
                t = steps + (i * BLOCK - inner)
                parts.append(
                    split2(
                        jnp.where((t >= 0) & (t < BLOCK), weights(1, i * BLOCK - inner), 0.0)
                    )
                )
            table = jnp.zeros((2 * rows_c, nodes), F32)
            for t in range(BLOCK):
                phase = tab_ref[anchor[2] + t]
                phase = jnp.concatenate([phase] * (nodes // 128), axis=1)
                table = table + phase * wz[t : t + 1, :]
            return wx, table, parts

        def lay(buffer, local_y, parts, doubled):
            first = local_y // BLOCK
            places = []
            for i, (high, low) in enumerate(parts):
                near_row = ((first + i) % 8) * BLOCK
                if doubled:
                    writes = (
                        (near_row, high),
                        (((first + i + 4) % 8) * BLOCK, low),
                        (near_row + HALF, high),
                    )
                else:
                    writes = ((near_row, high), (near_row + HALF, low))
                for row, part in writes:
                    row = pl.multiple_of(row, BLOCK)
                    wy[buffer, pl.ds(row, BLOCK), :] = part
                    places.append(row)
            return places

        def prepare(at, s, buffer, doubled):
            anchor, where, tile, local_y = positions(s)
            if doubled and keep:
                wx, table = kept_wx[at], kept_table[at]
                parts = [(kept_wy[at, i], kept_wy[at, 2 + i]) for i in range(2)]
            else:
                wx, table, parts = factors(s, anchor, local_y)
                if keep:
                    kept_wx[at] = wx
                    kept_table[at] = table
                    for i in range(2):
                        kept_wy[at, i] = parts[i][0]
                        kept_wy[at, 2 + i] = parts[i][1]
            places = lay(buffer, local_y, parts, doubled)
            zed = jnp.concatenate([table[:rows_c], table], axis=0)
            return where, tile, local_y, wx, zed, places

        def forget(buffer, places):
            for row in places:
                wy[buffer, pl.ds(row, BLOCK), :] = jnp.zeros((BLOCK, nodes), BF16)

        def members(i):
            found = []
            for u in range(UNROLL):
                at = i * UNROLL + u
                there = (at < count).astype(F32)
                found.append((listed[jnp.minimum(at, count - 1)], there))
            return found

        trips = (count + (UNROLL - 1)) // UNROLL

        def spread(i, c):
            group = members(i)
            ready = [prepare(i * UNROLL + u, s, u, False) for u, (s, _) in enumerate(group)]
            patches = []
            for u, (s, there) in enumerate(group):
                _, _, _, wx, zed, _ = ready[u]
                force = jnp.concatenate(
                    [
                        jnp.broadcast_to(force_row(s, d) * there, (rows_c, nodes))
                        for d in range(3)
                    ],
                    axis=0,
                )
                loaded = force * zed
                left = jnp.concatenate([loaded * wx[a : a + 1, :] for a in range(BLOCK)], axis=0)
                high, low = split2(left)
                upper = dot(high, wy[u], NT)
                lower = dot(low, wy[u], NT)
                patches.append(upper[:, :HALF] + (upper[:, HALF:] + lower[:, :HALF]))
            for u, patch in enumerate(patches):
                where, tile, _, _, _, places = ready[u]
                acc[tile, where, :] = acc[tile, where, :] + patch
                forget(u, places)
            return c

        lax.fori_loop(0, trips, spread, 0)
        acc[:, : BLOCK * rows, :] = acc[:, : BLOCK * rows, :] + acc[:, GRID * rows :, :]
        low_half = lax.broadcasted_iota(jnp.int32, (GRID, HALF), 1) < HALF // 2

        def turned(value):
            return pltpu.roll(value, HALF // 2, 1)

        damping = (ewald_split * np.pi / GRID) ** 2
        constant = spread_norm**2 * GRID * GRID / (4.0 * np.pi**2) / GRID**3
        k_lane = lax.broadcasted_iota(jnp.int32, (8, HALF), 1).astype(F32)
        y_edge = jnp.where(k_lane == 0.0, float(HALF), 0.0)
        ky = ((k_lane, jnp.zeros_like(k_lane)), (k_lane, y_edge))
        y_factor = jnp.where(k_lane == 0.0, 1.0, 2.0)

        def wave_slot(r, c):
            pair = z_group * pairs + r // 2
            is_first = pair == 0
            kz = jnp.where(is_first, 0, pair).astype(F32)
            nz = jnp.where(is_first & (r % 2 == 1), HALF, 0).astype(F32)
            kz2 = kz * kz + nz * nz
            z_factor = jnp.where(is_first, 1.0, 2.0) * constant
            slabs = []
            for comp in range(3):
                line = pl.ds(comp * rows_c + r, GRID, stride=rows)
                odd0, odd1 = turned(acc[1, line, :]), turned(acc[3, line, :])
                data = jnp.concatenate(
                    [
                        acc[0, line, :] + jnp.where(low_half, odd1, odd0),
                        acc[2, line, :] + jnp.where(low_half, odd0, odd1),
                    ],
                    axis=1,
                )
                slabs.append(data)
            for comp in range(3):
                mid = dot3(split2(slabs[comp]), (ryh[...], ryl[...]))
                sbuf[comp] = dot3((rxth[...], rxtl[...]), split2(mid))

            def filtered(i, c2):
                row = pl.multiple_of(i * 8, 8)
                k_row = (
                    lax.broadcasted_iota(jnp.int32, (8, HALF), 0) + (row + x_group * half_x)
                ).astype(F32)
                x_edge = jnp.where(k_row == 0.0, float(HALF), 0.0)
                kxn = (None, x_edge)
                scale = jnp.where(k_row == 0.0, 1.0, 2.0) * y_factor * z_factor
                spectrum = [
                    [
                        [
                            sbuf[comp, pl.ds(row + hx * half_x, 8), hy * HALF : (hy + 1) * HALF]
                            for hy in range(2)
                        ]
                        for hx in range(2)
                    ]
                    for comp in range(3)
                ]
                sx, sy, sz = spectrum
                total = [[None, None], [None, None]]
                for hx in range(2):
                    for hy in range(2):
                        jx = sx[0][hy] if hx else -sx[1][hy]
                        jy = sy[hx][0] if hy else -sy[hx][1]
                        total[hx][hy] = k_row * jx + k_lane * jy + kz * sz[hx][hy]
                for hx in range(2):
                    for hy in range(2):
                        square = k_row * k_row + k_lane * k_lane + kz2
                        edge = nz * sz[hx][hy]
                        if hx:
                            square = square + x_edge * x_edge
                            edge = edge + x_edge * sx[hx][hy]
                        if hy:
                            square = square + y_edge * y_edge
                            edge = edge + y_edge * sy[hx][hy]
                        inverse = 1.0 / jnp.maximum(square, 1.0)
                        factor = jnp.where(
                            square > 0.5, jnp.exp(-damping * square) * inverse, 0.0
                        ) * scale
                        tx = total[0][hy] if hx else -total[1][hy]
                        ty = total[hx][0] if hy else -total[hx][1]
                        along_x = k_row * tx
                        along_y = k_lane * ty
                        if hx:
                            along_x = along_x - x_edge * edge
                        if hy:
                            along_y = along_y - y_edge * edge
                        along_z = kz * total[hx][hy] + nz * edge
                        lanes = slice(hy * HALF, (hy + 1) * HALF)
                        at = pl.ds(row + hx * half_x, 8)
                        sbuf[0, at, lanes] = factor * (sx[hx][hy] + along_x * inverse)
                        sbuf[1, at, lanes] = factor * (sy[hx][hy] + along_y * inverse)
                        sbuf[2, at, lanes] = factor * (sz[hx][hy] - along_z * inverse)
                return c2

            lax.fori_loop(0, half_x // 8, filtered, 0, unroll=True)
            for comp in range(3):
                line = pl.ds(comp * rows_c + r, GRID, stride=rows)
                mid = dot3((rxh[...], rxl[...]), split2(sbuf[comp]))
                data = dot3(split2(mid), (ryth[...], rytl[...]))
                even0, even1 = data[:, :HALF], data[:, HALF:]
                odd0, odd1 = turned(even0), turned(even1)
                acc[0, line, :] = even0
                acc[1, line, :] = jnp.where(low_half, odd0, odd1)
                acc[2, line, :] = even1
                acc[3, line, :] = jnp.where(low_half, odd1, odd0)
            return c

        lax.fori_loop(0, rows_c, wave_slot, 0, unroll=4)
        acc[:, GRID * rows :, :] = acc[:, : BLOCK * rows, :]
        slot_lane = lax.broadcasted_iota(jnp.int32, (8, hyd.shape[1]), 1)

        def add_out(s, values):
            padded = jnp.concatenate([values, jnp.zeros((5, nodes), F32)], axis=0)
            for d in range(3):
                at = lines(s, d)
                holder = s // per_device
                out_ref[holder, :, at] = out_ref[holder, :, at] + values[d : d + 1]
            mean = jnp.sum(padded, axis=1, keepdims=True) * (1.0 / nodes)
            hyd[...] = hyd[...] + jnp.where(slot_lane == s, mean, 0.0)

        lanes = lax.broadcasted_iota(jnp.int32, (BLOCK * rows, HALF), 1)

        def sample(i, c):
            group = members(i)
            ready = [prepare(i * UNROLL + u, s, u, True) for u, (s, _) in enumerate(group)]
            results = []
            for u in range(UNROLL):
                where, tile, local_y, wx, zed, _ = ready[u]
                block = acc[tile, where, :]
                chosen = ((lanes - local_y) & (HALF - 1)) < HALF // 2
                high, low = split2(jnp.where(chosen, block, turned(block)))
                seen = dot(jnp.concatenate([high, low], axis=1), wy[u])
                total = seen[:rows] * wx[0:1, :]
                for a in range(1, BLOCK):
                    total = total + seen[a * rows : (a + 1) * rows] * wx[a : a + 1, :]
                total = total * zed
                results.append(
                    jnp.concatenate(
                        [
                            jnp.sum(total[d * rows_c : (d + 1) * rows_c], axis=0, keepdims=True)
                            for d in range(3)
                        ],
                        axis=0,
                    )
                )
            for u, (s, there) in enumerate(group):
                add_out(s, results[u] * there)
                forget(u, ready[u][5])
            return c

        lax.fori_loop(0, trips, sample, 0)

        def near_task(i, c):
            task = device + i * devices
            s = listed[task // 2]
            source = scalar(s, 7 + task % 2).astype(jnp.int32)
            ft[...] = jnp.concatenate(
                [force_row(source, d) for d in range(3)] + [jnp.zeros((5, nodes), F32)], axis=0
            ).T
            shifted = []
            for d in range(3):
                gap = jnp.full((1, nodes), scalar(s, d) - scalar(source, d), F32)
                gap = gap - GRID * jnp.floor(gap / GRID + 0.5)
                shifted.append(gap + off_ref[d : d + 1, :])
            add_out(s, near_tile(shifted, offt_ref, ft, nodes))
            return c

        tasks = (2 * count - device + (devices - 1)) // devices
        lax.fori_loop(0, tasks, near_task, 0)
        for k in range(per_device):
            add_out(device * per_device + k, self_ref[k])

        def publish(holder, c):
            for d in range(3):
                first = 3 * per_device * nodes + d * slots
                out_ref[holder, :, first : first + slots] = hyd[d : d + 1, :]
            return c

        lax.fori_loop(0, devices, publish, 0)

    return kernel


def prepare_kernel(slots, devices, own_contacts):
    per_tile = 128 // own_contacts
    tiles = devices // per_tile

    def kernel(g_ref, incidence, rows_ref):
        contacts = incidence.shape[1]
        lane = lax.broadcasted_iota(jnp.int32, (tiles, 128), 1)

        def field(q):
            which, shift = divmod(field_lane(q, own_contacts), 128)
            low = g_ref.shape[2] - 256 + 128 * which
            total = jnp.zeros((tiles, 128), F32)
            for j in range(per_tile):
                part = jnp.concatenate(
                    [
                        g_ref[t * per_tile + j, :, low : low + 128]
                        for t in range(tiles)
                    ],
                    axis=0,
                )
                turn = (j * own_contacts - shift) % 128
                if turn:
                    part = pltpu.roll(part, turn, 1)
                total = jnp.where(lane // own_contacts == j, part, total)
            return jnp.concatenate([total[t : t + 1] for t in range(tiles)], axis=1)

        first = field(0).astype(jnp.int32)
        second = field(1).astype(jnp.int32)
        polar = field(3)
        azimuth = field(4)
        rows_ref[...] = jnp.concatenate(
            [
                jnp.sin(polar) * jnp.cos(azimuth),
                jnp.sin(polar) * jnp.sin(azimuth),
                jnp.cos(polar),
                field(2),
                jnp.zeros((4, contacts), F32),
            ],
            axis=0,
        )

        def build(i, c):
            row = pl.multiple_of(i * 16, 16)
            ids = lax.broadcasted_iota(jnp.int32, (16, contacts), 0) + row
            value = jnp.where(first == ids, 1.0, 0.0) - jnp.where(second == ids, 1.0, 0.0)
            incidence[pl.ds(row, 16), :] = value.astype(BF16)
            return c

        lax.fori_loop(0, slots // 16, build, 0)

    return kernel


def contact_kernel(slots, devices, own_contacts):
    per_device = slots // devices

    def kernel(
        ranks,
        recv_ref,
        incidence,
        rows_ref,
        centers,
        velocity_ref,
        force_ref,
        moved_ref,
        wide_force,
        wide_drift,
    ):
        contacts = rows_ref.shape[1]
        side = centers.shape[0]
        device = ranks[2]

        def gather(holder, total):
            return total + recv_ref[holder]

        summed = lax.fori_loop(1, devices, gather, recv_ref[0], unroll=8)
        nodes = velocity_ref.shape[3]
        for a in range(side):
            for b in range(side):
                for d in range(3):
                    first = ((a * side + b) * 3 + d) * nodes
                    velocity_ref[a, d : d + 1, b] = summed[:, first : first + nodes]
        means = 3 * per_device * nodes
        hydro = jnp.concatenate(
            [summed[:, means + d * slots : means + (d + 1) * slots] for d in range(3)]
            + [jnp.zeros((5, slots), F32)],
            axis=0,
        )
        gap = rows_ref[3:4, :]
        kind = lax.broadcasted_iota(jnp.int32, (8, contacts), 0)
        normal = jnp.where(kind < 3, rows_ref[...], 0.0)

        def totals(magnitude):
            spread = dot(split_rows(magnitude * normal), incidence[...], NT)
            return spread[0:8] + (spread[8:16] + spread[16:24])

        def sweep(i, magnitude):
            velocity = hydro + mobility * totals(magnitude)
            seen = dot(split_rows(velocity), incidence[...])
            relative = jnp.sum(
                normal * (seen[0:8] + (seen[8:16] + seen[16:24])), axis=0, keepdims=True
            )
            return jnp.maximum(
                magnitude
                - relaxation * (gap + time_step * relative) / (2.0 * time_step * mobility),
                0.0,
            )

        magnitude = lax.fori_loop(0, SWEEPS, sweep, jnp.zeros((1, contacts), F32))
        drift = time_step * (hydro + mobility * totals(magnitude))
        wide_force[...] = jnp.broadcast_to(magnitude, wide_force.shape)
        wide_drift[...] = drift
        place = device * own_contacts
        at = pl.ds(pl.multiple_of(place // 128 * 128, 128), 128)
        turned = pltpu.roll(wide_force[:, at], (128 - place % 128) % 128, 1)
        force_ref[...] = turned[0:1, :own_contacts]
        place = device * per_device
        at = pl.ds(pl.multiple_of(place // 128 * 128, 128), 128)
        own = pltpu.roll(wide_drift[:, at], (128 - place % 128) % 128, 1).T
        for a in range(side):
            moved_ref[a] = centers[a] + own[a * side : (a + 1) * side, 0:3]

    return kernel


def vmem_of(held):
    return pltpu.CompilerParams(vmem_limit_bytes=min(60 << 20, 2 * held + (12 << 20)))


def local(
    tractions,
    centers,
    node_offsets,
    occupied,
    anchors,
    near_list,
    contact_pairs,
    contact_gap,
    contact_angles,
):
    side = tractions.shape[0]
    per_device = side * side
    nodes = tractions.shape[3]
    narrow_count = lax.axis_size("narrow")
    devices = lax.axis_size("wide") * narrow_count
    rank = lax.axis_index("wide") * narrow_count + lax.axis_index("narrow")
    slots = devices * per_device
    contacts_own = contact_gap.shape[0]
    contacts = contacts_own * devices
    pairs = max(MIN_PAIRS, HALF // devices)
    z_groups = HALF // pairs
    x_groups = max(1, devices // z_groups)
    half_x = HALF // x_groups
    z_group = rank % z_groups
    x_group = rank // z_groups
    rows = 6 * pairs

    vmem = pl.BlockSpec(memory_space=pltpu.VMEM)
    smem = pl.BlockSpec(memory_space=pltpu.SMEM)
    forces = 3 * per_device * nodes
    by_row = tractions.transpose(0, 2, 1, 3)
    packed = pl.pallas_call(
        pack_kernel,
        out_shape=jax.ShapeDtypeStruct((devices, 1, forces + 256), F32),
        in_specs=[smem] * 4 + [vmem] * 4,
        out_specs=vmem,
        scratch_shapes=[pltpu.VMEM((8, 128), F32)],
        name="pack",
    )(
        centers,
        anchors,
        occupied,
        near_list,
        by_row,
        contact_pairs,
        contact_gap[None],
        contact_angles,
    )
    gathered = lax.all_to_all(packed, AXES, split_axis=0, concat_axis=0, tiled=True)
    offsets_t = node_offsets.T
    self_near = pl.pallas_call(
        self_kernel,
        out_shape=jax.ShapeDtypeStruct((per_device, 3, nodes), F32),
        in_specs=[smem] + [vmem] * 3,
        out_specs=vmem,
        scratch_shapes=[pltpu.VMEM((nodes, 8), F32)],
        name="near_self",
    )(occupied, by_row, node_offsets, offsets_t)
    scalars = gathered[:, 0, forces : forces + 16 * per_device]

    xy, zz = z_tables()
    tables = np.concatenate(
        [
            xy.reshape(z_groups, 2 * pairs, GRID + BLOCK),
            zz.reshape(z_groups, 2 * pairs, GRID + BLOCK),
        ],
        axis=1,
    )
    table = lax.dynamic_index_in_dim(jnp.asarray(tables, F32), z_group, 0, keepdims=False)
    basis = real_basis()
    turned = np.ascontiguousarray(basis.T)
    ry = [jnp.asarray(v) for v in split_np(basis)]
    ryt = [jnp.asarray(v) for v in split_np(turned)]
    if x_groups == 1:
        rx, rxt = ry, ryt
    else:
        rxt = [
            lax.dynamic_index_in_dim(
                v.reshape(2, x_groups, half_x, GRID), x_group, 1, keepdims=False
            ).reshape(2 * half_x, GRID)
            for v in ryt
        ]
        rx = [v.T for v in rxt]

    keep = slots * nodes * BLOCK * 16 <= KEEP_BYTES
    kept = slots + UNROLL if keep else 1
    ranks = jnp.stack([z_group, x_group, rank]).astype(jnp.int32)
    partial = pl.pallas_call(
        far_kernel(pairs, slots, devices, keep),
        out_shape=jax.ShapeDtypeStruct((devices, 1, forces + 3 * slots), F32),
        in_specs=[smem, smem] + [vmem] * 13,
        out_specs=vmem,
        scratch_shapes=[
            pltpu.SMEM((slots + 1,), jnp.int32),
            pltpu.VMEM((4, (GRID + BLOCK) * rows, HALF), F32),
            pltpu.VMEM((UNROLL, GRID, nodes), BF16),
            pltpu.VMEM((3, 2 * half_x, GRID), F32),
            pltpu.VMEM((8, slots), F32),
            pltpu.VMEM((nodes, 8), F32),
            pltpu.VMEM((GRID + BLOCK, 4 * pairs, 128), F32),
            pltpu.VMEM((kept, BLOCK, nodes), F32),
            pltpu.VMEM((kept, 4 * pairs, nodes), F32),
            pltpu.VMEM((kept, 4, BLOCK, nodes), BF16),
        ],
        compiler_params=vmem_of(8 * slots * nodes * 4 + 4 * (GRID + BLOCK) * 6 * pairs * HALF * 4),
        name="far_near",
    )(
        scalars,
        ranks,
        gathered,
        node_offsets,
        offsets_t,
        self_near,
        table,
        *ry,
        *ryt,
        *rx,
        *rxt,
    )
    received = lax.all_to_all(partial, AXES, split_axis=0, concat_axis=0, tiled=True)
    incidence, contact_rows = pl.pallas_call(
        prepare_kernel(slots, devices, contacts_own),
        out_shape=(
            jax.ShapeDtypeStruct((slots, contacts), BF16),
            jax.ShapeDtypeStruct((8, contacts), F32),
        ),
        in_specs=[vmem],
        out_specs=(vmem, vmem),
        compiler_params=vmem_of(4 * slots * nodes * 4 + slots * contacts * 2),
        name="contact_rows",
    )(gathered)
    velocity, force, moved = pl.pallas_call(
        contact_kernel(slots, devices, contacts_own),
        out_shape=(
            jax.ShapeDtypeStruct((side, 3, side, nodes), F32),
            jax.ShapeDtypeStruct((1, contacts_own), F32),
            jax.ShapeDtypeStruct((side, side, 3), F32),
        ),
        in_specs=[smem, vmem, vmem, vmem, vmem],
        out_specs=(vmem, vmem, vmem),
        scratch_shapes=[
            pltpu.VMEM((8, contacts), F32),
            pltpu.VMEM((8, slots), F32),
        ],
        compiler_params=vmem_of(8 * slots * nodes * 4 + slots * contacts * 2),
        name="contacts",
    )(ranks, received, incidence, contact_rows, centers)
    return (velocity.transpose(0, 2, 1, 3), force[0], moved)


def solution(mesh):
    placed = (
        P("wide", "narrow", None, None),
        P("wide", "narrow", None),
        P(),
        P("wide", "narrow"),
        P("wide", "narrow", None),
        P("wide", "narrow", None),
        P(None, ("wide", "narrow")),
        P(("wide", "narrow")),
        P(None, ("wide", "narrow")),
    )
    return jax.shard_map(
        local,
        mesh=mesh,
        in_specs=placed,
        out_specs=(
            P("wide", "narrow", None, None),
            P(("wide", "narrow")),
            P("wide", "narrow", None),
        ),
        check_vma=False,
    )
```

```python
import jax
import jax.numpy as jnp
import numpy as np
from jax import lax
from jax.experimental import pallas as pl
from jax.experimental.pallas import tpu as pltpu
from jax.sharding import PartitionSpec as P

GRID = 256
HALF = GRID // 2
BLOCK = 16
SWEEPS = 6
MIN_PAIRS = 4
AXES = ("wide", "narrow")
KEEP_BYTES = 16 << 20
UNROLL = 7

soften = 1.0
screen = 0.0625
near_scale = 0.05
spread_norm = 0.17958712212516656
mobility = 0.2
time_step = 0.5
relaxation = 0.35
ewald_split = 0.5

F32 = jnp.float32
BF16 = jnp.bfloat16
NT = (((1,), (1,)), ((), ()))
NN = (((1,), (0,)), ((), ()))


def real_basis():
    cells = np.arange(GRID)
    angle = 2.0 * np.pi * (np.outer(cells, np.arange(HALF)) % GRID) / GRID
    sine = np.sin(angle)
    sine[:, 0] = np.cos(np.pi * cells)
    return np.concatenate([np.cos(angle), sine], axis=1)


def z_tables():
    pairs = np.arange(HALF)
    cells = np.arange(GRID + BLOCK)
    angle = 2.0 * np.pi * (np.outer(pairs, cells) % GRID) / GRID
    cosine, sine = np.cos(angle), np.sin(angle)
    nyquist = np.cos(np.pi * cells)
    xy = np.stack([cosine, sine], axis=1)
    zz = np.stack([-sine, cosine], axis=1)
    xy[0, 0] = zz[0, 0] = 1.0
    xy[0, 1] = zz[0, 1] = nyquist
    return xy, zz


def split_np(table):
    high = np.asarray(table, dtype=BF16)
    low = np.asarray(table - high.astype(np.float64), dtype=BF16)
    return high, low


def split2(value):
    high = value.astype(BF16)
    return high, (value - high.astype(F32)).astype(BF16)


def dot(a, b, dims=NN):
    return lax.dot_general(a, b, dims, preferred_element_type=F32)


def dot3(a, b):
    count = a[0].shape[0]
    both = dot(jnp.concatenate([a[0], a[1]], axis=0), b[0])
    return both[:count] + (both[count:] + dot(a[0], b[1]))


def split_rows(value):
    high = value.astype(BF16).astype(F32)
    rest = value - high
    middle = rest.astype(BF16).astype(F32)
    return jnp.concatenate([high, middle, rest - middle], axis=0).astype(BF16)


def near_tile(shifted, offt_ref, push_ref, nodes):
    def part(j, sums):
        at = pl.ds(pl.multiple_of(j * 8, 8), 8)
        own = offt_ref[at, :]
        push = push_ref[at, :]
        sep = [shifted[d] - own[:, d : d + 1] for d in range(3)]
        pushes = [push[:, d : d + 1] for d in range(3)]
        square = sep[0] * sep[0] + sep[1] * sep[1] + sep[2] * sep[2]
        root = lax.rsqrt(square + soften)
        weight = jnp.exp(-square * screen) * (root * root * root)
        projected = sep[0] * pushes[0] + sep[1] * pushes[1] + sep[2] * pushes[2]
        diagonal = (square + 2.0 * soften) * weight
        leaning = projected * weight
        return tuple(sums[d] + (diagonal * pushes[d] + sep[d] * leaning) for d in range(3))

    zero = jnp.zeros((8, nodes), F32)
    sums = lax.fori_loop(0, nodes // 8, part, (zero, zero, zero), unroll=True)
    return near_scale * jnp.concatenate(
        [jnp.sum(v, axis=0, keepdims=True) for v in sums], axis=0
    )


def field_lane(q, own_contacts):
    per_tile = 128 // own_contacts
    ahead = per_tile // 2
    return 64 + q * own_contacts if q < ahead else 128 + (q - ahead) * own_contacts


def pack_kernel(
    centers, anchors, occupied, near_list, tractions, pairs, gap, angles, out_ref, fields
):
    side = tractions.shape[0]
    per_device = side * side
    own_contacts = pairs.shape[1]
    fields[...] = jnp.zeros(fields.shape, F32)
    fields[0:2, :own_contacts] = pairs[...].astype(F32)
    fields[2:3, :own_contacts] = gap[...]
    fields[3:5, :own_contacts] = angles[...]
    lane = lax.broadcasted_iota(jnp.int32, (1, 128), 1)
    row = jnp.zeros((1, 128), F32)
    pieces = []
    for k in range(per_device):
        a, b = divmod(k, side)
        values = [centers[a, b, d] for d in range(3)]
        values += [anchors[a, b, d].astype(F32) for d in range(3)]
        values.append(occupied[a, b].astype(F32))
        values += [near_list[a, b, j].astype(F32) for j in range(near_list.shape[2])]
        for j, value in enumerate(values):
            row = jnp.where(lane == k * 16 + j, value, row)
        pieces += [tractions[a, d : d + 1, b] for d in range(3)]
    tail = [row, jnp.zeros((1, 128), F32)]
    for q in range(5):
        which, shift = divmod(field_lane(q, own_contacts), 128)
        field = fields[q : q + 1, :]
        tail[which] = tail[which] + (pltpu.roll(field, shift, 1) if shift else field)
    message = jnp.concatenate(pieces + tail, axis=1)

    def send(holder, c):
        out_ref[holder] = message
        return c

    lax.fori_loop(0, out_ref.shape[0], send, 0, unroll=8)


def self_kernel(occupied, tractions, off_ref, offt_ref, out_ref, push):
    side = tractions.shape[0]
    nodes = tractions.shape[3]
    out_ref[...] = jnp.zeros(out_ref.shape, F32)

    for k in range(side * side):
        a, b = divmod(k, side)

        @pl.when(occupied[a, b] > 0)
        def _(a=a, b=b, k=k):
            push[...] = jnp.concatenate(
                [tractions[a, :, b], jnp.zeros((5, nodes), F32)], axis=0
            ).T
            shifted = [off_ref[d : d + 1, :] for d in range(3)]
            out_ref[k] = near_tile(shifted, offt_ref, push, nodes)


def far_kernel(pairs, slots, devices, keep):
    rows_c = 2 * pairs
    rows = 3 * rows_c

    def kernel(
        misc,
        ranks,
        g_ref,
        off_ref,
        offt_ref,
        self_ref,
        tab_in,
        ryh,
        ryl,
        ryth,
        rytl,
        rxh,
        rxl,
        rxth,
        rxtl,
        out_ref,
        listed,
        acc,
        wy,
        sbuf,
        hyd,
        ft,
        tab_ref,
        kept_wx,
        kept_table,
        kept_wy,
    ):
        z_group, x_group, device = ranks[0], ranks[1], ranks[2]
        nodes = off_ref.shape[1]
        per_device = slots // devices

        def scalar(s, j):
            return misc[s // per_device, s % per_device * 16 + j]

        def lines(s, d):
            return pl.ds(pl.multiple_of((s % per_device * 3 + d) * nodes, nodes), nodes)

        def force_row(s, d):
            return g_ref[s // per_device, :, lines(s, d)]

        half_x = rxh.shape[1] // 2

        out_ref[...] = jnp.zeros(out_ref.shape, F32)
        strip = acc.shape[1] // BLOCK
        scanned = slots // BLOCK

        def start(i, n):
            at = pl.ds(pl.multiple_of(i * strip, 8), strip)
            for tile in range(4):
                acc[tile, at, :] = jnp.zeros((strip, HALF), F32)
            for j in range(scanned):
                s = i * scanned + j
                listed[n] = s
                n = n + (scalar(s, 6) > 0.5).astype(jnp.int32)
            return n

        count = lax.fori_loop(0, BLOCK, start, jnp.int32(0))
        for z in range(GRID + BLOCK):
            tab_ref[z] = jnp.broadcast_to(tab_in[:, z : z + 1], tab_ref.shape[1:])
        wy[...] = jnp.zeros(wy.shape, BF16)
        hyd[...] = jnp.zeros(hyd.shape, F32)

        steps = lax.broadcasted_iota(jnp.int32, (BLOCK, nodes), 0)

        def positions(s):
            anchor = [scalar(s, 3 + d).astype(jnp.int32) for d in range(3)]
            local_y = anchor[1] % HALF
            late = (local_y > HALF - BLOCK).astype(jnp.int32)
            local_y = local_y - late * (HALF // 2)
            tile = 2 * (anchor[1] // HALF) + late
            where = pl.ds(pl.multiple_of(anchor[0] * rows, rows), BLOCK * rows)
            return anchor, where, tile, local_y

        def factors(s, anchor, local_y):
            pos = [off_ref[d : d + 1, :] + scalar(s, d) for d in range(3)]

            def weights(d, shift):
                away = pos[d] - (anchor[d] + steps + shift).astype(F32)
                return jnp.exp(-away * away)

            wx = weights(0, 0)
            wz = weights(2, 0)
            inner = local_y % BLOCK
            parts = []
            for i in range(2):
                t = steps + (i * BLOCK - inner)
                parts.append(
                    split2(
                        jnp.where((t >= 0) & (t < BLOCK), weights(1, i * BLOCK - inner), 0.0)
                    )
                )
            table = jnp.zeros((2 * rows_c, nodes), F32)
            for t in range(BLOCK):
                phase = tab_ref[anchor[2] + t]
                phase = jnp.concatenate([phase] * (nodes // 128), axis=1)
                table = table + phase * wz[t : t + 1, :]
            return wx, table, parts

        def lay(buffer, local_y, parts, doubled):
            first = local_y // BLOCK
            places = []
            for i, (high, low) in enumerate(parts):
                near_row = ((first + i) % 8) * BLOCK
                if doubled:
                    writes = (
                        (near_row, high),
                        (((first + i + 4) % 8) * BLOCK, low),
                        (near_row + HALF, high),
                    )
                else:
                    writes = ((near_row, high), (near_row + HALF, low))
                for row, part in writes:
                    row = pl.multiple_of(row, BLOCK)
                    wy[buffer, pl.ds(row, BLOCK), :] = part
                    places.append(row)
            return places

        def prepare(at, s, buffer, doubled):
            anchor, where, tile, local_y = positions(s)
            if doubled and keep:
                wx, table = kept_wx[at], kept_table[at]
                parts = [(kept_wy[at, i], kept_wy[at, 2 + i]) for i in range(2)]
            else:
                wx, table, parts = factors(s, anchor, local_y)
                if keep:
                    kept_wx[at] = wx
                    kept_table[at] = table
                    for i in range(2):
                        kept_wy[at, i] = parts[i][0]
                        kept_wy[at, 2 + i] = parts[i][1]
            places = lay(buffer, local_y, parts, doubled)
            zed = jnp.concatenate([table[:rows_c], table], axis=0)
            return where, tile, local_y, wx, zed, places

        def forget(buffer, places):
            for row in places:
                wy[buffer, pl.ds(row, BLOCK), :] = jnp.zeros((BLOCK, nodes), BF16)

        def members(i):
            found = []
            for u in range(UNROLL):
                at = i * UNROLL + u
                there = (at < count).astype(F32)
                found.append((listed[jnp.minimum(at, count - 1)], there))
            return found

        trips = (count + (UNROLL - 1)) // UNROLL

        def spread(i, c):
            group = members(i)
            ready = [prepare(i * UNROLL + u, s, u, False) for u, (s, _) in enumerate(group)]
            patches = []
            for u, (s, there) in enumerate(group):
                _, _, _, wx, zed, _ = ready[u]
                force = jnp.concatenate(
                    [
                        jnp.broadcast_to(force_row(s, d) * there, (rows_c, nodes))
                        for d in range(3)
                    ],
                    axis=0,
                )
                loaded = force * zed
                left = jnp.concatenate([loaded * wx[a : a + 1, :] for a in range(BLOCK)], axis=0)
                high, low = split2(left)
                upper = dot(high, wy[u], NT)
                lower = dot(low, wy[u], NT)
                patches.append(upper[:, :HALF] + (upper[:, HALF:] + lower[:, :HALF]))
            for u, patch in enumerate(patches):
                where, tile, _, _, _, places = ready[u]
                acc[tile, where, :] = acc[tile, where, :] + patch
                forget(u, places)
            return c

        lax.fori_loop(0, trips, spread, 0)
        acc[:, : BLOCK * rows, :] = acc[:, : BLOCK * rows, :] + acc[:, GRID * rows :, :]
        low_half = lax.broadcasted_iota(jnp.int32, (GRID, HALF), 1) < HALF // 2

        def turned(value):
            return pltpu.roll(value, HALF // 2, 1)

        damping = (ewald_split * np.pi / GRID) ** 2
        constant = spread_norm**2 * GRID * GRID / (4.0 * np.pi**2) / GRID**3
        k_lane = lax.broadcasted_iota(jnp.int32, (8, HALF), 1).astype(F32)
        y_edge = jnp.where(k_lane == 0.0, float(HALF), 0.0)
        ky = ((k_lane, jnp.zeros_like(k_lane)), (k_lane, y_edge))
        y_factor = jnp.where(k_lane == 0.0, 1.0, 2.0)

        def wave_slot(r, c):
            pair = z_group * pairs + r // 2
            is_first = pair == 0
            kz = jnp.where(is_first, 0, pair).astype(F32)
            nz = jnp.where(is_first & (r % 2 == 1), HALF, 0).astype(F32)
            kz2 = kz * kz + nz * nz
            z_factor = jnp.where(is_first, 1.0, 2.0) * constant
            slabs = []
            for comp in range(3):
                line = pl.ds(comp * rows_c + r, GRID, stride=rows)
                odd0, odd1 = turned(acc[1, line, :]), turned(acc[3, line, :])
                data = jnp.concatenate(
                    [
                        acc[0, line, :] + jnp.where(low_half, odd1, odd0),
                        acc[2, line, :] + jnp.where(low_half, odd0, odd1),
                    ],
                    axis=1,
                )
                slabs.append(data)
            for comp in range(3):
                mid = dot3(split2(slabs[comp]), (ryh[...], ryl[...]))
                sbuf[comp] = dot3((rxth[...], rxtl[...]), split2(mid))

            def filtered(i, c2):
                row = pl.multiple_of(i * 8, 8)
                k_row = (
                    lax.broadcasted_iota(jnp.int32, (8, HALF), 0) + (row + x_group * half_x)
                ).astype(F32)
                x_edge = jnp.where(k_row == 0.0, float(HALF), 0.0)
                kxn = (None, x_edge)
                scale = jnp.where(k_row == 0.0, 1.0, 2.0) * y_factor * z_factor
                spectrum = [
                    [
                        [
                            sbuf[comp, pl.ds(row + hx * half_x, 8), hy * HALF : (hy + 1) * HALF]
                            for hy in range(2)
                        ]
                        for hx in range(2)
                    ]
                    for comp in range(3)
                ]
                sx, sy, sz = spectrum
                total = [[None, None], [None, None]]
                for hx in range(2):
                    for hy in range(2):
                        jx = sx[0][hy] if hx else -sx[1][hy]
                        jy = sy[hx][0] if hy else -sy[hx][1]
                        total[hx][hy] = k_row * jx + k_lane * jy + kz * sz[hx][hy]
                for hx in range(2):
                    for hy in range(2):
                        square = k_row * k_row + k_lane * k_lane + kz2
                        edge = nz * sz[hx][hy]
                        if hx:
                            square = square + x_edge * x_edge
                            edge = edge + x_edge * sx[hx][hy]
                        if hy:
                            square = square + y_edge * y_edge
                            edge = edge + y_edge * sy[hx][hy]
                        inverse = 1.0 / jnp.maximum(square, 1.0)
                        factor = jnp.where(
                            square > 0.5, jnp.exp(-damping * square) * inverse, 0.0
                        ) * scale
                        tx = total[0][hy] if hx else -total[1][hy]
                        ty = total[hx][0] if hy else -total[hx][1]
                        along_x = k_row * tx
                        along_y = k_lane * ty
                        if hx:
                            along_x = along_x - x_edge * edge
                        if hy:
                            along_y = along_y - y_edge * edge
                        along_z = kz * total[hx][hy] + nz * edge
                        lanes = slice(hy * HALF, (hy + 1) * HALF)
                        at = pl.ds(row + hx * half_x, 8)
                        sbuf[0, at, lanes] = factor * (sx[hx][hy] + along_x * inverse)
                        sbuf[1, at, lanes] = factor * (sy[hx][hy] + along_y * inverse)
                        sbuf[2, at, lanes] = factor * (sz[hx][hy] - along_z * inverse)
                return c2

            lax.fori_loop(0, half_x // 8, filtered, 0, unroll=True)
            for comp in range(3):
                line = pl.ds(comp * rows_c + r, GRID, stride=rows)
                mid = dot3((rxh[...], rxl[...]), split2(sbuf[comp]))
                data = dot3(split2(mid), (ryth[...], rytl[...]))
                even0, even1 = data[:, :HALF], data[:, HALF:]
                odd0, odd1 = turned(even0), turned(even1)
                acc[0, line, :] = even0
                acc[1, line, :] = jnp.where(low_half, odd0, odd1)
                acc[2, line, :] = even1
                acc[3, line, :] = jnp.where(low_half, odd1, odd0)
            return c

        lax.fori_loop(0, rows_c, wave_slot, 0, unroll=8)
        acc[:, GRID * rows :, :] = acc[:, : BLOCK * rows, :]
        slot_lane = lax.broadcasted_iota(jnp.int32, (8, hyd.shape[1]), 1)

        def add_out(s, values):
            padded = jnp.concatenate([values, jnp.zeros((5, nodes), F32)], axis=0)
            for d in range(3):
                at = lines(s, d)
                holder = s // per_device
                out_ref[holder, :, at] = out_ref[holder, :, at] + values[d : d + 1]
            mean = jnp.sum(padded, axis=1, keepdims=True) * (1.0 / nodes)
            hyd[...] = hyd[...] + jnp.where(slot_lane == s, mean, 0.0)

        lanes = lax.broadcasted_iota(jnp.int32, (BLOCK * rows, HALF), 1)

        def sample(i, c):
            group = members(i)
            ready = [prepare(i * UNROLL + u, s, u, True) for u, (s, _) in enumerate(group)]
            results = []
            for u in range(UNROLL):
                where, tile, local_y, wx, zed, _ = ready[u]
                block = acc[tile, where, :]
                chosen = ((lanes - local_y) & (HALF - 1)) < HALF // 2
                high, low = split2(jnp.where(chosen, block, turned(block)))
                seen = dot(jnp.concatenate([high, low], axis=1), wy[u])
                total = seen[:rows] * wx[0:1, :]
                for a in range(1, BLOCK):
                    total = total + seen[a * rows : (a + 1) * rows] * wx[a : a + 1, :]
                total = total * zed
                results.append(
                    jnp.concatenate(
                        [
                            jnp.sum(total[d * rows_c : (d + 1) * rows_c], axis=0, keepdims=True)
                            for d in range(3)
                        ],
                        axis=0,
                    )
                )
            for u, (s, there) in enumerate(group):
                add_out(s, results[u] * there)
                forget(u, ready[u][5])
            return c

        lax.fori_loop(0, trips, sample, 0)

        def near_task(i, c):
            task = device + i * devices
            s = listed[task // 2]
            source = scalar(s, 7 + task % 2).astype(jnp.int32)
            ft[...] = jnp.concatenate(
                [force_row(source, d) for d in range(3)] + [jnp.zeros((5, nodes), F32)], axis=0
            ).T
            shifted = []
            for d in range(3):
                gap = jnp.full((1, nodes), scalar(s, d) - scalar(source, d), F32)
                gap = gap - GRID * jnp.floor(gap / GRID + 0.5)
                shifted.append(gap + off_ref[d : d + 1, :])
            add_out(s, near_tile(shifted, offt_ref, ft, nodes))
            return c

        tasks = (2 * count - device + (devices - 1)) // devices
        lax.fori_loop(0, tasks, near_task, 0)
        for k in range(per_device):
            add_out(device * per_device + k, self_ref[k])

        def publish(holder, c):
            for d in range(3):
                first = 3 * per_device * nodes + d * slots
                out_ref[holder, :, first : first + slots] = hyd[d : d + 1, :]
            return c

        lax.fori_loop(0, devices, publish, 0)

    return kernel


def prepare_kernel(slots, devices, own_contacts):
    per_tile = 128 // own_contacts
    tiles = devices // per_tile

    def kernel(g_ref, incidence, rows_ref):
        contacts = incidence.shape[1]
        lane = lax.broadcasted_iota(jnp.int32, (tiles, 128), 1)

        def field(q):
            which, shift = divmod(field_lane(q, own_contacts), 128)
            low = g_ref.shape[2] - 256 + 128 * which
            total = jnp.zeros((tiles, 128), F32)
            for j in range(per_tile):
                part = jnp.concatenate(
                    [
                        g_ref[t * per_tile + j, :, low : low + 128]
                        for t in range(tiles)
                    ],
                    axis=0,
                )
                turn = (j * own_contacts - shift) % 128
                if turn:
                    part = pltpu.roll(part, turn, 1)
                total = jnp.where(lane // own_contacts == j, part, total)
            return jnp.concatenate([total[t : t + 1] for t in range(tiles)], axis=1)

        first = field(0).astype(jnp.int32)
        second = field(1).astype(jnp.int32)
        polar = field(3)
        azimuth = field(4)
        rows_ref[...] = jnp.concatenate(
            [
                jnp.sin(polar) * jnp.cos(azimuth),
                jnp.sin(polar) * jnp.sin(azimuth),
                jnp.cos(polar),
                field(2),
                jnp.zeros((4, contacts), F32),
            ],
            axis=0,
        )

        def build(i, c):
            row = pl.multiple_of(i * 16, 16)
            ids = lax.broadcasted_iota(jnp.int32, (16, contacts), 0) + row
            value = jnp.where(first == ids, 1.0, 0.0) - jnp.where(second == ids, 1.0, 0.0)
            incidence[pl.ds(row, 16), :] = value.astype(BF16)
            return c

        lax.fori_loop(0, slots // 16, build, 0)

    return kernel


def contact_kernel(slots, devices, own_contacts):
    per_device = slots // devices

    def kernel(
        ranks,
        recv_ref,
        incidence,
        rows_ref,
        centers,
        velocity_ref,
        force_ref,
        moved_ref,
        wide_force,
        wide_drift,
    ):
        contacts = rows_ref.shape[1]
        side = centers.shape[0]
        device = ranks[2]

        def gather(holder, total):
            return total + recv_ref[holder]

        summed = lax.fori_loop(1, devices, gather, recv_ref[0], unroll=8)
        nodes = velocity_ref.shape[3]
        for a in range(side):
            for b in range(side):
                for d in range(3):
                    first = ((a * side + b) * 3 + d) * nodes
                    velocity_ref[a, d : d + 1, b] = summed[:, first : first + nodes]
        means = 3 * per_device * nodes
        hydro = jnp.concatenate(
            [summed[:, means + d * slots : means + (d + 1) * slots] for d in range(3)]
            + [jnp.zeros((5, slots), F32)],
            axis=0,
        )
        gap = rows_ref[3:4, :]
        kind = lax.broadcasted_iota(jnp.int32, (8, contacts), 0)
        normal = jnp.where(kind < 3, rows_ref[...], 0.0)

        def totals(magnitude):
            spread = dot(split_rows(magnitude * normal), incidence[...], NT)
            return spread[0:8] + (spread[8:16] + spread[16:24])

        def sweep(i, magnitude):
            velocity = hydro + mobility * totals(magnitude)
            seen = dot(split_rows(velocity), incidence[...])
            relative = jnp.sum(
                normal * (seen[0:8] + (seen[8:16] + seen[16:24])), axis=0, keepdims=True
            )
            return jnp.maximum(
                magnitude
                - relaxation * (gap + time_step * relative) / (2.0 * time_step * mobility),
                0.0,
            )

        magnitude = lax.fori_loop(0, SWEEPS, sweep, jnp.zeros((1, contacts), F32))
        drift = time_step * (hydro + mobility * totals(magnitude))
        wide_force[...] = jnp.broadcast_to(magnitude, wide_force.shape)
        wide_drift[...] = drift
        place = device * own_contacts
        at = pl.ds(pl.multiple_of(place // 128 * 128, 128), 128)
        turned = pltpu.roll(wide_force[:, at], (128 - place % 128) % 128, 1)
        force_ref[...] = turned[0:1, :own_contacts]
        place = device * per_device
        at = pl.ds(pl.multiple_of(place // 128 * 128, 128), 128)
        own = pltpu.roll(wide_drift[:, at], (128 - place % 128) % 128, 1).T
        for a in range(side):
            moved_ref[a] = centers[a] + own[a * side : (a + 1) * side, 0:3]

    return kernel


def vmem_of(held):
    return pltpu.CompilerParams(vmem_limit_bytes=min(60 << 20, 2 * held + (12 << 20)))


def local(
    tractions,
    centers,
    node_offsets,
    occupied,
    anchors,
    near_list,
    contact_pairs,
    contact_gap,
    contact_angles,
):
    side = tractions.shape[0]
    per_device = side * side
    nodes = tractions.shape[3]
    narrow_count = lax.axis_size("narrow")
    devices = lax.axis_size("wide") * narrow_count
    rank = lax.axis_index("wide") * narrow_count + lax.axis_index("narrow")
    slots = devices * per_device
    contacts_own = contact_gap.shape[0]
    contacts = contacts_own * devices
    pairs = max(MIN_PAIRS, HALF // devices)
    z_groups = HALF // pairs
    x_groups = max(1, devices // z_groups)
    half_x = HALF // x_groups
    z_group = rank % z_groups
    x_group = rank // z_groups
    rows = 6 * pairs

    vmem = pl.BlockSpec(memory_space=pltpu.VMEM)
    smem = pl.BlockSpec(memory_space=pltpu.SMEM)
    forces = 3 * per_device * nodes
    by_row = tractions.transpose(0, 2, 1, 3)
    packed = pl.pallas_call(
        pack_kernel,
        out_shape=jax.ShapeDtypeStruct((devices, 1, forces + 256), F32),
        in_specs=[smem] * 4 + [vmem] * 4,
        out_specs=vmem,
        scratch_shapes=[pltpu.VMEM((8, 128), F32)],
        name="pack",
    )(
        centers,
        anchors,
        occupied,
        near_list,
        by_row,
        contact_pairs,
        contact_gap[None],
        contact_angles,
    )
    gathered = lax.all_to_all(packed, AXES, split_axis=0, concat_axis=0, tiled=True)
    offsets_t = node_offsets.T
    self_near = pl.pallas_call(
        self_kernel,
        out_shape=jax.ShapeDtypeStruct((per_device, 3, nodes), F32),
        in_specs=[smem] + [vmem] * 3,
        out_specs=vmem,
        scratch_shapes=[pltpu.VMEM((nodes, 8), F32)],
        name="near_self",
    )(occupied, by_row, node_offsets, offsets_t)
    scalars = gathered[:, 0, forces : forces + 16 * per_device]

    xy, zz = z_tables()
    tables = np.concatenate(
        [
            xy.reshape(z_groups, 2 * pairs, GRID + BLOCK),
            zz.reshape(z_groups, 2 * pairs, GRID + BLOCK),
        ],
        axis=1,
    )
    table = lax.dynamic_index_in_dim(jnp.asarray(tables, F32), z_group, 0, keepdims=False)
    basis = real_basis()
    turned = np.ascontiguousarray(basis.T)
    ry = [jnp.asarray(v) for v in split_np(basis)]
    ryt = [jnp.asarray(v) for v in split_np(turned)]
    if x_groups == 1:
        rx, rxt = ry, ryt
    else:
        rxt = [
            lax.dynamic_index_in_dim(
                v.reshape(2, x_groups, half_x, GRID), x_group, 1, keepdims=False
            ).reshape(2 * half_x, GRID)
            for v in ryt
        ]
        rx = [v.T for v in rxt]

    keep = slots * nodes * BLOCK * 16 <= KEEP_BYTES
    kept = slots + UNROLL if keep else 1
    ranks = jnp.stack([z_group, x_group, rank]).astype(jnp.int32)
    partial = pl.pallas_call(
        far_kernel(pairs, slots, devices, keep),
        out_shape=jax.ShapeDtypeStruct((devices, 1, forces + 3 * slots), F32),
        in_specs=[smem, smem] + [vmem] * 13,
        out_specs=vmem,
        scratch_shapes=[
            pltpu.SMEM((slots + 1,), jnp.int32),
            pltpu.VMEM((4, (GRID + BLOCK) * rows, HALF), F32),
            pltpu.VMEM((UNROLL, GRID, nodes), BF16),
            pltpu.VMEM((3, 2 * half_x, GRID), F32),
            pltpu.VMEM((8, slots), F32),
            pltpu.VMEM((nodes, 8), F32),
            pltpu.VMEM((GRID + BLOCK, 4 * pairs, 128), F32),
            pltpu.VMEM((kept, BLOCK, nodes), F32),
            pltpu.VMEM((kept, 4 * pairs, nodes), F32),
            pltpu.VMEM((kept, 4, BLOCK, nodes), BF16),
        ],
        compiler_params=vmem_of(8 * slots * nodes * 4 + 4 * (GRID + BLOCK) * 6 * pairs * HALF * 4),
        name="far_near",
    )(
        scalars,
        ranks,
        gathered,
        node_offsets,
        offsets_t,
        self_near,
        table,
        *ry,
        *ryt,
        *rx,
        *rxt,
    )
    received = lax.all_to_all(partial, AXES, split_axis=0, concat_axis=0, tiled=True)
    incidence, contact_rows = pl.pallas_call(
        prepare_kernel(slots, devices, contacts_own),
        out_shape=(
            jax.ShapeDtypeStruct((slots, contacts), BF16),
            jax.ShapeDtypeStruct((8, contacts), F32),
        ),
        in_specs=[vmem],
        out_specs=(vmem, vmem),
        compiler_params=vmem_of(4 * slots * nodes * 4 + slots * contacts * 2),
        name="contact_rows",
    )(gathered)
    velocity, force, moved = pl.pallas_call(
        contact_kernel(slots, devices, contacts_own),
        out_shape=(
            jax.ShapeDtypeStruct((side, 3, side, nodes), F32),
            jax.ShapeDtypeStruct((1, contacts_own), F32),
            jax.ShapeDtypeStruct((side, side, 3), F32),
        ),
        in_specs=[smem, vmem, vmem, vmem, vmem],
        out_specs=(vmem, vmem, vmem),
        scratch_shapes=[
            pltpu.VMEM((8, contacts), F32),
            pltpu.VMEM((8, slots), F32),
        ],
        compiler_params=vmem_of(8 * slots * nodes * 4 + slots * contacts * 2),
        name="contacts",
    )(ranks, received, incidence, contact_rows, centers)
    return (velocity.transpose(0, 2, 1, 3), force[0], moved)


def solution(mesh):
    placed = (
        P("wide", "narrow", None, None),
        P("wide", "narrow", None),
        P(),
        P("wide", "narrow"),
        P("wide", "narrow", None),
        P("wide", "narrow", None),
        P(None, ("wide", "narrow")),
        P(("wide", "narrow")),
        P(None, ("wide", "narrow")),
    )
    return jax.shard_map(
        local,
        mesh=mesh,
        in_specs=placed,
        out_specs=(
            P("wide", "narrow", None, None),
            P(("wide", "narrow")),
            P("wide", "narrow", None),
        ),
        check_vma=False,
    )
```
